256 devices in a mesh: dp: 16 (over x, y), tensor: 16 (over z, core).
Axes of the slice: x: 4, y: 4, z: 8, core: 2. Of those that a mesh axis runs over, the one named last changes fastest.
Arguments:
- tokens: bfloat16 [32768, 1280], P(('dp', 'tensor'))
- cotangent: bfloat16 [32768, 1280], P(('dp', 'tensor')), may hold values from -6 to 6
- gate_weights: float32 [32768, 2], P(('dp', 'tensor')), may hold values from 0.2 to 1
- routes: int32 [32768, 2], P(('dp', 'tensor')), may hold values from 0 to 31, as said below
- slot_index: int32 [32768, 2], P(('dp', 'tensor')), may hold values from -1 to 1, as said below
- qkv_weight: bfloat16 [1280, 16, 240], P(None, 'tensor'), may hold values from -0.15625 to 0.15625
- proj_weight: bfloat16 [16, 80, 1280], P('tensor'), may hold values from -1.25 to 1.25
- up_weight: bfloat16 [32, 1280, 5120], P('dp', None, 'tensor'), may hold values from -0.15625 to 0.15625
- down_weight: bfloat16 [32, 5120, 1280], P('dp', 'tensor'), may hold values from -0.078125 to 0.078125
Outputs:
- layer_out: bfloat16 [32768, 1280], P(('dp', 'tensor'))
- gate_grad: float32 [32768, 2], P(('dp', 'tensor'))
- grad_qkv: float32 [1280, 16, 240], P('dp', 'tensor')
- grad_proj: float32 [16, 80, 1280], P('tensor', None, 'dp')
- grad_up: bfloat16 [32, 1280, 5120], P('dp', None, 'tensor')
- grad_down: bfloat16 [32, 5120, 1280], P('dp', 'tensor')
The draws below stay inside these ranges and needn't reach their ends.
Inputs may be any that keep to these rules, and one draw needn't show every extreme that they name: `routes`: the two experts of a row differ. `slot_index`: -1 marks a dropped pair; within the rows of one device (aligned blocks of 128 rows) and one expert, the kept pairs hold the slots 0, 1, 2, ... without gaps, each at most once.
All inputs are finite; a program needn't handle non-finite values.
Results may differ from the reference program's by a relative error of at most 0.035.
Values may be sent and summed in bfloat16 or wider, within the bound.
A program may use at most 128 MiB of HBM per device.

```python
import math
import jax
import jax.numpy as jnp
from jax import lax

D = 1280
HEADS = 16
HD = 80
FF = 5120
CAP = 2
ROWS_DEV = 128
EXPERTS = 32
SEQ = 2048
TOKENS = 32768
HEADS_DEV = 1
FF_DEV = 320
N_DP = 16
N_TENSOR = 16


def route_table(key):
    base_key = jax.random.fold_in(key, 71)
    key_relabel, key_pick, key_offset, key_order = jax.random.split(base_key, 4)
    relabel = jax.random.permutation(key_relabel, EXPERTS).astype(jnp.int32)
    first_pick = jax.random.randint(key_pick, (TOKENS,), 0, 2 * EXPERTS, dtype=jnp.int32)
    hot_count = max(EXPERTS // 4, 1)
    first_expert = jnp.where(first_pick < EXPERTS, first_pick, first_pick % hot_count)
    offset = jax.random.randint(key_offset, (TOKENS,), 1, EXPERTS, dtype=jnp.int32)
    second_expert = (first_expert + offset) % EXPERTS
    routes = jnp.take(relabel, jnp.stack([first_expert, second_expert], axis=1))
    block_total = TOKENS // ROWS_DEV

    def order_rows(block_key):
        return jax.random.permutation(block_key, ROWS_DEV).astype(jnp.int32)
    orders = jax.vmap(order_rows)(jax.random.split(key_order, block_total))
    priority = jnp.stack([orders, orders + ROWS_DEV], axis=2).reshape(block_total, ROWS_DEV * 2)
    block_routes = routes.reshape(block_total, ROWS_DEV * 2)

    def rank_block(pieces):
        chosen, order_rank = pieces
        same_expert = chosen[:, None] == chosen[None, :]
        earlier = order_rank[None, :] < order_rank[:, None]
        return jnp.sum((same_expert & earlier).astype(jnp.int32), axis=1)
    rank_counts = lax.map(rank_block, (block_routes, priority))
    slot_values = jnp.where(rank_counts < CAP, rank_counts, -1).reshape(TOKENS, 2)
    return (routes.astype(jnp.int32), slot_values.astype(jnp.int32))


def draw_routes(key, part):
    return route_table(key)[0]


def draw_slot_index(key, part):
    return route_table(key)[1]


def draw_tokens(key, part):
    base_key = jax.random.fold_in(key, 29)
    key_rows, key_cols, key_main = jax.random.split(base_key, 3)
    low_end = math.log(0.3)
    high_end = math.log(3.0)
    row_scale = jnp.exp(jax.random.uniform(key_rows, (TOKENS, 1), jnp.float32, low_end, high_end))
    col_scale = jnp.exp(jax.random.uniform(key_cols, (1, D), jnp.float32, low_end, high_end))
    main_part = jax.random.normal(key_main, (TOKENS, D), jnp.float32)
    return (main_part * row_scale * col_scale).astype(jnp.bfloat16)


def block_levels(own_key, extent, shards, smallest, largest):
    factor_of = 1.0
    for axis_at, blocks in shards:
        steps = jax.random.uniform(jax.random.fold_in(jax.random.fold_in(own_key, 6), axis_at), (blocks,), jnp.float32, smallest / len(shards), largest / len(shards))
        factor_of = factor_of * jnp.repeat(jnp.exp(steps), extent[axis_at] // blocks).reshape((-1,) + (1,) * (len(extent) - 1 - axis_at))
    return factor_of


def scatter_about(stream_key, shape, spread, limit, shards=(), kind=jnp.bfloat16):
    result = spread * jax.random.normal(stream_key, shape, jnp.float32)
    if shards:
        result = result * block_levels(stream_key, shape, shards, -0.22, 0.18)
    return jnp.clip(result, -limit, limit).astype(kind)


def setup_inputs(seed: int = 0) -> dict:
    keys = jax.random.split(jax.random.key(seed), 10)
    return {
        "tokens": draw_tokens(jax.random.fold_in(keys[9], 71), 0),
        "cotangent": scatter_about(keys[1], (TOKENS, D), 1.0, 6.0, ((0, 256),)),
        "gate_weights": jnp.clip(jnp.exp(math.log(1.0) - 1.609438 * jax.random.uniform(keys[2], (TOKENS, 2), jnp.float32) ** block_levels(keys[2], (TOKENS, 2), ((0, 256),), -0.2, 0.2)), 0.2, 1.0),
        "routes": draw_routes(jax.random.fold_in(keys[9], 71), 0),
        "slot_index": draw_slot_index(jax.random.fold_in(keys[9], 71), 0),
        "qkv_weight": scatter_about(keys[5], (D, HEADS, 3 * HD), D ** -0.5, 0.15625, ((1, 16),)),
        "proj_weight": scatter_about(keys[6], (HEADS, HD, D), (HEADS * HD // 64) ** -0.5, 1.25, ((0, 16),)),
        "up_weight": scatter_about(keys[7], (EXPERTS, D, FF), D ** -0.5, 0.15625, ((0, 16), (2, 16))),
        "down_weight": scatter_about(keys[8], (EXPERTS, FF, D), FF ** -0.5, 0.078125, ((0, 16), (1, 16))),
    }


epsilon = 1e-06
half_root = 1.0 / math.sqrt(2.0)
bell_scale = 1.0 / math.sqrt(2.0 * math.pi)

def norm_parts(row_block):
    widened = row_block.astype(jnp.float32)
    center = widened - lax.optimization_barrier(jnp.mean(widened, axis=-1, keepdims=True))
    factor = lax.rsqrt(lax.optimization_barrier(jnp.mean(center * center, axis=-1, keepdims=True)) + epsilon)
    return (center * factor, factor)

def norm_back(normal_rows, factor, upstream):
    mean_up = lax.optimization_barrier(jnp.mean(upstream, axis=-1, keepdims=True))
    mean_mix = lax.optimization_barrier(jnp.mean(upstream * normal_rows, axis=-1, keepdims=True))
    return factor * (upstream - mean_up - normal_rows * mean_mix)

def gelu_value(pre_act):
    return 0.5 * pre_act * (1.0 + lax.erf(pre_act * half_root))

def gelu_slope(pre_act):
    return 0.5 * (1.0 + lax.erf(pre_act * half_root)) + pre_act * jnp.exp(-0.5 * pre_act * pre_act) * bell_scale

def round_low(values):
    return lax.optimization_barrier(values.astype(jnp.bfloat16)).astype(jnp.float32)

def split_parts(widened):
    shaped = widened.reshape(SEQ, HEADS, 3 * HD)
    return (shaped[:, :, :HD], shaped[:, :, HD:2 * HD], shaped[:, :, 2 * HD:])

def chart_shares(queries, key_rows):
    scores = jnp.einsum('shk,thk->hst', queries, key_rows) * HD ** (-0.5)
    raised = jnp.exp(scores)
    return raised / lax.optimization_barrier(jnp.sum(raised, axis=-1, keepdims=True))

def reference(tokens, cotangent, gate_weights, routes, slot_index, qkv_weight, proj_weight, up_weight, down_weight):
    score_scale = HD ** (-0.5)
    block_total = N_DP * N_TENSOR
    places = EXPERTS * CAP
    slot_rows = block_total * CAP
    normal_in, factor_in = norm_parts(tokens)
    normed = normal_in.astype(jnp.bfloat16)
    flat_qkv = qkv_weight.reshape(D, HEADS * 3 * HD)
    proj_groups = proj_weight.reshape(N_TENSOR, HEADS_DEV, HD, D).astype(jnp.float32)

    def chart_forward(chart_norm):
        raw_qkv = jnp.dot(chart_norm, flat_qkv, preferred_element_type=jnp.float32)
        queries, key_rows, value_rows = split_parts(round_low(raw_qkv))
        shares = chart_shares(queries, key_rows)
        context = jnp.einsum('hst,thk->hsk', round_low(shares), value_rows)
        partial_value = jnp.einsum('ghsk,ghkd->gsd', round_low(context).reshape(N_TENSOR, HEADS_DEV, SEQ, HD), proj_groups)
        attention = lax.optimization_barrier(jnp.sum(round_low(partial_value), axis=0))
        return (raw_qkv.astype(jnp.bfloat16), context.astype(jnp.bfloat16), attention)
    qkv_all, context_all, attention_all = lax.map(chart_forward, normed.reshape(N_DP, SEQ, D))
    mid = (tokens.astype(jnp.float32) + attention_all.reshape(TOKENS, D)).astype(jnp.bfloat16)
    normal_mid, factor_mid = norm_parts(mid)
    mid_normed = normal_mid.astype(jnp.bfloat16)
    row_owner = (jnp.arange(TOKENS, dtype=jnp.int32) // ROWS_DEV)[:, None]
    target = jnp.where(slot_index >= 0, row_owner * places + routes * CAP + slot_index, block_total * places)
    target = target.reshape(TOKENS * 2).astype(jnp.int32)

    def scatter_slots(pair_rows):
        filled = jnp.zeros((block_total * places + 1, D), pair_rows.dtype).at[target].set(pair_rows.reshape(TOKENS * 2, D))
        shaped = filled[:-1].reshape(block_total, EXPERTS, CAP, D)
        return shaped.transpose(1, 0, 2, 3).reshape(EXPERTS, slot_rows, D)

    def gather_slots(per_expert):
        flat = per_expert.reshape(EXPERTS, block_total, CAP, D).transpose(1, 0, 2, 3).reshape(block_total * places, D)
        flat = jnp.concatenate([flat, jnp.zeros((1, D), flat.dtype)], axis=0)
        return flat[target].reshape(TOKENS, 2, D)
    slot_in = scatter_slots(jnp.broadcast_to(mid_normed[:, None, :], (TOKENS, 2, D)))

    def expert_forward(pieces):
        inputs, up_mat, down_mat = pieces
        pre_act = jnp.dot(inputs, up_mat, preferred_element_type=jnp.float32)
        hidden = round_low(gelu_value(pre_act))
        partial_value = jnp.einsum('mgf,gfd->mgd', hidden.reshape(slot_rows, N_TENSOR, FF_DEV), down_mat.astype(jnp.float32).reshape(N_TENSOR, FF_DEV, D))
        return lax.optimization_barrier(jnp.sum(round_low(partial_value), axis=1)).astype(jnp.bfloat16)
    expert_out = lax.map(expert_forward, (slot_in, up_weight, down_weight))
    picked = gather_slots(expert_out).astype(jnp.float32)
    mixed_rows = gate_weights[:, 0:1] * picked[:, 0] + gate_weights[:, 1:2] * picked[:, 1]
    layer_out = (mid.astype(jnp.float32) + mixed_rows).astype(jnp.bfloat16)
    upstream = cotangent.astype(jnp.float32)
    gate_grad = lax.optimization_barrier(jnp.sum(upstream[:, None, :] * picked, axis=-1))
    grad_pairs = (gate_weights[:, :, None] * upstream[:, None, :]).astype(jnp.bfloat16)
    grad_slot = scatter_slots(grad_pairs)

    def expert_backward(pieces):
        inputs, grads, up_mat, down_mat = pieces
        pre_act = jnp.dot(inputs, up_mat, preferred_element_type=jnp.float32)
        hidden = gelu_value(pre_act).astype(jnp.bfloat16)
        grad_hidden = jnp.dot(grads, down_mat.T, preferred_element_type=jnp.float32)
        grad_pre_wide = grad_hidden * gelu_slope(pre_act)
        grad_pre = grad_pre_wide.astype(jnp.bfloat16)
        grad_down = jnp.dot(hidden.T, grads, preferred_element_type=jnp.float32).astype(jnp.bfloat16)
        grad_up = jnp.dot(inputs.T, grad_pre, preferred_element_type=jnp.float32).astype(jnp.bfloat16)
        partial_value = jnp.einsum('mgf,dgf->mgd', round_low(grad_pre_wide).reshape(slot_rows, N_TENSOR, FF_DEV), up_mat.astype(jnp.float32).reshape(D, N_TENSOR, FF_DEV))
        grad_in = lax.optimization_barrier(jnp.sum(round_low(partial_value), axis=1)).astype(jnp.bfloat16)
        return (grad_in, grad_up, grad_down)
    grad_in, grad_up, grad_down = lax.map(expert_backward, (slot_in, grad_slot, up_weight, down_weight))
    back_pairs = gather_slots(grad_in).astype(jnp.float32)
    grad_norm = back_pairs[:, 0] + back_pairs[:, 1]
    grad_mid = (upstream + norm_back(normal_mid, factor_mid, grad_norm)).astype(jnp.bfloat16)

    def chart_backward(pieces):
        chart_norm, chart_qkv, context, chart_grad = pieces
        queries, key_rows, value_rows = split_parts(chart_qkv.astype(jnp.float32))
        shares = chart_shares(queries, key_rows)
        grad_wide = chart_grad.astype(jnp.float32)
        grad_context = round_low(jnp.einsum('sd,hkd->hsk', grad_wide, proj_weight.astype(jnp.float32)))
        grad_proj = jnp.einsum('hsk,sd->hkd', context.astype(jnp.float32), grad_wide)
        grad_shares = jnp.einsum('hsk,thk->hst', grad_context, value_rows)
        grad_scores = round_low(shares * (grad_shares - lax.optimization_barrier(jnp.sum(shares * grad_shares, axis=-1, keepdims=True))) * score_scale)
        grad_query = jnp.einsum('hst,thk->shk', grad_scores, key_rows).astype(jnp.bfloat16)
        grad_key = jnp.einsum('hst,shk->thk', grad_scores, queries).astype(jnp.bfloat16)
        grad_value = jnp.einsum('hst,hsk->thk', round_low(shares), grad_context).astype(jnp.bfloat16)
        grad_rows = jnp.concatenate([grad_query, grad_key, grad_value], axis=-1).reshape(SEQ, HEADS * 3 * HD)
        grad_qkv = jnp.dot(chart_norm.T, grad_rows, preferred_element_type=jnp.float32)
        return (grad_qkv, grad_proj)
    per_qkv, per_proj = lax.map(chart_backward, (normed.reshape(N_DP, SEQ, D), qkv_all, context_all, grad_mid.reshape(N_DP, SEQ, D)))
    grad_qkv = lax.optimization_barrier(jnp.sum(per_qkv, axis=0)).reshape(D, HEADS, 3 * HD)
    grad_proj = lax.optimization_barrier(jnp.sum(per_proj, axis=0))
    return (layer_out, gate_grad, grad_qkv, grad_proj, grad_up, grad_down)
```

```python
from functools import partial
import math

import jax
import jax.numpy as jnp
from jax import lax
from jax.experimental import pallas as pl
from jax.experimental.pallas import tpu as pltpu
from jax.sharding import PartitionSpec as P

CAP = 2


MESH = pl.DeviceIdType.MESH
VM = pl.BlockSpec(memory_space=pltpu.VMEM)
DMA = pltpu.SemaphoreType.DMA
PIECES = 4


def ring_places():
    spot = lax.axis_index("tensor")
    return spot, lax.div(spot, 2), lax.rem(spot, 2)


def level_at(level, steps, count):
    return lax.rem(level + steps + count, count)


def ring_peers(count):
    spot, level, side = ring_places()
    return (
        level_at(level, 1, count) * 2 + side,
        level_at(level, -1, count) * 2 + side,
        level * 2 + 1 - side,
    )


def greet_ring(count):
    barrier = pltpu.get_barrier_semaphore()
    peers = ring_peers(count)
    for peer in peers:
        pl.semaphore_signal(barrier, inc=1, device_id={"tensor": peer}, device_id_type=MESH)
    return len(peers)


def greet_groups():
    barrier = pltpu.get_barrier_semaphore()
    me = lax.axis_index("dp")
    count = lax.axis_size("dp")

    def call(step, carry):
        peer = lax.rem(me + step, count)
        pl.semaphore_signal(barrier, inc=1, device_id={"dp": peer}, device_id_type=MESH)
        return carry

    lax.fori_loop(1, count, call, 0)
    return count - 1


def await_peers(total):
    pl.semaphore_wait(pltpu.get_barrier_semaphore(), total)


def remote(source, target, send, recv, axis, peer):
    return pltpu.make_async_remote_copy(
        src_ref=source,
        dst_ref=target,
        send_sem=send,
        recv_sem=recv,
        device_id={axis: peer},
        device_id_type=MESH,
    )


def travels(way, step, piece, last):
    return step != last or (piece < PIECES // 2) == (way == 0)


def gather_ring(own_ref, full_ref, send, recv, give, take, mine_sem, count):
    spot, level, side = ring_places()
    peers = ring_peers(count)
    size = own_ref.shape[0] // PIECES
    reach = count // 2

    def place(way, step):
        return level_at(level, -step if way == 0 else step, count)

    def hop(way, step, piece):
        rows = pl.ds(piece * size, size)
        target = full_ref.at[place(way, step) * 2 + side, rows]
        source = own_ref.at[rows] if step == 0 else target
        return remote(
            source, target, send.at[way, step, piece], recv.at[way, step, piece], "tensor", peers[way]
        )

    def landed(way, step, piece):
        rows = pl.ds(piece * size, size)
        target = full_ref.at[place(way, step + 1) * 2 + side, rows]
        return remote(
            target, target, send.at[way, step, piece], recv.at[way, step, piece], "tensor", peers[way]
        )

    def across(way, step, piece, from_side):
        rows = pl.ds(piece * size, size)
        target = full_ref.at[place(way, step) * 2 + from_side, rows]
        source = own_ref.at[rows] if step == 0 else target
        return remote(
            source, target, give.at[way, step, piece], take.at[way, step, piece], "tensor", peers[2]
        )

    for piece in range(PIECES):
        for way in range(2):
            hop(way, 0, piece).start()
    keep = pltpu.make_async_copy(own_ref, full_ref.at[spot], mine_sem)
    keep.start()
    for piece in range(PIECES):
        across(0, 0, piece, side).start()
    moved = [(0, 0, piece) for piece in range(PIECES)]
    left = [(way, 0, piece) for piece in range(PIECES) for way in range(2)]
    for step in range(reach):
        for piece in range(PIECES):
            for way in range(2):
                if not travels(way, step, piece, reach - 1):
                    continue
                landed(way, step, piece).wait_recv()
                if step + 1 < reach and travels(way, step + 1, piece, reach - 1):
                    hop(way, step + 1, piece).start()
                    left.append((way, step + 1, piece))
                across(way, step + 1, piece, side).start()
                moved.append((way, step + 1, piece))
    keep.wait()
    for item in left:
        hop(*item).wait_send()
    for item in moved:
        across(*item, side).wait_send()
        across(*item, 1 - side).wait_recv()


def ring_sems(count):
    reach = count // 2
    return [
        DMA((2, reach, PIECES)),
        DMA((2, reach, PIECES)),
        DMA((2, reach + 1, PIECES)),
        DMA((2, reach + 1, PIECES)),
        DMA(()),
    ]


def gather_kernel(count, own_ref, full_ref, *sems):
    await_peers(greet_ring(count))
    gather_ring(own_ref, full_ref, *sems, count)


def comm_call(kernel, out_shape, operands, scratch, ident):
    single = not isinstance(out_shape, list)
    return pl.pallas_call(
        kernel,
        out_shape=out_shape,
        in_specs=[VM] * len(operands),
        out_specs=VM if single else [VM] * len(out_shape),
        scratch_shapes=scratch,
        compiler_params=pltpu.CompilerParams(
            collective_id=ident, has_side_effects=True, vmem_limit_bytes=60 * 1024 * 1024
        ),
    )(*operands)


def gather_tensor(own, ident):
    spots = lax.axis_size("tensor")
    return comm_call(
        partial(gather_kernel, spots // 2),
        jax.ShapeDtypeStruct((spots,) + own.shape, own.dtype),
        [own],
        ring_sems(spots // 2),
        ident,
    )


class Exchange:
    def __init__(self, source_ref, target_ref, send, recv, local_sem):
        self.me = lax.axis_index("dp")
        self.count = source_ref.shape[0]
        self.refs = (source_ref, target_ref, send, recv)
        self.keep = pltpu.make_async_copy(
            source_ref.at[self.me], target_ref.at[self.me], local_sem
        )

    def put(self, step):
        source_ref, target_ref, send, recv = self.refs
        peer = lax.rem(self.me + step, self.count)
        return remote(
            source_ref.at[peer], target_ref.at[self.me], send.at[step], recv.at[step], "dp", peer
        )

    def got(self, step):
        source_ref, target_ref, send, recv = self.refs
        peer = lax.rem(self.me - step + self.count, self.count)
        return remote(
            source_ref.at[peer], target_ref.at[peer], send.at[step], recv.at[step], "dp", peer
        )

    def start(self):
        def put_one(step, carry):
            self.put(step).start()
            return carry

        lax.fori_loop(1, self.count, put_one, 0)
        self.keep.start()

    def finish(self):
        self.keep.wait()

        def take_one(step, carry):
            self.got(step).wait_recv()
            self.put(step).wait_send()
            return carry

        lax.fori_loop(1, self.count, take_one, 0)


def exchange_sems(groups):
    return [DMA((groups,)), DMA((groups,)), DMA(())]


def slots_kernel(count, out_ref, full_ref, landing, dsend, drecv, dlocal, *sems):
    await_peers(greet_groups() + greet_ring(count))
    swap = Exchange(out_ref, landing, dsend, drecv, dlocal)
    swap.start()
    swap.finish()
    gather_ring(landing, full_ref, *sems, count)


def slots_out(outgoing, ident):
    spots = lax.axis_size("tensor")
    return comm_call(
        partial(slots_kernel, spots // 2),
        jax.ShapeDtypeStruct((spots,) + outgoing.shape, outgoing.dtype),
        [outgoing],
        [pltpu.VMEM(outgoing.shape, outgoing.dtype)]
        + exchange_sems(outgoing.shape[0])
        + ring_sems(spots // 2),
        ident,
    )


def reduce_ring(part_ref, total_ref, pair, stage, landing, send, recv, give, take, count):
    spot, level, side = ring_places()
    peers = ring_peers(count)
    size = part_ref.shape[1] // PIECES
    reach = count // 2

    def place(way, step):
        return level_at(level, reach - step if way == 0 else step - reach, count)

    def across(way, step, piece):
        rows = pl.ds(piece * size, size)
        there = place(way, step)
        return remote(
            part_ref.at[there * 2 + 1 - side, rows],
            pair.at[there, rows],
            give.at[way, step, piece],
            take.at[way, step, piece],
            "tensor",
            peers[2],
        )

    def hop(way, step, piece):
        rows = pl.ds(piece * size, size)
        return remote(
            stage.at[way, step, rows],
            landing.at[way, step, rows],
            send.at[way, step, piece],
            recv.at[way, step, piece],
            "tensor",
            peers[way],
        )

    plan = [
        (way, step, piece)
        for step in range(reach)
        for piece in range(PIECES)
        for way in range(2)
        if travels(way, step, piece, 0)
    ]
    own = [(0, reach, piece) for piece in range(PIECES)]
    for item in plan + own:
        across(*item).start()

    def local_sum(way, step, piece):
        rows = pl.ds(piece * size, size)
        there = place(way, step)
        across(way, step, piece).wait_recv()
        return part_ref[there * 2 + side, rows].astype(jnp.float32) + pair[there, rows].astype(
            jnp.float32
        )

    def arrived(way, step, piece):
        hop(way, step, piece).wait_recv()
        return landing[way, step, pl.ds(piece * size, size)].astype(jnp.float32)

    for way, step, piece in plan:
        term = local_sum(way, step, piece)
        if step > 0 and travels(way, step - 1, piece, 0):
            term = term + arrived(way, step - 1, piece)
        stage[way, step, pl.ds(piece * size, size)] = term.astype(stage.dtype)
        hop(way, step, piece).start()
    for way, step, piece in own:
        term = local_sum(way, step, piece)
        term = term + arrived(0, reach - 1, piece) + arrived(1, reach - 1, piece)
        total_ref[pl.ds(piece * size, size)] = term.astype(total_ref.dtype)
    for item in plan:
        hop(*item).wait_send()
    for item in plan + own:
        across(*item).wait_send()


def reduce_scratch(part, count):
    block = part.shape[1:]
    reach = count // 2
    return [
        pltpu.VMEM((count,) + block, part.dtype),
        pltpu.VMEM((2, reach) + block, part.dtype),
        pltpu.VMEM((2, reach) + block, part.dtype),
        DMA((2, reach, PIECES)),
        DMA((2, reach, PIECES)),
        DMA((2, reach + 1, PIECES)),
        DMA((2, reach + 1, PIECES)),
    ]


def reduce_kernel(count, part_ref, total_ref, *scratch):
    await_peers(greet_ring(count))
    reduce_ring(part_ref, total_ref, *scratch, count)


def reduce_tensor(part, ident):
    count = lax.axis_size("tensor") // 2
    return comm_call(
        partial(reduce_kernel, count),
        jax.ShapeDtypeStruct(part.shape[1:], jnp.float32),
        [part],
        reduce_scratch(part, count),
        ident,
    )


def back_kernel(count, parts, *refs):
    part_refs, refs = refs[:parts], refs[parts:]
    out_refs, refs = refs[:parts], refs[parts:]
    await_peers(greet_groups() + greet_ring(count))
    each = len(refs) // parts
    swaps = []
    for index in range(parts):
        total, dsend, drecv, dlocal, *ring = refs[index * each : (index + 1) * each]
        reduce_ring(part_refs[index], total, *ring, count)
        swaps.append(Exchange(total, out_refs[index], dsend, drecv, dlocal))
        swaps[-1].start()
    for swap in swaps:
        swap.finish()


def slots_back(part_list, ident):
    count = lax.axis_size("tensor") // 2
    scratch = []
    for part in part_list:
        block = part.shape[1:]
        scratch += [pltpu.VMEM(block, part.dtype)] + exchange_sems(block[0])
        scratch += reduce_scratch(part, count)
    return comm_call(
        partial(back_kernel, count, len(part_list)),
        [jax.ShapeDtypeStruct(part.shape[1:], part.dtype) for part in part_list],
        part_list,
        scratch,
        ident,
    )


def groups_kernel(parts, *refs):
    part_refs, refs = refs[:parts], refs[parts:]
    out_refs, refs = refs[:parts], refs[parts:]
    await_peers(greet_groups())
    swaps = []
    for index in range(parts):
        landing, dsend, drecv, dlocal = refs[index * 4 : index * 4 + 4]
        swaps.append(Exchange(part_refs[index], landing, dsend, drecv, dlocal))
        swaps[-1].start()
    for index in range(parts):
        swaps[index].finish()
        landing = refs[index * 4]
        total = landing[0].astype(jnp.float32)
        for group in range(1, landing.shape[0]):
            total = total + landing[group].astype(jnp.float32)
        out_refs[index][...] = total


def reduce_groups(part_list, ident):
    scratch = []
    for part in part_list:
        scratch += [pltpu.VMEM(part.shape, part.dtype)] + exchange_sems(part.shape[0])
    return comm_call(
        partial(groups_kernel, len(part_list)),
        [jax.ShapeDtypeStruct(part.shape[1:], jnp.float32) for part in part_list],
        part_list,
        scratch,
        ident,
    )


epsilon = 1e-06
half_root = 1.0 / math.sqrt(2.0)
bell_scale = 1.0 / math.sqrt(2.0 * math.pi)


def norm_parts(row_block):
    widened = row_block.astype(jnp.float32)
    center = widened - jnp.mean(widened, axis=-1, keepdims=True)
    factor = lax.rsqrt(jnp.mean(center * center, axis=-1, keepdims=True) + epsilon)
    return (center * factor, factor)


def norm_back(normal_rows, factor, upstream):
    mean_up = jnp.mean(upstream, axis=-1, keepdims=True)
    mean_mix = jnp.mean(upstream * normal_rows, axis=-1, keepdims=True)
    return factor * (upstream - mean_up - normal_rows * mean_mix)


def gelu_value(pre_act):
    return 0.5 * pre_act * (1.0 + lax.erf(pre_act * half_root))


def gelu_slope(pre_act):
    return (
        0.5 * (1.0 + lax.erf(pre_act * half_root))
        + pre_act * jnp.exp(-0.5 * pre_act * pre_act) * bell_scale
    )


def block_shares(query_block, key_rows, score_scale):
    scores = (
        jnp.einsum("qk,tk->qt", query_block, key_rows, preferred_element_type=jnp.float32)
        * score_scale
    )
    raised = jnp.exp(scores)
    return raised / jnp.sum(raised, axis=-1, keepdims=True)


def attend_head(queries, key_rows, value_rows, block_rows, score_scale):
    block_count = queries.shape[0] // block_rows

    def attend_one_block(query_block):
        shares = block_shares(query_block, key_rows, score_scale)
        context = jnp.dot(
            shares.astype(jnp.bfloat16), value_rows, preferred_element_type=jnp.float32
        )
        return context.astype(jnp.bfloat16)

    outputs = lax.map(attend_one_block, queries.reshape(block_count, block_rows, queries.shape[1]))
    return outputs.reshape(queries.shape)


def head_backward(queries, key_rows, value_rows, grad_context, block_rows, score_scale):
    block_count = queries.shape[0] // block_rows

    def head_one_block(carry, pieces):
        grad_keys, grad_values = carry
        query_block, grad_block = pieces
        shares = block_shares(query_block, key_rows, score_scale)
        grad_shares = jnp.einsum(
            "qk,tk->qt", grad_block, value_rows, preferred_element_type=jnp.float32
        )
        grad_scores = (
            shares
            * (grad_shares - jnp.sum(shares * grad_shares, axis=-1, keepdims=True))
            * score_scale
        ).astype(jnp.bfloat16)
        grad_query = jnp.dot(grad_scores, key_rows, preferred_element_type=jnp.float32).astype(
            jnp.bfloat16
        )
        grad_keys = grad_keys + jnp.einsum(
            "qt,qk->tk", grad_scores, query_block, preferred_element_type=jnp.float32
        )
        grad_values = grad_values + jnp.einsum(
            "qt,qk->tk", shares.astype(jnp.bfloat16), grad_block, preferred_element_type=jnp.float32
        )
        return ((grad_keys, grad_values), grad_query)

    zeros_rows = jnp.zeros(key_rows.shape, jnp.float32)
    shaped = (
        queries.reshape(block_count, block_rows, queries.shape[1]),
        grad_context.reshape(block_count, block_rows, queries.shape[1]),
    )
    (grad_keys, grad_values), grad_queries = lax.scan(
        head_one_block, (zeros_rows, zeros_rows), shaped
    )
    return (
        grad_queries.reshape(queries.shape),
        grad_keys.astype(jnp.bfloat16),
        grad_values.astype(jnp.bfloat16),
    )


def shards(
    tokens,
    cotangent,
    gate_weights,
    routes,
    slot_index,
    qkv_weight,
    proj_weight,
    up_weight,
    down_weight,
):
    rows_dev, model_width = tokens.shape
    head_size = qkv_weight.shape[2] // 3
    score_scale = head_size ** (-0.5)
    group_count = lax.axis_size("dp")
    local_experts = up_weight.shape[0]
    places = group_count * local_experts * CAP
    normal_in, factor_in = norm_parts(tokens)
    normed = normal_in.astype(jnp.bfloat16)
    full_norm = gather_tensor(normed, 1).reshape(-1, model_width)
    seq_len = full_norm.shape[0]
    block_rows = min(512, seq_len)
    qkv_rows = jnp.einsum(
        "sd,dhc->hsc", full_norm, qkv_weight, preferred_element_type=jnp.float32
    ).astype(jnp.bfloat16)
    queries = qkv_rows[:, :, :head_size]
    key_rows = qkv_rows[:, :, head_size : 2 * head_size]
    value_rows = qkv_rows[:, :, 2 * head_size :]
    context = jax.vmap(partial(attend_head, block_rows=block_rows, score_scale=score_scale))(
        queries, key_rows, value_rows
    )
    attention = reduce_tensor(
        jnp.einsum("hsk,hkd->sd", context, proj_weight, preferred_element_type=jnp.float32)
        .astype(jnp.bfloat16)
        .reshape(seq_len // rows_dev, rows_dev, model_width),
        2,
    )
    mid = (tokens.astype(jnp.float32) + attention).astype(jnp.bfloat16)
    normal_mid, factor_mid = norm_parts(mid)
    mid_normed = normal_mid.astype(jnp.bfloat16)
    slot_code = jnp.where(slot_index >= 0, routes * CAP + slot_index, -1)
    positions = jnp.arange(places, dtype=jnp.int32)
    pick_both = (slot_code[None, :, :] == positions[:, None, None]).astype(jnp.bfloat16)
    pick_first = pick_both[:, :, 0]
    pick_second = pick_both[:, :, 1]
    dispatch_rows = pick_first + pick_second
    outgoing = jnp.dot(dispatch_rows, mid_normed, preferred_element_type=jnp.float32).astype(
        jnp.bfloat16
    )
    arrived = slots_out(
        outgoing.astype(jnp.bfloat16).reshape(group_count, local_experts * CAP, model_width), 3
    ).reshape(-1, group_count, local_experts, CAP, model_width)
    pre_act = jnp.einsum("tsecd,edf->tsecf", arrived, up_weight, preferred_element_type=jnp.float32)
    hidden = gelu_value(pre_act).astype(jnp.bfloat16)
    expert_partial = jnp.einsum(
        "tsecf,efd->tsecd", hidden, down_weight, preferred_element_type=jnp.float32
    )
    upstream = cotangent.astype(jnp.float32)
    grad_first = (gate_weights[:, 0:1] * upstream).astype(jnp.bfloat16)
    grad_second = (gate_weights[:, 1:2] * upstream).astype(jnp.bfloat16)
    grad_outgoing = jnp.dot(pick_first, grad_first, preferred_element_type=jnp.float32) + jnp.dot(
        pick_second, grad_second, preferred_element_type=jnp.float32
    )
    grad_arrived = slots_out(
        grad_outgoing.astype(jnp.bfloat16).reshape(group_count, local_experts * CAP, model_width), 4
    ).reshape(-1, group_count, local_experts, CAP, model_width)
    grad_hidden = jnp.einsum(
        "tsecd,efd->tsecf", grad_arrived, down_weight, preferred_element_type=jnp.float32
    )
    grad_pre = (grad_hidden * gelu_slope(pre_act)).astype(jnp.bfloat16)
    grad_down = jnp.einsum(
        "tsecf,tsecd->efd", hidden, grad_arrived, preferred_element_type=jnp.float32
    ).astype(jnp.bfloat16)
    grad_up = jnp.einsum(
        "tsecd,tsecf->edf", arrived, grad_pre, preferred_element_type=jnp.float32
    ).astype(jnp.bfloat16)
    grad_partial = jnp.einsum(
        "tsecf,edf->tsecd", grad_pre, up_weight, preferred_element_type=jnp.float32
    )
    grad_back, returned = slots_back(
        [
            grad_partial.astype(jnp.bfloat16).reshape(-1, group_count, local_experts * CAP, model_width),
            expert_partial.astype(jnp.bfloat16).reshape(
                -1, group_count, local_experts * CAP, model_width
            ),
        ],
        5,
    )
    grad_back = grad_back.reshape(places, model_width)
    returned = returned.reshape(places, model_width)
    expert_first = jnp.einsum("pr,pd->rd", pick_first, returned, preferred_element_type=jnp.float32)
    expert_second = jnp.einsum(
        "pr,pd->rd", pick_second, returned, preferred_element_type=jnp.float32
    )
    mixed_rows = gate_weights[:, 0:1] * expert_first + gate_weights[:, 1:2] * expert_second
    layer_out = (mid.astype(jnp.float32) + mixed_rows).astype(jnp.bfloat16)
    gate_grad = jnp.stack(
        [jnp.sum(upstream * expert_first, axis=-1), jnp.sum(upstream * expert_second, axis=-1)],
        axis=1,
    )
    grad_norm = jnp.einsum(
        "pr,pd->rd", dispatch_rows, grad_back, preferred_element_type=jnp.float32
    )
    grad_mid = (upstream + norm_back(normal_mid, factor_mid, grad_norm)).astype(jnp.bfloat16)
    full_grad = gather_tensor(grad_mid, 6).reshape(-1, model_width)
    grad_context = jnp.einsum(
        "sd,hkd->hsk", full_grad, proj_weight, preferred_element_type=jnp.float32
    ).astype(jnp.bfloat16)
    grad_proj = jnp.einsum("hsk,sd->hdk", context, full_grad, preferred_element_type=jnp.float32)
    grad_queries, grad_keys, grad_values = jax.vmap(
        partial(head_backward, block_rows=block_rows, score_scale=score_scale)
    )(queries, key_rows, value_rows, grad_context)
    grad_rows = jnp.concatenate([grad_queries, grad_keys, grad_values], axis=-1)
    grad_qkv = jnp.einsum("sd,hsc->dhc", full_norm, grad_rows, preferred_element_type=jnp.float32)
    grad_qkv, grad_proj = reduce_groups(
        [
            grad_qkv.astype(jnp.bfloat16).reshape(group_count, -1, grad_qkv.shape[2]),
            grad_proj.astype(jnp.bfloat16).reshape(group_count, -1, head_size),
        ],
        7,
    )
    grad_qkv = grad_qkv[:, None, :]
    grad_proj = grad_proj.T[None]
    return (layer_out, gate_grad, grad_qkv, grad_proj, grad_up, grad_down)


def solution(mesh):
    return jax.shard_map(
        shards,
        mesh=mesh,
        in_specs=(
            P(("dp", "tensor"), None),
            P(("dp", "tensor"), None),
            P(("dp", "tensor"), None),
            P(("dp", "tensor"), None),
            P(("dp", "tensor"), None),
            P(None, "tensor", None),
            P("tensor", None, None),
            P("dp", None, "tensor"),
            P("dp", "tensor", None),
        ),
        out_specs=(
            P(("dp", "tensor"), None),
            P(("dp", "tensor"), None),
            P("dp", "tensor", None),
            P("tensor", None, "dp"),
            P("dp", None, "tensor"),
            P("dp", "tensor", None),
        ),
        check_vma=False,
    )
```

```python
from functools import partial
import math

import jax
import jax.numpy as jnp
from jax import lax
from jax.experimental import pallas as pl
from jax.experimental.pallas import tpu as pltpu
from jax.sharding import PartitionSpec as P

CAP = 2


MESH = pl.DeviceIdType.MESH
VM = pl.BlockSpec(memory_space=pltpu.VMEM)
DMA = pltpu.SemaphoreType.DMA
PIECES = 4
SIDE = 4


def ring_places():
    spot = lax.axis_index("tensor")
    return spot, lax.div(spot, 2), lax.rem(spot, 2)


def level_at(level, steps, count):
    return lax.rem(level + steps + count, count)


def ring_peers(count):
    spot, level, side = ring_places()
    return (
        level_at(level, 1, count) * 2 + side,
        level_at(level, -1, count) * 2 + side,
        level * 2 + 1 - side,
    )


def plane_peer(along_x, step):
    me = lax.axis_index("dp")
    x, y = lax.div(me, SIDE), lax.rem(me, SIDE)
    if along_x:
        return lax.rem(x + step + SIDE, SIDE) * SIDE + y
    return x * SIDE + lax.rem(y + step + SIDE, SIDE)


def signal(axis, peer):
    pl.semaphore_signal(
        pltpu.get_barrier_semaphore(), inc=1, device_id={axis: peer}, device_id_type=MESH
    )


def greet_ring(count):
    peers = ring_peers(count)
    for peer in peers:
        signal("tensor", peer)
    return len(peers)


def greet_plane():
    for along_x in (True, False):
        for step in range(1, SIDE):
            signal("dp", plane_peer(along_x, step))
    return 2 * (SIDE - 1)


def greet_groups():
    me = lax.axis_index("dp")
    count = lax.axis_size("dp")

    def call(step, carry):
        signal("dp", lax.rem(me + step, count))
        return carry

    lax.fori_loop(1, count, call, 0)
    return count - 1


def await_peers(total):
    pl.semaphore_wait(pltpu.get_barrier_semaphore(), total)


def remote(source, target, send, recv, axis, peer):
    return pltpu.make_async_remote_copy(
        src_ref=source,
        dst_ref=target,
        send_sem=send,
        recv_sem=recv,
        device_id={axis: peer},
        device_id_type=MESH,
    )


def travels(way, step, piece, last):
    return step != last or (piece < PIECES // 2) == (way == 0)


def block_at(ref, spot, piece):
    if len(ref.shape) == 3:
        size = ref.shape[1] // PIECES
        return ref.at[spot, pl.ds(piece * size, size)]
    per = PIECES // ref.shape[0]
    size = ref.shape[2] // per
    return ref.at[piece // per, spot, pl.ds(piece % per * size, size)]


def rows_at(ref, piece):
    size = ref.shape[0] // PIECES
    return ref.at[pl.ds(piece * size, size)]


class GatherRing:
    def __init__(self, own_ref, full_ref, send, recv, give, take, mine, count):
        self.spot, self.level, self.side = ring_places()
        self.peers = ring_peers(count)
        self.refs = (own_ref, full_ref, send, recv, give, take, mine)
        self.count, self.reach = count, count // 2
        self.left, self.moved = [], []

    def place(self, way, step):
        return level_at(self.level, -step if way == 0 else step, self.count)

    def hop(self, way, step, piece):
        own_ref, full_ref, send, recv = self.refs[:4]
        target = block_at(full_ref, self.place(way, step) * 2 + self.side, piece)
        source = rows_at(own_ref, piece) if step == 0 else target
        item = (way, step, piece)
        return remote(source, target, send.at[item], recv.at[item], "tensor", self.peers[way])

    def landed(self, way, step, piece):
        full_ref, send, recv = self.refs[1:4]
        target = block_at(full_ref, self.place(way, step + 1) * 2 + self.side, piece)
        item = (way, step, piece)
        return remote(target, target, send.at[item], recv.at[item], "tensor", self.peers[way])

    def across(self, way, step, piece, from_side):
        own_ref, full_ref, _, _, give, take, _ = self.refs
        target = block_at(full_ref, self.place(way, step) * 2 + from_side, piece)
        source = rows_at(own_ref, piece) if step == 0 else target
        item = (way, step, piece)
        return remote(source, target, give.at[item], take.at[item], "tensor", self.peers[2])

    def keep(self, piece):
        own_ref, full_ref, mine = self.refs[0], self.refs[1], self.refs[6]
        return pltpu.make_async_copy(
            rows_at(own_ref, piece), block_at(full_ref, self.spot, piece), mine.at[piece]
        )

    def begin(self):
        for piece in range(PIECES):
            for way in range(2):
                self.hop(way, 0, piece).start()
                self.left.append((way, 0, piece))
        for piece in range(PIECES):
            self.keep(piece).start()
            self.across(0, 0, piece, self.side).start()
            self.moved.append((0, 0, piece))

    def run(self, step):
        last = self.reach - 1
        for piece in range(PIECES):
            for way in range(2):
                if not travels(way, step, piece, last):
                    continue
                self.landed(way, step, piece).wait_recv()
                if step < last and travels(way, step + 1, piece, last):
                    self.hop(way, step + 1, piece).start()
                    self.left.append((way, step + 1, piece))
                self.across(way, step + 1, piece, self.side).start()
                self.moved.append((way, step + 1, piece))

    def finish(self):
        for piece in range(PIECES):
            self.keep(piece).wait()
        for item in self.left:
            self.hop(*item).wait_send()
        for item in self.moved:
            self.across(*item, self.side).wait_send()
            self.across(*item, 1 - self.side).wait_recv()


def gather_sems(count):
    reach = count // 2
    return [
        DMA((2, reach, PIECES)),
        DMA((2, reach, PIECES)),
        DMA((2, reach + 1, PIECES)),
        DMA((2, reach + 1, PIECES)),
        DMA((PIECES,)),
    ]


GATHER_SEMS = 5


def comm_call(kernel, out_shape, operands, scratch, ident):
    single = not isinstance(out_shape, list)
    return pl.pallas_call(
        kernel,
        out_shape=out_shape,
        in_specs=[VM] * len(operands),
        out_specs=VM if single else [VM] * len(out_shape),
        scratch_shapes=scratch,
        compiler_params=pltpu.CompilerParams(
            collective_id=ident, has_side_effects=True, vmem_limit_bytes=60 * 1024 * 1024
        ),
    )(*operands)


def gather_kernel(count, own_ref, full_ref, *sems):
    await_peers(greet_ring(count))
    ring = GatherRing(own_ref, full_ref, *sems, count)
    ring.begin()
    for step in range(count // 2):
        ring.run(step)
    ring.finish()


def gather_tensor(own, ident):
    spots = lax.axis_size("tensor")
    return comm_call(
        partial(gather_kernel, spots // 2),
        jax.ShapeDtypeStruct((spots,) + own.shape, own.dtype),
        [own],
        gather_sems(spots // 2),
        ident,
    )


class Swap:
    def __init__(self, along_x, source_ref, target_ref, send, recv, mine):
        me = lax.axis_index("dp")
        self.me = lax.div(me, SIDE) if along_x else lax.rem(me, SIDE)
        self.along_x = along_x
        self.refs = (source_ref, target_ref, send, recv)
        self.keep = pltpu.make_async_copy(
            self.block(source_ref, self.me), self.block(target_ref, self.me), mine
        )

    def block(self, ref, index):
        size = ref.shape[0] // SIDE
        return ref.at[pl.ds(pl.multiple_of(index * size, size), size)]

    def copy(self, step, outward):
        source_ref, target_ref, send, recv = self.refs
        there = lax.rem(self.me + (step if outward else SIDE - step), SIDE)
        return remote(
            self.block(source_ref, there),
            self.block(target_ref, self.me if outward else there),
            send.at[step],
            recv.at[step],
            "dp",
            plane_peer(self.along_x, step if outward else -step),
        )

    def start(self):
        for step in range(1, SIDE):
            self.copy(step, True).start()
        self.keep.start()

    def finish(self):
        self.keep.wait()
        for step in range(1, SIDE):
            self.copy(step, False).wait_recv()
        for step in range(1, SIDE):
            self.copy(step, True).wait_send()


def swap_sems():
    return [DMA((SIDE,)), DMA((SIDE,)), DMA(())]


def reorder(rows, kind):
    count = rows.shape[0]
    target = lax.broadcasted_iota(jnp.int32, (count, count), 0)
    source = lax.broadcasted_iota(jnp.int32, (count, count), 1)
    extents = {"x": SIDE, "y": SIDE, "e": count // (SIDE * SIDE * CAP), "c": CAP}

    def code(index, order):
        digits = {}
        for name in reversed(order):
            digits[name] = index % extents[name]
            index = index // extents[name]
        total = digits["x"]
        for name in "yec":
            total = total * extents[name] + digits[name]
        return total

    before, after = kind
    orders = {"x": "xyec", "y": "yexc", "e": "eyxc"}
    pick = (code(target, orders[after]) == code(source, orders[before])).astype(rows.dtype)
    return jnp.dot(pick, rows, preferred_element_type=jnp.float32).astype(rows.dtype)


class SlotsOut:
    def __init__(self, source_ref, first, second, third, done, sems):
        self.refs = (first, second, third, done)
        self.by_x = Swap(True, source_ref, first, *sems[:3])
        self.by_y = Swap(False, second, third, *sems[3:])

    def begin(self):
        self.by_x.start()

    def middle(self):
        first, second = self.refs[:2]
        self.by_x.finish()
        second[...] = reorder(first[...], "xy")
        self.by_y.start()

    def finish(self):
        third, done = self.refs[2:]
        self.by_y.finish()
        done[...] = reorder(third[...], "ye")


def out_scratch(slots):
    return [pltpu.VMEM(slots.shape, slots.dtype)] * 4 + swap_sems() + swap_sems()


OUT_SCRATCH = 10


def slots_kernel(count, source_ref, full_ref, *scratch):
    await_peers(greet_plane() + greet_ring(count))
    out = SlotsOut(source_ref, *scratch[:4], scratch[4:OUT_SCRATCH])
    out.begin()
    out.middle()
    out.finish()
    ring = GatherRing(scratch[3], full_ref, *scratch[OUT_SCRATCH:], count)
    ring.begin()
    for step in range(count // 2):
        ring.run(step)
    ring.finish()


def slots_shape(slots, local_experts):
    spots = lax.axis_size("tensor")
    rows, width = slots.shape
    return jax.ShapeDtypeStruct((local_experts, spots, rows // local_experts, width), slots.dtype)


def slots_out(slots, local_experts, ident):
    count = lax.axis_size("tensor") // 2
    return comm_call(
        partial(slots_kernel, count),
        slots_shape(slots, local_experts),
        [slots],
        out_scratch(slots) + gather_sems(count),
        ident,
    )


def opening_kernel(count, own_ref, source_ref, full_ref, slots_ref, *scratch):
    await_peers(greet_plane() + greet_ring(count))
    out = SlotsOut(source_ref, *scratch[:4], scratch[4:OUT_SCRATCH])
    sems = scratch[OUT_SCRATCH:]
    first = GatherRing(own_ref, full_ref, *sems[:GATHER_SEMS], count)
    second = GatherRing(scratch[3], slots_ref, *sems[GATHER_SEMS:], count)
    out.begin()
    first.begin()
    first.run(0)
    out.middle()
    first.run(1)
    out.finish()
    for step in range(2, count // 2):
        first.run(step)
    second.begin()
    first.finish()
    for step in range(count // 2):
        second.run(step)
    second.finish()


def opening(own, slots, local_experts, ident):
    spots = lax.axis_size("tensor")
    count = spots // 2
    return comm_call(
        partial(opening_kernel, count),
        [
            jax.ShapeDtypeStruct((spots,) + own.shape, own.dtype),
            slots_shape(slots, local_experts),
        ],
        [own, slots],
        out_scratch(slots) + gather_sems(count) + gather_sems(count),
        ident,
    )


class ReduceRing:
    def __init__(self, part_ref, total_ref, pair, stage, landing, send, recv, give, take, count):
        self.spot, self.level, self.side = ring_places()
        self.peers = ring_peers(count)
        self.part, self.total, self.pair = part_ref, total_ref, pair
        self.stage, self.landing = stage, landing
        self.sems = (send, recv, give, take)
        self.count, self.reach = count, count // 2
        self.plan = [
            (way, step, piece)
            for step in range(self.reach)
            for piece in range(PIECES)
            for way in range(2)
            if travels(way, step, piece, 0)
        ]
        self.own = [(0, self.reach, piece) for piece in range(PIECES)]

    def place(self, way, step):
        steps = self.reach - step
        return level_at(self.level, steps if way == 0 else -steps, self.count)

    def rows(self, way, step, piece):
        size = self.stage.shape[2] // PIECES
        return way, step, pl.ds(piece * size, size)

    def across(self, way, step, piece):
        there = self.place(way, step)
        item = (way, step, piece)
        return remote(
            block_at(self.part, there * 2 + 1 - self.side, piece),
            rows_at(self.pair.at[there], piece),
            self.sems[2].at[item],
            self.sems[3].at[item],
            "tensor",
            self.peers[2],
        )

    def hop(self, way, step, piece):
        item = (way, step, piece)
        where = self.rows(*item)
        return remote(
            self.stage.at[where],
            self.landing.at[where],
            self.sems[0].at[item],
            self.sems[1].at[item],
            "tensor",
            self.peers[way],
        )

    def local_sum(self, way, step, piece):
        there = self.place(way, step)
        self.across(way, step, piece).wait_recv()
        mine = block_at(self.part, there * 2 + self.side, piece)[...]
        return mine.astype(jnp.float32) + rows_at(self.pair.at[there], piece)[...].astype(
            jnp.float32
        )

    def arrived(self, way, step, piece):
        self.hop(way, step, piece).wait_recv()
        return self.landing[self.rows(way, step, piece)].astype(jnp.float32)

    def begin(self):
        for item in self.plan + self.own:
            self.across(*item).start()

    def run(self):
        for way, step, piece in self.plan:
            term = self.local_sum(way, step, piece)
            if step > 0 and travels(way, step - 1, piece, 0):
                term = term + self.arrived(way, step - 1, piece)
            self.stage[self.rows(way, step, piece)] = term.astype(self.stage.dtype)
            self.hop(way, step, piece).start()
        for way, step, piece in self.own:
            term = self.local_sum(way, step, piece)
            for side in range(2):
                term = term + self.arrived(side, self.reach - 1, piece)
            rows_at(self.total, piece)[...] = term.astype(self.total.dtype)

    def finish(self):
        for item in self.plan:
            self.hop(*item).wait_send()
        for item in self.plan + self.own:
            self.across(*item).wait_send()


def reduce_scratch(rows, width, dtype, count):
    reach = count // 2
    return [
        pltpu.VMEM((count, rows, width), dtype),
        pltpu.VMEM((2, reach, rows, width), dtype),
        pltpu.VMEM((2, reach, rows, width), dtype),
        DMA((2, reach, PIECES)),
        DMA((2, reach, PIECES)),
        DMA((2, reach + 1, PIECES)),
        DMA((2, reach + 1, PIECES)),
    ]


REDUCE_SCRATCH = 7


def reduce_kernel(count, part_ref, total_ref, *scratch):
    await_peers(greet_ring(count))
    ring = ReduceRing(part_ref, total_ref, *scratch, count)
    ring.begin()
    ring.run()
    ring.finish()


def reduce_tensor(part, ident):
    count = lax.axis_size("tensor") // 2
    _, rows, width = part.shape
    return comm_call(
        partial(reduce_kernel, count),
        jax.ShapeDtypeStruct((rows, width), jnp.float32),
        [part],
        reduce_scratch(rows, width, part.dtype, count),
        ident,
    )


class SlotsBack:
    def __init__(self, done, third, second, first, target_ref, sems):
        self.refs = (done, third, second, first)
        self.by_y = Swap(False, third, second, *sems[:3])
        self.by_x = Swap(True, first, target_ref, *sems[3:])

    def begin(self):
        done, third = self.refs[:2]
        third[...] = reorder(done[...], "ey")
        self.by_y.start()

    def middle(self):
        second, first = self.refs[2:]
        self.by_y.finish()
        first[...] = reorder(second[...], "yx")
        self.by_x.start()

    def finish(self):
        self.by_x.finish()


def back_kernel(count, parts, *refs):
    part_refs, refs = refs[:parts], refs[parts:]
    out_refs, refs = refs[:parts], refs[parts:]
    each = len(refs) // parts
    rings, backs = [], []
    for index in range(parts):
        mine = refs[index * each : (index + 1) * each]
        slots, ring = mine[:OUT_SCRATCH], mine[OUT_SCRATCH:]
        rings.append(ReduceRing(part_refs[index], slots[0], *ring, count))
        backs.append(SlotsBack(*slots[:4], out_refs[index], slots[4:]))
    await_peers(greet_plane() + greet_ring(count))
    for ring in rings:
        ring.begin()
    for ring, back in zip(rings, backs):
        ring.run()
        back.begin()
    for back in backs:
        back.middle()
    for back in backs:
        back.finish()
    for ring in rings:
        ring.finish()


def slots_back(part_list, ident):
    count = lax.axis_size("tensor") // 2
    scratch, shapes = [], []
    for part in part_list:
        experts, _, rows, width = part.shape
        slots = jax.ShapeDtypeStruct((experts * rows, width), part.dtype)
        shapes.append(slots)
        scratch += out_scratch(slots) + reduce_scratch(experts * rows, width, part.dtype, count)
    return comm_call(
        partial(back_kernel, count, len(part_list)), shapes, part_list, scratch, ident
    )


class Exchange:
    def __init__(self, source_ref, target_ref, send, recv, local_sem):
        self.me = lax.axis_index("dp")
        self.count = source_ref.shape[0]
        self.refs = (source_ref, target_ref, send, recv)
        self.keep = pltpu.make_async_copy(
            source_ref.at[self.me], target_ref.at[self.me], local_sem
        )

    def put(self, step):
        source_ref, target_ref, send, recv = self.refs
        peer = lax.rem(self.me + step, self.count)
        return remote(
            source_ref.at[peer], target_ref.at[self.me], send.at[step], recv.at[step], "dp", peer
        )

    def got(self, step):
        source_ref, target_ref, send, recv = self.refs
        peer = lax.rem(self.me - step + self.count, self.count)
        return remote(
            source_ref.at[peer], target_ref.at[peer], send.at[step], recv.at[step], "dp", peer
        )

    def start(self):
        def put_one(step, carry):
            self.put(step).start()
            return carry

        lax.fori_loop(1, self.count, put_one, 0)
        self.keep.start()

    def finish(self):
        self.keep.wait()

        def take_one(step, carry):
            self.got(step).wait_recv()
            self.put(step).wait_send()
            return carry

        lax.fori_loop(1, self.count, take_one, 0)


def exchange_sems(groups):
    return [DMA((groups,)), DMA((groups,)), DMA(())]


def groups_kernel(parts, *refs):
    part_refs, refs = refs[:parts], refs[parts:]
    out_refs, refs = refs[:parts], refs[parts:]
    await_peers(greet_groups())
    swaps = []
    for index in range(parts):
        landing, dsend, drecv, dlocal = refs[index * 4 : index * 4 + 4]
        swaps.append(Exchange(part_refs[index], landing, dsend, drecv, dlocal))
        swaps[-1].start()
    for index in range(parts):
        swaps[index].finish()
        landing = refs[index * 4]
        total = landing[0].astype(jnp.float32)
        for group in range(1, landing.shape[0]):
            total = total + landing[group].astype(jnp.float32)
        out_refs[index][...] = total


def reduce_groups(part_list, ident):
    scratch = []
    for part in part_list:
        scratch += [pltpu.VMEM(part.shape, part.dtype)] + exchange_sems(part.shape[0])
    return comm_call(
        partial(groups_kernel, len(part_list)),
        [jax.ShapeDtypeStruct(part.shape[1:], jnp.float32) for part in part_list],
        part_list,
        scratch,
        ident,
    )


epsilon = 1e-06
half_root = 1.0 / math.sqrt(2.0)
bell_scale = 1.0 / math.sqrt(2.0 * math.pi)


def norm_parts(row_block):
    widened = row_block.astype(jnp.float32)
    center = widened - jnp.mean(widened, axis=-1, keepdims=True)
    factor = lax.rsqrt(jnp.mean(center * center, axis=-1, keepdims=True) + epsilon)
    return (center * factor, factor)


def norm_back(normal_rows, factor, upstream):
    mean_up = jnp.mean(upstream, axis=-1, keepdims=True)
    mean_mix = jnp.mean(upstream * normal_rows, axis=-1, keepdims=True)
    return factor * (upstream - mean_up - normal_rows * mean_mix)


def gelu_value(pre_act):
    return 0.5 * pre_act * (1.0 + lax.erf(pre_act * half_root))


def gelu_slope(pre_act):
    return (
        0.5 * (1.0 + lax.erf(pre_act * half_root))
        + pre_act * jnp.exp(-0.5 * pre_act * pre_act) * bell_scale
    )


def block_shares(query_block, key_rows, score_scale):
    scores = (
        jnp.einsum("qk,tk->qt", query_block, key_rows, preferred_element_type=jnp.float32)
        * score_scale
    )
    raised = jnp.exp(scores)
    return raised / jnp.sum(raised, axis=-1, keepdims=True)


def attend_head(queries, key_rows, value_rows, block_rows, score_scale):
    block_count = queries.shape[0] // block_rows

    def attend_one_block(query_block):
        shares = block_shares(query_block, key_rows, score_scale)
        context = jnp.dot(
            shares.astype(jnp.bfloat16), value_rows, preferred_element_type=jnp.float32
        )
        return context.astype(jnp.bfloat16)

    outputs = lax.map(attend_one_block, queries.reshape(block_count, block_rows, queries.shape[1]))
    return outputs.reshape(queries.shape)


def head_backward(queries, key_rows, value_rows, grad_context, block_rows, score_scale):
    block_count = queries.shape[0] // block_rows

    def head_one_block(carry, pieces):
        grad_keys, grad_values = carry
        query_block, grad_block = pieces
        shares = block_shares(query_block, key_rows, score_scale)
        grad_shares = jnp.einsum(
            "qk,tk->qt", grad_block, value_rows, preferred_element_type=jnp.float32
        )
        grad_scores = (
            shares
            * (grad_shares - jnp.sum(shares * grad_shares, axis=-1, keepdims=True))
            * score_scale
        ).astype(jnp.bfloat16)
        grad_query = jnp.dot(grad_scores, key_rows, preferred_element_type=jnp.float32).astype(
            jnp.bfloat16
        )
        grad_keys = grad_keys + jnp.einsum(
            "qt,qk->tk", grad_scores, query_block, preferred_element_type=jnp.float32
        )
        grad_values = grad_values + jnp.einsum(
            "qt,qk->tk", shares.astype(jnp.bfloat16), grad_block, preferred_element_type=jnp.float32
        )
        return ((grad_keys, grad_values), grad_query)

    zeros_rows = jnp.zeros(key_rows.shape, jnp.float32)
    shaped = (
        queries.reshape(block_count, block_rows, queries.shape[1]),
        grad_context.reshape(block_count, block_rows, queries.shape[1]),
    )
    (grad_keys, grad_values), grad_queries = lax.scan(
        head_one_block, (zeros_rows, zeros_rows), shaped
    )
    return (
        grad_queries.reshape(queries.shape),
        grad_keys.astype(jnp.bfloat16),
        grad_values.astype(jnp.bfloat16),
    )


def shards(
    tokens,
    cotangent,
    gate_weights,
    routes,
    slot_index,
    qkv_weight,
    proj_weight,
    up_weight,
    down_weight,
):
    rows_dev, model_width = tokens.shape
    head_size = qkv_weight.shape[2] // 3
    score_scale = head_size ** (-0.5)
    group_count = lax.axis_size("dp")
    spots = lax.axis_size("tensor")
    local_experts = up_weight.shape[0]
    places = group_count * local_experts * CAP
    normal_in, factor_in = norm_parts(tokens)
    normed = normal_in.astype(jnp.bfloat16)
    slot_code = jnp.where(slot_index >= 0, routes * CAP + slot_index, -1)
    positions = jnp.arange(places, dtype=jnp.int32)
    pick_both = (slot_code[None, :, :] == positions[:, None, None]).astype(jnp.bfloat16)
    pick_first = pick_both[:, :, 0]
    pick_second = pick_both[:, :, 1]
    dispatch_rows = pick_first + pick_second
    upstream = cotangent.astype(jnp.float32)
    grad_first = (gate_weights[:, 0:1] * upstream).astype(jnp.bfloat16)
    grad_second = (gate_weights[:, 1:2] * upstream).astype(jnp.bfloat16)
    grad_outgoing = jnp.dot(pick_first, grad_first, preferred_element_type=jnp.float32) + jnp.dot(
        pick_second, grad_second, preferred_element_type=jnp.float32
    )
    full_norm, grad_arrived = opening(
        normed, grad_outgoing.astype(jnp.bfloat16), local_experts, 1
    )
    full_norm = full_norm.reshape(-1, model_width)
    grad_arrived = grad_arrived.reshape(local_experts, -1, model_width)
    seq_len = full_norm.shape[0]
    block_rows = min(512, seq_len)
    qkv_rows = jnp.einsum(
        "sd,dhc->hsc", full_norm, qkv_weight, preferred_element_type=jnp.float32
    ).astype(jnp.bfloat16)
    queries = qkv_rows[:, :, :head_size]
    key_rows = qkv_rows[:, :, head_size : 2 * head_size]
    value_rows = qkv_rows[:, :, 2 * head_size :]
    context = jax.vmap(partial(attend_head, block_rows=block_rows, score_scale=score_scale))(
        queries, key_rows, value_rows
    )
    attention = reduce_tensor(
        jnp.einsum("hsk,hkd->sd", context, proj_weight, preferred_element_type=jnp.float32)
        .astype(jnp.bfloat16)
        .reshape(spots, rows_dev, model_width),
        2,
    )
    mid = (tokens.astype(jnp.float32) + attention).astype(jnp.bfloat16)
    normal_mid, factor_mid = norm_parts(mid)
    mid_normed = normal_mid.astype(jnp.bfloat16)
    outgoing = jnp.dot(dispatch_rows, mid_normed, preferred_element_type=jnp.float32).astype(
        jnp.bfloat16
    )
    arrived = slots_out(outgoing, local_experts, 3).reshape(local_experts, -1, model_width)
    pre_act = jnp.einsum("end,edf->enf", arrived, up_weight, preferred_element_type=jnp.float32)
    hidden = gelu_value(pre_act).astype(jnp.bfloat16)
    expert_partial = jnp.einsum(
        "enf,efd->end", hidden, down_weight, preferred_element_type=jnp.float32
    )
    grad_hidden = jnp.einsum(
        "end,efd->enf", grad_arrived, down_weight, preferred_element_type=jnp.float32
    )
    grad_pre = (grad_hidden * gelu_slope(pre_act)).astype(jnp.bfloat16)
    grad_down = jnp.einsum(
        "enf,end->efd", hidden, grad_arrived, preferred_element_type=jnp.float32
    ).astype(jnp.bfloat16)
    grad_up = jnp.einsum(
        "end,enf->edf", arrived, grad_pre, preferred_element_type=jnp.float32
    ).astype(jnp.bfloat16)
    grad_partial = jnp.einsum(
        "enf,edf->end", grad_pre, up_weight, preferred_element_type=jnp.float32
    )
    grad_back, returned = slots_back(
        [
            part.astype(jnp.bfloat16).reshape(local_experts, spots, -1, model_width)
            for part in (grad_partial, expert_partial)
        ],
        5,
    )
    expert_first = jnp.einsum("pr,pd->rd", pick_first, returned, preferred_element_type=jnp.float32)
    expert_second = jnp.einsum(
        "pr,pd->rd", pick_second, returned, preferred_element_type=jnp.float32
    )
    mixed_rows = gate_weights[:, 0:1] * expert_first + gate_weights[:, 1:2] * expert_second
    layer_out = (mid.astype(jnp.float32) + mixed_rows).astype(jnp.bfloat16)
    gate_grad = jnp.stack(
        [jnp.sum(upstream * expert_first, axis=-1), jnp.sum(upstream * expert_second, axis=-1)],
        axis=1,
    )
    grad_norm = jnp.einsum(
        "pr,pd->rd", dispatch_rows, grad_back, preferred_element_type=jnp.float32
    )
    grad_mid = (upstream + norm_back(normal_mid, factor_mid, grad_norm)).astype(jnp.bfloat16)
    full_grad = gather_tensor(grad_mid, 6).reshape(-1, model_width)
    grad_context = jnp.einsum(
        "sd,hkd->hsk", full_grad, proj_weight, preferred_element_type=jnp.float32
    ).astype(jnp.bfloat16)
    grad_proj = jnp.einsum("hsk,sd->hdk", context, full_grad, preferred_element_type=jnp.float32)
    grad_queries, grad_keys, grad_values = jax.vmap(
        partial(head_backward, block_rows=block_rows, score_scale=score_scale)
    )(queries, key_rows, value_rows, grad_context)
    grad_rows = jnp.concatenate([grad_queries, grad_keys, grad_values], axis=-1)
    grad_qkv = jnp.einsum("sd,hsc->dhc", full_norm, grad_rows, preferred_element_type=jnp.float32)
    grad_qkv, grad_proj = reduce_groups(
        [
            grad_qkv.astype(jnp.bfloat16).reshape(group_count, -1, grad_qkv.shape[2]),
            grad_proj.astype(jnp.bfloat16).reshape(group_count, -1, head_size),
        ],
        7,
    )
    return (layer_out, gate_grad, grad_qkv[:, None, :], grad_proj.T[None], grad_up, grad_down)


def solution(mesh):
    return jax.shard_map(
        shards,
        mesh=mesh,
        in_specs=(
            P(("dp", "tensor"), None),
            P(("dp", "tensor"), None),
            P(("dp", "tensor"), None),
            P(("dp", "tensor"), None),
            P(("dp", "tensor"), None),
            P(None, "tensor", None),
            P("tensor", None, None),
            P("dp", None, "tensor"),
            P("dp", "tensor", None),
        ),
        out_specs=(
            P(("dp", "tensor"), None),
            P(("dp", "tensor"), None),
            P("dp", "tensor", None),
            P("tensor", None, "dp"),
            P("dp", None, "tensor"),
            P("dp", "tensor", None),
        ),
        check_vma=False,
    )
```

```python
from functools import partial
import math

import jax
import jax.numpy as jnp
from jax import lax
from jax.experimental import pallas as pl
from jax.experimental.pallas import tpu as pltpu
from jax.sharding import PartitionSpec as P

CAP = 2


MESH = pl.DeviceIdType.MESH
VM = pl.BlockSpec(memory_space=pltpu.VMEM)
DMA = pltpu.SemaphoreType.DMA
PIECES = 4
SIDE = 4


def ring_places():
    spot = lax.axis_index("tensor")
    return spot, lax.div(spot, 2), lax.rem(spot, 2)


def level_at(level, steps, count):
    return lax.rem(level + steps + count, count)


def ring_peers(count):
    spot, level, side = ring_places()
    return (
        level_at(level, 1, count) * 2 + side,
        level_at(level, -1, count) * 2 + side,
        level * 2 + 1 - side,
    )


def plane_peer(along_x, step):
    me = lax.axis_index("dp")
    x, y = lax.div(me, SIDE), lax.rem(me, SIDE)
    if along_x:
        return lax.rem(x + step + SIDE, SIDE) * SIDE + y
    return x * SIDE + lax.rem(y + step + SIDE, SIDE)


def signal(axis, peer):
    pl.semaphore_signal(
        pltpu.get_barrier_semaphore(), inc=1, device_id={axis: peer}, device_id_type=MESH
    )


def greet_ring(count):
    peers = ring_peers(count)
    for peer in peers:
        signal("tensor", peer)
    return len(peers)


def greet_plane():
    for along_x in (True, False):
        for step in range(1, SIDE):
            signal("dp", plane_peer(along_x, step))
    return 2 * (SIDE - 1)


def greet_groups():
    me = lax.axis_index("dp")
    count = lax.axis_size("dp")

    def call(step, carry):
        signal("dp", lax.rem(me + step, count))
        return carry

    lax.fori_loop(1, count, call, 0)
    return count - 1


def await_peers(total):
    pl.semaphore_wait(pltpu.get_barrier_semaphore(), total)


def remote(source, target, send, recv, axis, peer):
    return pltpu.make_async_remote_copy(
        src_ref=source,
        dst_ref=target,
        send_sem=send,
        recv_sem=recv,
        device_id={axis: peer},
        device_id_type=MESH,
    )


def travels(way, step, piece, last):
    return step != last or (piece < PIECES // 2) == (way == 0)


def block_at(ref, spot, piece):
    if len(ref.shape) == 3:
        size = ref.shape[1] // PIECES
        return ref.at[spot, pl.ds(piece * size, size)]
    per = PIECES // ref.shape[0]
    size = ref.shape[2] // per
    return ref.at[piece // per, spot, pl.ds(piece % per * size, size)]


def rows_at(ref, piece):
    size = ref.shape[0] // PIECES
    return ref.at[pl.ds(piece * size, size)]


class GatherRing:
    def __init__(self, own_ref, full_ref, send, recv, give, take, mine, count):
        self.spot, self.level, self.side = ring_places()
        self.peers = ring_peers(count)
        self.refs = (own_ref, full_ref, send, recv, give, take, mine)
        self.count, self.reach = count, count // 2
        self.left, self.moved = [], []

    def place(self, way, step):
        return level_at(self.level, -step if way == 0 else step, self.count)

    def hop(self, way, step, piece):
        own_ref, full_ref, send, recv = self.refs[:4]
        target = block_at(full_ref, self.place(way, step) * 2 + self.side, piece)
        source = rows_at(own_ref, piece) if step == 0 else target
        item = (way, step, piece)
        return remote(source, target, send.at[item], recv.at[item], "tensor", self.peers[way])

    def landed(self, way, step, piece):
        full_ref, send, recv = self.refs[1:4]
        target = block_at(full_ref, self.place(way, step + 1) * 2 + self.side, piece)
        item = (way, step, piece)
        return remote(target, target, send.at[item], recv.at[item], "tensor", self.peers[way])

    def across(self, way, step, piece, from_side):
        own_ref, full_ref, _, _, give, take, _ = self.refs
        target = block_at(full_ref, self.place(way, step) * 2 + from_side, piece)
        source = rows_at(own_ref, piece) if step == 0 else target
        item = (way, step, piece)
        return remote(source, target, give.at[item], take.at[item], "tensor", self.peers[2])

    def keep(self, piece):
        own_ref, full_ref, mine = self.refs[0], self.refs[1], self.refs[6]
        return pltpu.make_async_copy(
            rows_at(own_ref, piece), block_at(full_ref, self.spot, piece), mine.at[piece]
        )

    def begin(self):
        for piece in range(PIECES):
            for way in range(2):
                self.hop(way, 0, piece).start()
                self.left.append((way, 0, piece))
        for piece in range(PIECES):
            self.keep(piece).start()
            self.across(0, 0, piece, self.side).start()
            self.moved.append((0, 0, piece))

    def run(self, step):
        last = self.reach - 1
        for piece in range(PIECES):
            for way in range(2):
                if not travels(way, step, piece, last):
                    continue
                self.landed(way, step, piece).wait_recv()
                if step < last and travels(way, step + 1, piece, last):
                    self.hop(way, step + 1, piece).start()
                    self.left.append((way, step + 1, piece))
                self.across(way, step + 1, piece, self.side).start()
                self.moved.append((way, step + 1, piece))

    def finish(self):
        for piece in range(PIECES):
            self.keep(piece).wait()
        for item in self.left:
            self.hop(*item).wait_send()
        for item in self.moved:
            self.across(*item, self.side).wait_send()
            self.across(*item, 1 - self.side).wait_recv()


def gather_sems(count):
    reach = count // 2
    return [
        DMA((2, reach, PIECES)),
        DMA((2, reach, PIECES)),
        DMA((2, reach + 1, PIECES)),
        DMA((2, reach + 1, PIECES)),
        DMA((PIECES,)),
    ]


GATHER_SEMS = 5


def comm_call(kernel, out_shape, operands, scratch, ident):
    single = not isinstance(out_shape, list)
    return pl.pallas_call(
        kernel,
        out_shape=out_shape,
        in_specs=[VM] * len(operands),
        out_specs=VM if single else [VM] * len(out_shape),
        scratch_shapes=scratch,
        compiler_params=pltpu.CompilerParams(
            collective_id=ident, has_side_effects=True, vmem_limit_bytes=60 * 1024 * 1024
        ),
    )(*operands)


def gather_kernel(count, own_ref, full_ref, *sems):
    await_peers(greet_ring(count))
    ring = GatherRing(own_ref, full_ref, *sems, count)
    ring.begin()
    for step in range(count // 2):
        ring.run(step)
    ring.finish()


def gather_tensor(own, ident):
    spots = lax.axis_size("tensor")
    return comm_call(
        partial(gather_kernel, spots // 2),
        jax.ShapeDtypeStruct((spots,) + own.shape, own.dtype),
        [own],
        gather_sems(spots // 2),
        ident,
    )


class Swap:
    def __init__(self, along_x, source_ref, target_ref, send, recv, mine):
        me = lax.axis_index("dp")
        self.me = lax.div(me, SIDE) if along_x else lax.rem(me, SIDE)
        self.along_x = along_x
        self.refs = (source_ref, target_ref, send, recv)
        self.keep = pltpu.make_async_copy(
            self.block(source_ref, self.me), self.block(target_ref, self.me), mine
        )

    def block(self, ref, index):
        size = ref.shape[0] // SIDE
        return ref.at[pl.ds(pl.multiple_of(index * size, size), size)]

    def copy(self, step, outward):
        source_ref, target_ref, send, recv = self.refs
        there = lax.rem(self.me + (step if outward else SIDE - step), SIDE)
        return remote(
            self.block(source_ref, there),
            self.block(target_ref, self.me if outward else there),
            send.at[step],
            recv.at[step],
            "dp",
            plane_peer(self.along_x, step if outward else -step),
        )

    def start(self):
        for step in range(1, SIDE):
            self.copy(step, True).start()
        self.keep.start()

    def finish(self):
        self.keep.wait()
        for step in range(1, SIDE):
            self.copy(step, False).wait_recv()
        for step in range(1, SIDE):
            self.copy(step, True).wait_send()


def swap_sems():
    return [DMA((SIDE,)), DMA((SIDE,)), DMA(())]


def reorder(rows, kind):
    count = rows.shape[0]
    target = lax.broadcasted_iota(jnp.int32, (count, count), 0)
    source = lax.broadcasted_iota(jnp.int32, (count, count), 1)
    extents = {"x": SIDE, "y": SIDE, "e": count // (SIDE * SIDE * CAP), "c": CAP}

    def code(index, order):
        digits = {}
        for name in reversed(order):
            digits[name] = index % extents[name]
            index = index // extents[name]
        total = digits["x"]
        for name in "yec":
            total = total * extents[name] + digits[name]
        return total

    before, after = kind
    orders = {"x": "xyec", "y": "yexc", "e": "eyxc"}
    pick = (code(target, orders[after]) == code(source, orders[before])).astype(rows.dtype)
    return jnp.dot(pick, rows, preferred_element_type=jnp.float32).astype(rows.dtype)


class SlotsOut:
    def __init__(self, source_ref, first, second, third, done, sems):
        self.refs = (first, second, third, done)
        self.by_x = Swap(True, source_ref, first, *sems[:3])
        self.by_y = Swap(False, second, third, *sems[3:])

    def begin(self):
        self.by_x.start()

    def middle(self):
        first, second = self.refs[:2]
        self.by_x.finish()
        second[...] = reorder(first[...], "xy")
        self.by_y.start()

    def finish(self):
        third, done = self.refs[2:]
        self.by_y.finish()
        done[...] = reorder(third[...], "ye")


def out_scratch(slots):
    return [pltpu.VMEM(slots.shape, slots.dtype)] * 4 + swap_sems() + swap_sems()


OUT_SCRATCH = 10


def slots_kernel(count, source_ref, full_ref, *scratch):
    await_peers(greet_plane() + greet_ring(count))
    out = SlotsOut(source_ref, *scratch[:4], scratch[4:OUT_SCRATCH])
    out.begin()
    out.middle()
    out.finish()
    ring = GatherRing(scratch[3], full_ref, *scratch[OUT_SCRATCH:], count)
    ring.begin()
    for step in range(count // 2):
        ring.run(step)
    ring.finish()


def slots_shape(slots, local_experts):
    spots = lax.axis_size("tensor")
    rows, width = slots.shape
    return jax.ShapeDtypeStruct((local_experts, spots, rows // local_experts, width), slots.dtype)


def slots_out(slots, local_experts, ident):
    count = lax.axis_size("tensor") // 2
    return comm_call(
        partial(slots_kernel, count),
        slots_shape(slots, local_experts),
        [slots],
        out_scratch(slots) + gather_sems(count),
        ident,
    )


def opening_kernel(count, own_ref, source_ref, full_ref, slots_ref, *scratch):
    await_peers(greet_plane() + greet_ring(count))
    out = SlotsOut(source_ref, *scratch[:4], scratch[4:OUT_SCRATCH])
    sems = scratch[OUT_SCRATCH:]
    first = GatherRing(own_ref, full_ref, *sems[:GATHER_SEMS], count)
    second = GatherRing(scratch[3], slots_ref, *sems[GATHER_SEMS:], count)
    out.begin()
    first.begin()
    first.run(0)
    out.middle()
    first.run(1)
    out.finish()
    for step in range(2, count // 2):
        first.run(step)
    second.begin()
    first.finish()
    for step in range(count // 2):
        second.run(step)
    second.finish()


def opening(own, slots, local_experts, ident):
    spots = lax.axis_size("tensor")
    count = spots // 2
    return comm_call(
        partial(opening_kernel, count),
        [
            jax.ShapeDtypeStruct((spots,) + own.shape, own.dtype),
            slots_shape(slots, local_experts),
        ],
        [own, slots],
        out_scratch(slots) + gather_sems(count) + gather_sems(count),
        ident,
    )


class ReduceRing:
    def __init__(self, part_ref, total_ref, pair, stage, landing, send, recv, give, take, count):
        self.spot, self.level, self.side = ring_places()
        self.peers = ring_peers(count)
        self.part, self.total, self.pair = part_ref, total_ref, pair
        self.stage, self.landing = stage, landing
        self.sems = (send, recv, give, take)
        self.count, self.reach = count, count // 2
        self.plan = [
            (way, step, piece)
            for step in range(self.reach)
            for piece in range(PIECES)
            for way in range(2)
            if travels(way, step, piece, 0)
        ]
        self.own = [(0, self.reach, piece) for piece in range(PIECES)]

    def place(self, way, step):
        steps = self.reach - step
        return level_at(self.level, steps if way == 0 else -steps, self.count)

    def rows(self, way, step, piece):
        size = self.stage.shape[2] // PIECES
        return way, step, pl.ds(piece * size, size)

    def across(self, way, step, piece):
        there = self.place(way, step)
        item = (way, step, piece)
        return remote(
            block_at(self.part, there * 2 + 1 - self.side, piece),
            rows_at(self.pair.at[there], piece),
            self.sems[2].at[item],
            self.sems[3].at[item],
            "tensor",
            self.peers[2],
        )

    def hop(self, way, step, piece):
        item = (way, step, piece)
        where = self.rows(*item)
        return remote(
            self.stage.at[where],
            self.landing.at[where],
            self.sems[0].at[item],
            self.sems[1].at[item],
            "tensor",
            self.peers[way],
        )

    def local_sum(self, way, step, piece):
        there = self.place(way, step)
        self.across(way, step, piece).wait_recv()
        mine = block_at(self.part, there * 2 + self.side, piece)[...]
        return mine.astype(jnp.float32) + rows_at(self.pair.at[there], piece)[...].astype(
            jnp.float32
        )

    def arrived(self, way, step, piece):
        self.hop(way, step, piece).wait_recv()
        return self.landing[self.rows(way, step, piece)].astype(jnp.float32)

    def begin(self):
        for item in self.plan + self.own:
            self.across(*item).start()

    def run(self):
        for way, step, piece in self.plan:
            term = self.local_sum(way, step, piece)
            if step > 0 and travels(way, step - 1, piece, 0):
                term = term + self.arrived(way, step - 1, piece)
            self.stage[self.rows(way, step, piece)] = term.astype(self.stage.dtype)
            self.hop(way, step, piece).start()
        for way, step, piece in self.own:
            term = self.local_sum(way, step, piece)
            for side in range(2):
                term = term + self.arrived(side, self.reach - 1, piece)
            rows_at(self.total, piece)[...] = term.astype(self.total.dtype)

    def finish(self):
        for item in self.plan:
            self.hop(*item).wait_send()
        for item in self.plan + self.own:
            self.across(*item).wait_send()


def reduce_scratch(rows, width, dtype, count):
    reach = count // 2
    return [
        pltpu.VMEM((count, rows, width), dtype),
        pltpu.VMEM((2, reach, rows, width), dtype),
        pltpu.VMEM((2, reach, rows, width), dtype),
        DMA((2, reach, PIECES)),
        DMA((2, reach, PIECES)),
        DMA((2, reach + 1, PIECES)),
        DMA((2, reach + 1, PIECES)),
    ]


REDUCE_SCRATCH = 7


def reduce_kernel(count, part_ref, total_ref, *scratch):
    await_peers(greet_ring(count))
    ring = ReduceRing(part_ref, total_ref, *scratch, count)
    ring.begin()
    ring.run()
    ring.finish()


def reduce_tensor(part, ident):
    count = lax.axis_size("tensor") // 2
    _, rows, width = part.shape
    return comm_call(
        partial(reduce_kernel, count),
        jax.ShapeDtypeStruct((rows, width), jnp.float32),
        [part],
        reduce_scratch(rows, width, part.dtype, count),
        ident,
    )


class SlotsBack:
    def __init__(self, done, third, second, first, target_ref, sems):
        self.refs = (done, third, second, first)
        self.by_y = Swap(False, third, second, *sems[:3])
        self.by_x = Swap(True, first, target_ref, *sems[3:])

    def begin(self):
        done, third = self.refs[:2]
        third[...] = reorder(done[...], "ey")
        self.by_y.start()

    def middle(self):
        second, first = self.refs[2:]
        self.by_y.finish()
        first[...] = reorder(second[...], "yx")
        self.by_x.start()

    def finish(self):
        self.by_x.finish()


def back_kernel(count, parts, *refs):
    part_refs, refs = refs[:parts], refs[parts:]
    out_refs, refs = refs[:parts], refs[parts:]
    each = len(refs) // parts
    rings, backs = [], []
    for index in range(parts):
        mine = refs[index * each : (index + 1) * each]
        slots, ring = mine[:OUT_SCRATCH], mine[OUT_SCRATCH:]
        rings.append(ReduceRing(part_refs[index], slots[0], *ring, count))
        backs.append(SlotsBack(*slots[:4], out_refs[index], slots[4:]))
    await_peers(greet_plane() + greet_ring(count))
    for ring in rings:
        ring.begin()
    for ring, back in zip(rings, backs):
        ring.run()
        back.begin()
    for back in backs:
        back.middle()
    for back in backs:
        back.finish()
    for ring in rings:
        ring.finish()


def slots_back(part_list, ident):
    count = lax.axis_size("tensor") // 2
    scratch, shapes = [], []
    for part in part_list:
        experts, _, rows, width = part.shape
        slots = jax.ShapeDtypeStruct((experts * rows, width), part.dtype)
        shapes.append(slots)
        scratch += out_scratch(slots) + reduce_scratch(experts * rows, width, part.dtype, count)
    return comm_call(
        partial(back_kernel, count, len(part_list)), shapes, part_list, scratch, ident
    )


class Exchange:
    def __init__(self, source_ref, target_ref, send, recv, local_sem):
        self.me = lax.axis_index("dp")
        self.count = source_ref.shape[0]
        self.refs = (source_ref, target_ref, send, recv)
        self.keep = pltpu.make_async_copy(
            source_ref.at[self.me], target_ref.at[self.me], local_sem
        )

    def put(self, step):
        source_ref, target_ref, send, recv = self.refs
        peer = lax.rem(self.me + step, self.count)
        return remote(
            source_ref.at[peer], target_ref.at[self.me], send.at[step], recv.at[step], "dp", peer
        )

    def got(self, step):
        source_ref, target_ref, send, recv = self.refs
        peer = lax.rem(self.me - step + self.count, self.count)
        return remote(
            source_ref.at[peer], target_ref.at[peer], send.at[step], recv.at[step], "dp", peer
        )

    def start(self):
        def put_one(step, carry):
            self.put(step).start()
            return carry

        lax.fori_loop(1, self.count, put_one, 0)
        self.keep.start()

    def finish(self):
        self.keep.wait()

        def take_one(step, carry):
            self.got(step).wait_recv()
            self.put(step).wait_send()
            return carry

        lax.fori_loop(1, self.count, take_one, 0)


def exchange_sems(groups):
    return [DMA((groups,)), DMA((groups,)), DMA(())]


def groups_kernel(parts, *refs):
    part_refs, refs = refs[:parts], refs[parts:]
    out_refs, refs = refs[:parts], refs[parts:]
    await_peers(greet_groups())
    swaps = []
    for index in range(parts):
        landing, dsend, drecv, dlocal = refs[index * 4 : index * 4 + 4]
        swaps.append(Exchange(part_refs[index], landing, dsend, drecv, dlocal))
        swaps[-1].start()
    for index in range(parts):
        swaps[index].finish()
        landing = refs[index * 4]
        total = landing[0].astype(jnp.float32)
        for group in range(1, landing.shape[0]):
            total = total + landing[group].astype(jnp.float32)
        out_refs[index][...] = total


def reduce_groups(part_list, ident):
    scratch = []
    for part in part_list:
        scratch += [pltpu.VMEM(part.shape, part.dtype)] + exchange_sems(part.shape[0])
    return comm_call(
        partial(groups_kernel, len(part_list)),
        [jax.ShapeDtypeStruct(part.shape[1:], jnp.float32) for part in part_list],
        part_list,
        scratch,
        ident,
    )
LANES = 128
QUERY_BLOCK = 512
KEY_BLOCK = 256


def mm(left, right):
    return jnp.dot(left, right, preferred_element_type=jnp.float32)


def project_rows(norm_ref, weight_ref, rows_ref, cols_ref, index):
    size = QUERY_BLOCK
    rows = pl.ds(pl.multiple_of(index * size, size), size)
    block = mm(norm_ref[rows, :], weight_ref[...])
    rows_ref[rows, :] = block.astype(rows_ref.dtype)
    cols_ref[:, rows] = block.T.astype(cols_ref.dtype)


def attend_block(rows_ref, cols_ref, context_ref, inverse_ref, raised_ref, index, scale):
    seq = rows_ref.shape[0]
    here = pl.ds(pl.multiple_of(index * QUERY_BLOCK, QUERY_BLOCK), QUERY_BLOCK)
    queries = cols_ref[0:LANES, here]
    total = jnp.zeros((1, QUERY_BLOCK), jnp.float32)
    for at in range(0, seq, KEY_BLOCK):
        scores = mm(rows_ref[at : at + KEY_BLOCK, LANES : 2 * LANES], queries)
        raised = jnp.exp(scores * scale)
        raised_ref[at : at + KEY_BLOCK, :] = raised
        total = total + jnp.sum(raised, axis=0, keepdims=True)
    inverse = 1.0 / total
    inverse_ref[:, here] = inverse
    context = jnp.zeros((LANES, QUERY_BLOCK), jnp.float32)
    for at in range(0, seq, KEY_BLOCK):
        shares = (raised_ref[at : at + KEY_BLOCK, :] * inverse).astype(jnp.bfloat16)
        context = context + mm(cols_ref[2 * LANES : 3 * LANES, at : at + KEY_BLOCK], shares)
    context_ref[:, here] = context.astype(context_ref.dtype)


def forward_kernel(scale, norm_ref, weight_ref, rows_ref, cols_ref, context_ref, inverse_ref, raised_ref):
    blocks = norm_ref.shape[0] // QUERY_BLOCK

    def project(index, carry):
        project_rows(norm_ref, weight_ref, rows_ref, cols_ref, index)
        return carry

    def attend(index, carry):
        attend_block(rows_ref, cols_ref, context_ref, inverse_ref, raised_ref, index, scale)
        return carry

    lax.fori_loop(0, blocks, project, 0)
    lax.fori_loop(0, blocks, attend, 0)


def attend_forward(full_norm, weight, scale):
    seq = full_norm.shape[0]
    return pl.pallas_call(
        partial(forward_kernel, scale),
        out_shape=[
            jax.ShapeDtypeStruct((seq, 3 * LANES), jnp.bfloat16),
            jax.ShapeDtypeStruct((3 * LANES, seq), jnp.bfloat16),
            jax.ShapeDtypeStruct((LANES, seq), jnp.bfloat16),
            jax.ShapeDtypeStruct((1, seq), jnp.float32),
        ],
        in_specs=[VM] * 2,
        out_specs=[VM] * 4,
        scratch_shapes=[pltpu.VMEM((seq, QUERY_BLOCK), jnp.float32)],
        compiler_params=pltpu.CompilerParams(vmem_limit_bytes=60 * 1024 * 1024),
    )(full_norm, weight)


def backward_block(
    rows_ref, cols_ref, context_ref, inverse_ref, grad_ref, proj_ref, gcols_ref, gkeys, gvals, index, scale
):
    seq = rows_ref.shape[0]
    here = pl.ds(pl.multiple_of(index * QUERY_BLOCK, QUERY_BLOCK), QUERY_BLOCK)
    queries = cols_ref[0:LANES, here]
    query_rows = rows_ref[here, 0:LANES]
    wide = lax.dot_general(
        grad_ref[here, :],
        proj_ref[...],
        (((1,), (1,)), ((), ())),
        preferred_element_type=jnp.float32,
    )
    grad_rows = wide.astype(jnp.bfloat16)
    grad_cols = wide.T.astype(jnp.bfloat16)
    inverse = inverse_ref[:, here]
    delta = jnp.sum(
        grad_cols.astype(jnp.float32) * context_ref[:, here].astype(jnp.float32),
        axis=0,
        keepdims=True,
    )
    grad_query = jnp.zeros((LANES, QUERY_BLOCK), jnp.float32)
    for at in range(0, seq, KEY_BLOCK):
        keys = slice(at, at + KEY_BLOCK)
        scores = mm(rows_ref[keys, LANES : 2 * LANES], queries)
        shares = jnp.exp(scores * scale) * inverse
        grad_shares = mm(rows_ref[keys, 2 * LANES : 3 * LANES], grad_cols)
        grad_scores = (shares * (grad_shares - delta)).astype(jnp.bfloat16)
        gvals[keys, :] += mm(shares.astype(jnp.bfloat16), grad_rows)
        gkeys[keys, :] += mm(grad_scores, query_rows)
        grad_query = grad_query + mm(cols_ref[LANES : 2 * LANES, keys], grad_scores)
    size = gcols_ref.shape[0] // 3
    gcols_ref[0:size, here] = (grad_query[0:size] * scale).astype(gcols_ref.dtype)


def backward_kernel(
    scale,
    norm_ref,
    grad_ref,
    proj_ref,
    rows_ref,
    cols_ref,
    context_ref,
    inverse_ref,
    weights_ref,
    gcols_ref,
    gkeys,
    gvals,
):
    seq = rows_ref.shape[0]
    size = gcols_ref.shape[0] // 3
    gkeys[...] = jnp.zeros_like(gkeys)
    gvals[...] = jnp.zeros_like(gvals)

    def one_block(index, carry):
        backward_block(
            rows_ref, cols_ref, context_ref, inverse_ref, grad_ref, proj_ref, gcols_ref, gkeys, gvals, index, scale
        )
        return carry

    lax.fori_loop(0, seq // QUERY_BLOCK, one_block, 0)
    for at in range(0, seq, QUERY_BLOCK):
        there = slice(at, at + QUERY_BLOCK)
        key_cols = (gkeys[there, :] * scale).T
        value_cols = gvals[there, :].T
        gcols_ref[size : 2 * size, there] = key_cols[0:size].astype(gcols_ref.dtype)
        gcols_ref[2 * size : 3 * size, there] = value_cols[0:size].astype(gcols_ref.dtype)
    step = norm_ref.shape[1] // 5
    spare = jnp.zeros((3 * LANES - 4 * size, step), jnp.float32)

    def weights(index, carry):
        where = pl.ds(pl.multiple_of(index * step, step), step)
        for_qkv = mm(gcols_ref[...], norm_ref[:, where])
        for_proj = mm(context_ref[0:size, :], grad_ref[:, where])
        block = jnp.concatenate([for_qkv, for_proj, spare], axis=0).T
        weights_ref[where, :] = block[:, 0 : 4 * size].astype(weights_ref.dtype)
        return carry

    lax.fori_loop(0, 5, weights, 0)


def attend_backward(full_norm, full_grad, proj, rows, cols, context, inverse, scale, size):
    seq, width = full_norm.shape
    return pl.pallas_call(
        partial(backward_kernel, scale),
        out_shape=jax.ShapeDtypeStruct((width, 4 * size), jnp.bfloat16),
        in_specs=[VM] * 7,
        out_specs=VM,
        scratch_shapes=[
            pltpu.VMEM((3 * size, seq), jnp.bfloat16),
            pltpu.VMEM((seq, LANES), jnp.float32),
            pltpu.VMEM((seq, LANES), jnp.float32),
        ],
        compiler_params=pltpu.CompilerParams(vmem_limit_bytes=60 * 1024 * 1024),
    )(full_norm, full_grad, proj, rows, cols, context, inverse)


epsilon = 1e-06
half_root = 1.0 / math.sqrt(2.0)
bell_scale = 1.0 / math.sqrt(2.0 * math.pi)


def norm_parts(row_block):
    widened = row_block.astype(jnp.float32)
    center = widened - jnp.mean(widened, axis=-1, keepdims=True)
    factor = lax.rsqrt(jnp.mean(center * center, axis=-1, keepdims=True) + epsilon)
    return (center * factor, factor)


def norm_back(normal_rows, factor, upstream):
    mean_up = jnp.mean(upstream, axis=-1, keepdims=True)
    mean_mix = jnp.mean(upstream * normal_rows, axis=-1, keepdims=True)
    return factor * (upstream - mean_up - normal_rows * mean_mix)


def gelu_value(pre_act):
    return 0.5 * pre_act * (1.0 + lax.erf(pre_act * half_root))


def gelu_slope(pre_act):
    return (
        0.5 * (1.0 + lax.erf(pre_act * half_root))
        + pre_act * jnp.exp(-0.5 * pre_act * pre_act) * bell_scale
    )


def shards(
    tokens,
    cotangent,
    gate_weights,
    routes,
    slot_index,
    qkv_weight,
    proj_weight,
    up_weight,
    down_weight,
):
    rows_dev, model_width = tokens.shape
    head_size = qkv_weight.shape[2] // 3
    score_scale = head_size ** (-0.5)
    group_count = lax.axis_size("dp")
    spots = lax.axis_size("tensor")
    local_experts = up_weight.shape[0]
    places = group_count * local_experts * CAP
    normal_in, factor_in = norm_parts(tokens)
    normed = normal_in.astype(jnp.bfloat16)
    slot_code = jnp.where(slot_index >= 0, routes * CAP + slot_index, -1)
    positions = jnp.arange(places, dtype=jnp.int32)
    pick_both = (slot_code[None, :, :] == positions[:, None, None]).astype(jnp.bfloat16)
    pick_first = pick_both[:, :, 0]
    pick_second = pick_both[:, :, 1]
    dispatch_rows = pick_first + pick_second
    upstream = cotangent.astype(jnp.float32)
    grad_first = (gate_weights[:, 0:1] * upstream).astype(jnp.bfloat16)
    grad_second = (gate_weights[:, 1:2] * upstream).astype(jnp.bfloat16)
    grad_outgoing = jnp.dot(pick_first, grad_first, preferred_element_type=jnp.float32) + jnp.dot(
        pick_second, grad_second, preferred_element_type=jnp.float32
    )
    full_norm, grad_arrived = opening(
        normed, grad_outgoing.astype(jnp.bfloat16), local_experts, 1
    )
    full_norm = full_norm.reshape(-1, model_width)
    grad_arrived = grad_arrived.reshape(local_experts, -1, model_width)
    pad = ((0, 0), (0, 0), (0, LANES - head_size))
    wide_qkv = jnp.pad(qkv_weight.reshape(model_width, 3, head_size), pad)
    wide_qkv = wide_qkv.reshape(model_width, 3 * LANES)
    wide_proj = jnp.pad(proj_weight[0], ((0, LANES - head_size), (0, 0)))
    qkv_rows, qkv_cols, context, inverse = attend_forward(full_norm, wide_qkv, score_scale)
    attention = reduce_tensor(
        jnp.einsum("ks,kd->sd", context, wide_proj, preferred_element_type=jnp.float32)
        .astype(jnp.bfloat16)
        .reshape(spots, rows_dev, model_width),
        2,
    )
    mid = (tokens.astype(jnp.float32) + attention).astype(jnp.bfloat16)
    normal_mid, factor_mid = norm_parts(mid)
    mid_normed = normal_mid.astype(jnp.bfloat16)
    outgoing = jnp.dot(dispatch_rows, mid_normed, preferred_element_type=jnp.float32).astype(
        jnp.bfloat16
    )
    arrived = slots_out(outgoing, local_experts, 3).reshape(local_experts, -1, model_width)
    pre_act = jnp.einsum("end,edf->enf", arrived, up_weight, preferred_element_type=jnp.float32)
    hidden = gelu_value(pre_act).astype(jnp.bfloat16)
    expert_partial = jnp.einsum(
        "enf,efd->end", hidden, down_weight, preferred_element_type=jnp.float32
    )
    grad_hidden = jnp.einsum(
        "end,efd->enf", grad_arrived, down_weight, preferred_element_type=jnp.float32
    )
    grad_pre = (grad_hidden * gelu_slope(pre_act)).astype(jnp.bfloat16)
    grad_down = jnp.einsum(
        "enf,end->efd", hidden, grad_arrived, preferred_element_type=jnp.float32
    ).astype(jnp.bfloat16)
    grad_up = jnp.einsum(
        "end,enf->edf", arrived, grad_pre, preferred_element_type=jnp.float32
    ).astype(jnp.bfloat16)
    grad_partial = jnp.einsum(
        "enf,edf->end", grad_pre, up_weight, preferred_element_type=jnp.float32
    )
    grad_back, returned = slots_back(
        [
            part.astype(jnp.bfloat16).reshape(local_experts, spots, -1, model_width)
            for part in (grad_partial, expert_partial)
        ],
        5,
    )
    expert_first = jnp.einsum("pr,pd->rd", pick_first, returned, preferred_element_type=jnp.float32)
    expert_second = jnp.einsum(
        "pr,pd->rd", pick_second, returned, preferred_element_type=jnp.float32
    )
    mixed_rows = gate_weights[:, 0:1] * expert_first + gate_weights[:, 1:2] * expert_second
    layer_out = (mid.astype(jnp.float32) + mixed_rows).astype(jnp.bfloat16)
    gate_grad = jnp.stack(
        [jnp.sum(upstream * expert_first, axis=-1), jnp.sum(upstream * expert_second, axis=-1)],
        axis=1,
    )
    grad_norm = jnp.einsum(
        "pr,pd->rd", dispatch_rows, grad_back, preferred_element_type=jnp.float32
    )
    grad_mid = (upstream + norm_back(normal_mid, factor_mid, grad_norm)).astype(jnp.bfloat16)
    full_grad = gather_tensor(grad_mid, 6).reshape(-1, model_width)
    grad_weights = attend_backward(
        full_norm,
        full_grad,
        wide_proj,
        qkv_rows,
        qkv_cols,
        context,
        inverse,
        score_scale,
        head_size,
    )
    (grad_weights,) = reduce_groups(
        [grad_weights.reshape(group_count, -1, 4 * head_size)],
        7,
    )
    grad_qkv = grad_weights[:, None, : 3 * head_size]
    grad_proj = grad_weights[:, 3 * head_size :].T[None]
    return (layer_out, gate_grad, grad_qkv, grad_proj, grad_up, grad_down)


def solution(mesh):
    return jax.shard_map(
        shards,
        mesh=mesh,
        in_specs=(
            P(("dp", "tensor"), None),
            P(("dp", "tensor"), None),
            P(("dp", "tensor"), None),
            P(("dp", "tensor"), None),
            P(("dp", "tensor"), None),
            P(None, "tensor", None),
            P("tensor", None, None),
            P("dp", None, "tensor"),
            P("dp", "tensor", None),
        ),
        out_specs=(
            P(("dp", "tensor"), None),
            P(("dp", "tensor"), None),
            P("dp", "tensor", None),
            P("tensor", None, "dp"),
            P("dp", None, "tensor"),
            P("dp", "tensor", None),
        ),
        check_vma=False,
    )
```

```python
from functools import partial
import math

import jax
import jax.numpy as jnp
from jax import lax
from jax.experimental import pallas as pl
from jax.experimental.pallas import tpu as pltpu
from jax.sharding import PartitionSpec as P

CAP = 2


MESH = pl.DeviceIdType.MESH
VM = pl.BlockSpec(memory_space=pltpu.VMEM)
DMA = pltpu.SemaphoreType.DMA
PIECES = 4
SIDE = 4


def ring_places():
    spot = lax.axis_index("tensor")
    return spot, lax.div(spot, 2), lax.rem(spot, 2)


def level_at(level, steps, count):
    return lax.rem(level + steps + count, count)


def ring_peers(count):
    spot, level, side = ring_places()
    return (
        level_at(level, 1, count) * 2 + side,
        level_at(level, -1, count) * 2 + side,
        level * 2 + 1 - side,
    )


def plane_peer(along_x, step):
    me = lax.axis_index("dp")
    x, y = lax.div(me, SIDE), lax.rem(me, SIDE)
    if along_x:
        return lax.rem(x + step + SIDE, SIDE) * SIDE + y
    return x * SIDE + lax.rem(y + step + SIDE, SIDE)


def signal(axis, peer):
    pl.semaphore_signal(
        pltpu.get_barrier_semaphore(), inc=1, device_id={axis: peer}, device_id_type=MESH
    )


def greet_ring(count):
    peers = ring_peers(count)
    for peer in peers:
        signal("tensor", peer)
    return len(peers)


def greet_plane():
    for along_x in (True, False):
        for step in range(1, SIDE):
            signal("dp", plane_peer(along_x, step))
    return 2 * (SIDE - 1)


def greet_groups():
    me = lax.axis_index("dp")
    count = lax.axis_size("dp")

    def call(step, carry):
        signal("dp", lax.rem(me + step, count))
        return carry

    lax.fori_loop(1, count, call, 0)
    return count - 1


def await_peers(total):
    pl.semaphore_wait(pltpu.get_barrier_semaphore(), total)


def remote(source, target, send, recv, axis, peer):
    return pltpu.make_async_remote_copy(
        src_ref=source,
        dst_ref=target,
        send_sem=send,
        recv_sem=recv,
        device_id={axis: peer},
        device_id_type=MESH,
    )


def travels(way, step, piece, last):
    return step != last or (piece < PIECES // 2) == (way == 0)


def block_at(ref, spot, piece):
    if len(ref.shape) == 3:
        size = ref.shape[1] // PIECES
        return ref.at[spot, pl.ds(piece * size, size)]
    per = PIECES // ref.shape[0]
    size = ref.shape[2] // per
    return ref.at[piece // per, spot, pl.ds(piece % per * size, size)]


def rows_at(ref, piece):
    size = ref.shape[0] // PIECES
    return ref.at[pl.ds(piece * size, size)]


class GatherRing:
    def __init__(self, own_ref, full_ref, send, recv, give, take, mine, count):
        self.spot, self.level, self.side = ring_places()
        self.peers = ring_peers(count)
        self.refs = (own_ref, full_ref, send, recv, give, take, mine)
        self.count, self.reach = count, count // 2
        self.left, self.moved, self.settled = [], [], []

    def place(self, way, step):
        return level_at(self.level, -step if way == 0 else step, self.count)

    def hop(self, way, step, piece):
        own_ref, full_ref, send, recv = self.refs[:4]
        target = block_at(full_ref, self.place(way, step) * 2 + self.side, piece)
        source = rows_at(own_ref, piece) if step == 0 else target
        item = (way, step, piece)
        return remote(source, target, send.at[item], recv.at[item], "tensor", self.peers[way])

    def landed(self, way, step, piece):
        full_ref, send, recv = self.refs[1:4]
        target = block_at(full_ref, self.place(way, step + 1) * 2 + self.side, piece)
        item = (way, step, piece)
        return remote(target, target, send.at[item], recv.at[item], "tensor", self.peers[way])

    def across(self, way, step, piece, from_side):
        own_ref, full_ref, _, _, give, take, _ = self.refs
        target = block_at(full_ref, self.place(way, step) * 2 + from_side, piece)
        source = rows_at(own_ref, piece) if step == 0 else target
        item = (way, step, piece)
        return remote(source, target, give.at[item], take.at[item], "tensor", self.peers[2])

    def keep(self, piece):
        own_ref, full_ref, mine = self.refs[0], self.refs[1], self.refs[6]
        return pltpu.make_async_copy(
            rows_at(own_ref, piece), block_at(full_ref, self.spot, piece), mine.at[piece]
        )

    def begin(self):
        for piece in range(PIECES):
            for way in range(2):
                self.hop(way, 0, piece).start()
                self.left.append((way, 0, piece))
        for piece in range(PIECES):
            self.keep(piece).start()
            self.across(0, 0, piece, self.side).start()
            self.moved.append((0, 0, piece))

    def run(self, step):
        last = self.reach - 1
        for piece in range(PIECES):
            for way in range(2):
                if not travels(way, step, piece, last):
                    continue
                self.landed(way, step, piece).wait_recv()
                if step < last and travels(way, step + 1, piece, last):
                    self.hop(way, step + 1, piece).start()
                    self.left.append((way, step + 1, piece))
                self.across(way, step + 1, piece, self.side).start()
                self.moved.append((way, step + 1, piece))

    def settle(self, way, step):
        for item in [item for item in self.moved if item[:2] == (way, step)]:
            if step == 0:
                self.keep(item[2]).wait()
            self.across(*item, 1 - self.side).wait_recv()
            self.settled.append(item)

    def finish(self):
        for way, step in [(0, 0)] + [(way, step) for step in range(1, self.reach + 1) for way in range(2)]:
            if not any(item[:2] == (way, step) for item in self.settled):
                self.settle(way, step)
        for item in self.left:
            self.hop(*item).wait_send()
        for item in self.moved:
            self.across(*item, self.side).wait_send()


def gather_sems(count):
    reach = count // 2
    return [
        DMA((2, reach, PIECES)),
        DMA((2, reach, PIECES)),
        DMA((2, reach + 1, PIECES)),
        DMA((2, reach + 1, PIECES)),
        DMA((PIECES,)),
    ]


GATHER_SEMS = 5


def comm_call(kernel, out_shape, operands, scratch, ident):
    single = not isinstance(out_shape, list)
    return pl.pallas_call(
        kernel,
        out_shape=out_shape,
        in_specs=[VM] * len(operands),
        out_specs=VM if single else [VM] * len(out_shape),
        scratch_shapes=scratch,
        compiler_params=pltpu.CompilerParams(
            collective_id=ident, has_side_effects=True, vmem_limit_bytes=60 * 1024 * 1024
        ),
    )(*operands)


class Swap:
    def __init__(self, along_x, source_ref, target_ref, send, recv, mine):
        me = lax.axis_index("dp")
        self.me = lax.div(me, SIDE) if along_x else lax.rem(me, SIDE)
        self.along_x = along_x
        self.refs = (source_ref, target_ref, send, recv)
        self.keep = pltpu.make_async_copy(
            self.block(source_ref, self.me), self.block(target_ref, self.me), mine
        )

    def block(self, ref, index):
        size = ref.shape[0] // SIDE
        return ref.at[pl.ds(pl.multiple_of(index * size, size), size)]

    def copy(self, step, outward):
        source_ref, target_ref, send, recv = self.refs
        there = lax.rem(self.me + (step if outward else SIDE - step), SIDE)
        return remote(
            self.block(source_ref, there),
            self.block(target_ref, self.me if outward else there),
            send.at[step],
            recv.at[step],
            "dp",
            plane_peer(self.along_x, step if outward else -step),
        )

    def start(self):
        for step in range(1, SIDE):
            self.copy(step, True).start()
        self.keep.start()

    def finish(self):
        self.keep.wait()
        for step in range(1, SIDE):
            self.copy(step, False).wait_recv()
        for step in range(1, SIDE):
            self.copy(step, True).wait_send()


def swap_sems():
    return [DMA((SIDE,)), DMA((SIDE,)), DMA(())]


def reorder(rows, kind):
    count = rows.shape[0]
    target = lax.broadcasted_iota(jnp.int32, (count, count), 0)
    source = lax.broadcasted_iota(jnp.int32, (count, count), 1)
    extents = {"x": SIDE, "y": SIDE, "e": count // (SIDE * SIDE * CAP), "c": CAP}

    def code(index, order):
        digits = {}
        for name in reversed(order):
            digits[name] = index % extents[name]
            index = index // extents[name]
        total = digits["x"]
        for name in "yec":
            total = total * extents[name] + digits[name]
        return total

    before, after = kind
    orders = {"x": "xyec", "y": "yexc", "e": "eyxc"}
    pick = (code(target, orders[after]) == code(source, orders[before])).astype(rows.dtype)
    return jnp.dot(pick, rows, preferred_element_type=jnp.float32).astype(rows.dtype)


class SlotsOut:
    def __init__(self, source_ref, first, second, third, done, sems):
        self.refs = (first, second, third, done)
        self.by_x = Swap(True, source_ref, first, *sems[:3])
        self.by_y = Swap(False, second, third, *sems[3:])

    def begin(self):
        self.by_x.start()

    def middle(self):
        first, second = self.refs[:2]
        self.by_x.finish()
        second[...] = reorder(first[...], "xy")
        self.by_y.start()

    def finish(self):
        third, done = self.refs[2:]
        self.by_y.finish()
        done[...] = reorder(third[...], "ye")


def out_scratch(slots):
    return [pltpu.VMEM(slots.shape, slots.dtype)] * 4 + swap_sems() + swap_sems()


OUT_SCRATCH = 10


def slots_kernel(count, source_ref, full_ref, *scratch):
    await_peers(greet_plane() + greet_ring(count))
    out = SlotsOut(source_ref, *scratch[:4], scratch[4:OUT_SCRATCH])
    out.begin()
    out.middle()
    out.finish()
    ring = GatherRing(scratch[3], full_ref, *scratch[OUT_SCRATCH:], count)
    ring.begin()
    for step in range(count // 2):
        ring.run(step)
    ring.finish()


def slots_shape(slots, local_experts):
    spots = lax.axis_size("tensor")
    rows, width = slots.shape
    return jax.ShapeDtypeStruct((local_experts, spots, rows // local_experts, width), slots.dtype)


def slots_out(slots, local_experts, ident):
    count = lax.axis_size("tensor") // 2
    return comm_call(
        partial(slots_kernel, count),
        slots_shape(slots, local_experts),
        [slots],
        out_scratch(slots) + gather_sems(count),
        ident,
    )


def opening_kernel(count, own_ref, source_ref, full_ref, slots_ref, *scratch):
    await_peers(greet_plane() + greet_ring(count))
    out = SlotsOut(source_ref, *scratch[:4], scratch[4:OUT_SCRATCH])
    sems = scratch[OUT_SCRATCH:]
    first = GatherRing(own_ref, full_ref, *sems[:GATHER_SEMS], count)
    second = GatherRing(scratch[3], slots_ref, *sems[GATHER_SEMS:], count)
    out.begin()
    first.begin()
    first.run(0)
    out.middle()
    first.run(1)
    out.finish()
    for step in range(2, count // 2):
        first.run(step)
    second.begin()
    first.finish()
    for step in range(count // 2):
        second.run(step)
    second.finish()


def opening(own, slots, local_experts, ident):
    spots = lax.axis_size("tensor")
    count = spots // 2
    return comm_call(
        partial(opening_kernel, count),
        [
            jax.ShapeDtypeStruct((spots,) + own.shape, own.dtype),
            slots_shape(slots, local_experts),
        ],
        [own, slots],
        out_scratch(slots) + gather_sems(count) + gather_sems(count),
        ident,
    )


class ReduceRing:
    def __init__(self, part_ref, total_ref, pair, stage, landing, send, recv, give, take, count):
        self.spot, self.level, self.side = ring_places()
        self.peers = ring_peers(count)
        self.part, self.total, self.pair = part_ref, total_ref, pair
        self.stage, self.landing = stage, landing
        self.sems = (send, recv, give, take)
        self.count, self.reach = count, count // 2
        self.plan = [
            (way, step, piece)
            for step in range(self.reach)
            for piece in range(PIECES)
            for way in range(2)
            if travels(way, step, piece, 0)
        ]
        self.own = [(0, self.reach, piece) for piece in range(PIECES)]

    def place(self, way, step):
        steps = self.reach - step
        return level_at(self.level, steps if way == 0 else -steps, self.count)

    def rows(self, way, step, piece):
        size = self.stage.shape[2] // PIECES
        return way, step, pl.ds(piece * size, size)

    def across(self, way, step, piece):
        there = self.place(way, step)
        item = (way, step, piece)
        return remote(
            block_at(self.part, there * 2 + 1 - self.side, piece),
            rows_at(self.pair.at[there], piece),
            self.sems[2].at[item],
            self.sems[3].at[item],
            "tensor",
            self.peers[2],
        )

    def hop(self, way, step, piece):
        item = (way, step, piece)
        where = self.rows(*item)
        return remote(
            self.stage.at[where],
            self.landing.at[where],
            self.sems[0].at[item],
            self.sems[1].at[item],
            "tensor",
            self.peers[way],
        )

    def local_sum(self, way, step, piece):
        there = self.place(way, step)
        self.across(way, step, piece).wait_recv()
        mine = block_at(self.part, there * 2 + self.side, piece)[...]
        return mine.astype(jnp.float32) + rows_at(self.pair.at[there], piece)[...].astype(
            jnp.float32
        )

    def arrived(self, way, step, piece):
        self.hop(way, step, piece).wait_recv()
        return self.landing[self.rows(way, step, piece)].astype(jnp.float32)

    def begin(self):
        for item in self.plan + self.own:
            self.across(*item).start()

    def run_step(self, at):
        for way, step, piece in self.plan:
            if step != at:
                continue
            term = self.local_sum(way, step, piece)
            if step > 0 and travels(way, step - 1, piece, 0):
                term = term + self.arrived(way, step - 1, piece)
            self.stage[self.rows(way, step, piece)] = term.astype(self.stage.dtype)
            self.hop(way, step, piece).start()

    def close(self):
        for way, step, piece in self.own:
            term = self.local_sum(way, step, piece)
            for side in range(2):
                term = term + self.arrived(side, self.reach - 1, piece)
            rows_at(self.total, piece)[...] = term.astype(self.total.dtype)

    def run(self):
        for step in range(self.reach):
            self.run_step(step)
        self.close()

    def finish(self):
        for item in self.plan:
            self.hop(*item).wait_send()
        for item in self.plan + self.own:
            self.across(*item).wait_send()


def reduce_scratch(rows, width, dtype, count):
    reach = count // 2
    return [
        pltpu.VMEM((count, rows, width), dtype),
        pltpu.VMEM((2, reach, rows, width), dtype),
        pltpu.VMEM((2, reach, rows, width), dtype),
        DMA((2, reach, PIECES)),
        DMA((2, reach, PIECES)),
        DMA((2, reach + 1, PIECES)),
        DMA((2, reach + 1, PIECES)),
    ]


REDUCE_SCRATCH = 7


def reduce_kernel(count, part_ref, total_ref, *scratch):
    await_peers(greet_ring(count))
    ring = ReduceRing(part_ref, total_ref, *scratch, count)
    ring.begin()
    ring.run()
    ring.finish()


def reduce_tensor(part, ident):
    count = lax.axis_size("tensor") // 2
    _, rows, width = part.shape
    return comm_call(
        partial(reduce_kernel, count),
        jax.ShapeDtypeStruct((rows, width), jnp.float32),
        [part],
        reduce_scratch(rows, width, part.dtype, count),
        ident,
    )


class SlotsBack:
    def __init__(self, done, third, second, first, target_ref, sems):
        self.refs = (done, third, second, first)
        self.by_y = Swap(False, third, second, *sems[:3])
        self.by_x = Swap(True, first, target_ref, *sems[3:])

    def begin(self):
        done, third = self.refs[:2]
        third[...] = reorder(done[...], "ey")
        self.by_y.start()

    def middle(self):
        second, first = self.refs[2:]
        self.by_y.finish()
        first[...] = reorder(second[...], "yx")
        self.by_x.start()

    def finish(self):
        self.by_x.finish()


def back_kernel(count, parts, *refs):
    part_refs, refs = refs[:parts], refs[parts:]
    out_refs, refs = refs[:parts], refs[parts:]
    each = len(refs) // parts
    rings, backs = [], []
    for index in range(parts):
        mine = refs[index * each : (index + 1) * each]
        slots, ring = mine[:OUT_SCRATCH], mine[OUT_SCRATCH:]
        rings.append(ReduceRing(part_refs[index], slots[0], *ring, count))
        backs.append(SlotsBack(*slots[:4], out_refs[index], slots[4:]))
    await_peers(greet_plane() + greet_ring(count))
    for ring in rings:
        ring.begin()
    for ring, back in zip(rings, backs):
        ring.run()
        back.begin()
    for back in backs:
        back.middle()
    for back in backs:
        back.finish()
    for ring in rings:
        ring.finish()


def slots_back(part_list, ident):
    count = lax.axis_size("tensor") // 2
    scratch, shapes = [], []
    for part in part_list:
        experts, _, rows, width = part.shape
        slots = jax.ShapeDtypeStruct((experts * rows, width), part.dtype)
        shapes.append(slots)
        scratch += out_scratch(slots) + reduce_scratch(experts * rows, width, part.dtype, count)
    return comm_call(
        partial(back_kernel, count, len(part_list)), shapes, part_list, scratch, ident
    )


class Exchange:
    def __init__(self, source_ref, target_ref, send, recv, local_sem):
        self.me = lax.axis_index("dp")
        self.count = target_ref.shape[0]
        self.refs = (source_ref, target_ref, send, recv)
        self.keep = pltpu.make_async_copy(
            self.block(self.me), target_ref.at[self.me], local_sem
        )

    def block(self, index):
        source_ref, target_ref = self.refs[:2]
        size = target_ref.shape[1]
        return source_ref.at[pl.ds(pl.multiple_of(index * size, size), size)]

    def put(self, step):
        target_ref, send, recv = self.refs[1:]
        peer = lax.rem(self.me + step, self.count)
        return remote(
            self.block(peer), target_ref.at[self.me], send.at[step], recv.at[step], "dp", peer
        )

    def got(self, step):
        target_ref, send, recv = self.refs[1:]
        peer = lax.rem(self.me - step + self.count, self.count)
        return remote(
            self.block(peer), target_ref.at[peer], send.at[step], recv.at[step], "dp", peer
        )

    def start(self):
        def put_one(step, carry):
            self.put(step).start()
            return carry

        lax.fori_loop(1, self.count, put_one, 0)
        self.keep.start()

    def finish(self):
        self.keep.wait()

        def take_one(step, carry):
            self.got(step).wait_recv()
            self.put(step).wait_send()
            return carry

        lax.fori_loop(1, self.count, take_one, 0)


def exchange_sems(groups):
    return [DMA((groups,)), DMA((groups,)), DMA(())]
LANES = 128
QUERY_BLOCK = 512
KEY_BLOCK = 256
BACK_KEYS = 512


def mm(left, right):
    return jnp.dot(left, right, preferred_element_type=jnp.float32)


def project_rows(norm_ref, weight_ref, rows_ref, cols_ref, index):
    size = QUERY_BLOCK
    rows = pl.ds(pl.multiple_of(index * size, size), size)
    block = mm(norm_ref[rows, :], weight_ref[...])
    rows_ref[rows, :] = block.astype(rows_ref.dtype)
    cols_ref[:, rows] = block.T.astype(cols_ref.dtype)


def attend_block(rows_ref, cols_ref, context_ref, inverse_ref, raised_ref, index, scale):
    seq = rows_ref.shape[0]
    here = pl.ds(pl.multiple_of(index * QUERY_BLOCK, QUERY_BLOCK), QUERY_BLOCK)
    queries = cols_ref[0:LANES, here]
    total = jnp.zeros((1, QUERY_BLOCK), jnp.float32)
    for at in range(0, seq, KEY_BLOCK):
        scores = mm(rows_ref[at : at + KEY_BLOCK, LANES : 2 * LANES], queries)
        raised = jnp.exp(scores * scale)
        raised_ref[at : at + KEY_BLOCK, :] = raised
        total = total + jnp.sum(raised, axis=0, keepdims=True)
    inverse = 1.0 / total
    inverse_ref[:, here] = inverse
    context = jnp.zeros((LANES, QUERY_BLOCK), jnp.float32)
    for at in range(0, seq, KEY_BLOCK):
        shares = (raised_ref[at : at + KEY_BLOCK, :] * inverse).astype(jnp.bfloat16)
        context = context + mm(cols_ref[2 * LANES : 3 * LANES, at : at + KEY_BLOCK], shares)
    context_ref[:, here] = context.astype(context_ref.dtype)


def forward_kernel(scale, norm_ref, weight_ref, rows_ref, cols_ref, context_ref, inverse_ref, raised_ref):
    blocks = norm_ref.shape[0] // QUERY_BLOCK

    def project(index, carry):
        project_rows(norm_ref, weight_ref, rows_ref, cols_ref, index)
        return carry

    def attend(index, carry):
        attend_block(rows_ref, cols_ref, context_ref, inverse_ref, raised_ref, index, scale)
        return carry

    lax.fori_loop(0, blocks, project, 0)
    lax.fori_loop(0, blocks, attend, 0)


def attend_forward(full_norm, weight, scale):
    seq = full_norm.shape[0]
    return pl.pallas_call(
        partial(forward_kernel, scale),
        out_shape=[
            jax.ShapeDtypeStruct((seq, 3 * LANES), jnp.bfloat16),
            jax.ShapeDtypeStruct((3 * LANES, seq), jnp.bfloat16),
            jax.ShapeDtypeStruct((LANES, seq), jnp.bfloat16),
            jax.ShapeDtypeStruct((1, seq), jnp.float32),
        ],
        in_specs=[VM] * 2,
        out_specs=[VM] * 4,
        scratch_shapes=[pltpu.VMEM((seq, QUERY_BLOCK), jnp.float32)],
        compiler_params=pltpu.CompilerParams(vmem_limit_bytes=60 * 1024 * 1024),
    )(full_norm, weight)


def backward_block(
    rows_ref, cols_ref, context_ref, inverse_ref, grad_ref, proj_ref, gcols_ref, gkeys, gvals, level, scale
):
    seq = rows_ref.shape[0]
    size = gcols_ref.shape[0] // 3
    block = 2 * grad_ref.shape[1]
    here = pl.ds(pl.multiple_of(level * block, block), block)
    queries = cols_ref[0:LANES, here]
    query_rows = rows_ref[here, 0:LANES]
    wide = lax.dot_general(
        grad_ref[pl.ds(level * 2, 2)].reshape(block, grad_ref.shape[2]),
        proj_ref[...],
        (((1,), (1,)), ((), ())),
        preferred_element_type=jnp.float32,
    )
    grad_rows = wide.astype(jnp.bfloat16)
    grad_cols = wide.T.astype(jnp.bfloat16)
    inverse = inverse_ref[:, here]
    delta = jnp.sum(
        grad_cols.astype(jnp.float32) * context_ref[:, here].astype(jnp.float32),
        axis=0,
        keepdims=True,
    )
    grad_query = jnp.zeros((LANES, block), jnp.float32)
    for at in range(0, seq, BACK_KEYS):
        keys = slice(at, at + BACK_KEYS)
        scores = mm(rows_ref[keys, LANES : 2 * LANES], queries)
        shares = jnp.exp(scores * scale) * inverse
        grad_shares = mm(rows_ref[keys, 2 * LANES : 3 * LANES], grad_cols)
        grad_scores = (shares * (grad_shares - delta)).astype(jnp.bfloat16)
        gvals[keys, :] += mm(shares.astype(jnp.bfloat16), grad_rows)
        gkeys[keys, :] += mm(grad_scores, query_rows)
        grad_query = grad_query + mm(cols_ref[LANES : 2 * LANES, keys], grad_scores)
    gcols_ref[0:size, here] = (grad_query[0:size] * scale).astype(gcols_ref.dtype)


def flip_sums(gcols_ref, gkeys, gvals, scale):
    size = gcols_ref.shape[0] // 3
    for at in range(0, gkeys.shape[0], QUERY_BLOCK):
        there = slice(at, at + QUERY_BLOCK)
        key_cols = (gkeys[there, :] * scale).T
        value_cols = gvals[there, :].T
        gcols_ref[size : 2 * size, there] = key_cols[0:size].astype(gcols_ref.dtype)
        gcols_ref[2 * size : 3 * size, there] = value_cols[0:size].astype(gcols_ref.dtype)


def weight_sums(norm_ref, grad_ref, context_ref, gcols_ref, weights_ref, first, last):
    size = gcols_ref.shape[0] // 3
    step = 2 * LANES
    spare = jnp.zeros((3 * LANES - 4 * size, step), jnp.float32)

    def one(index, carry):
        where = pl.ds(pl.multiple_of(index * step, step), step)
        for_qkv = mm(gcols_ref[...], norm_ref[:, where])
        rows = grad_ref[:, :, where].reshape(norm_ref.shape[0], step)
        for_proj = mm(context_ref[0:size, :], rows)
        block = jnp.concatenate([for_qkv, for_proj, spare], axis=0).T
        weights_ref[where, :] = block[:, 0 : 4 * size].astype(weights_ref.dtype)
        return carry

    lax.fori_loop(first, last, one, 0)


def closing_kernel(
    count,
    scale,
    own_ref,
    part_ref,
    norm_ref,
    proj_ref,
    rows_ref,
    cols_ref,
    context_ref,
    inverse_ref,
    slots_ref,
    sum_ref,
    grad_ref,
    gcols_ref,
    gkeys,
    gvals,
    weights_ref,
    landing,
    *refs,
):
    ring_sems, refs = refs[:GATHER_SEMS], refs[GATHER_SEMS:]
    swap_refs, refs = refs[:3], refs[3:]
    slots, reduce = refs[:OUT_SCRATCH], refs[OUT_SCRATCH:]
    _, level, _ = ring_places()
    ring = GatherRing(own_ref, grad_ref, *ring_sems, count)
    back_ring = ReduceRing(part_ref, slots[0], *reduce, count)
    back = SlotsBack(*slots[:4], slots_ref, slots[4:])
    swap = Exchange(weights_ref, landing, *swap_refs)
    total = greet_groups() + greet_ring(count)
    gkeys[...] = jnp.zeros_like(gkeys)
    gvals[...] = jnp.zeros_like(gvals)
    await_peers(total)

    def block(level):
        backward_block(
            rows_ref, cols_ref, context_ref, inverse_ref, grad_ref, proj_ref, gcols_ref, gkeys, gvals, level, scale
        )

    reach = count // 2
    ring.begin()
    ring.settle(0, 0)
    block(level)
    back_ring.begin()

    for step in range(reach):
        ring.run(step)
        for way in range(2):
            ring.settle(way, step + 1)
        if step < reach - 1:

            def one_way(way, carry, step=step):
                away = (2 * way - 1) * (step + 1)
                block(level_at(level, away, count))
                return carry

            lax.fori_loop(0, 2, one_way, 0)
        else:
            back_ring.run_step(0)
            block(level_at(level, reach, count))
    flip_sums(gcols_ref, gkeys, gvals, scale)
    back_ring.run_step(1)
    parts = norm_ref.shape[1] // (2 * LANES)
    weight_sums(norm_ref, grad_ref, context_ref, gcols_ref, weights_ref, 0, parts // 2)
    back_ring.run_step(2)
    weight_sums(norm_ref, grad_ref, context_ref, gcols_ref, weights_ref, parts // 2, parts)
    swap.start()
    back_ring.run_step(3)
    back_ring.close()
    back.begin()
    back.middle()
    swap.finish()
    sums = landing[0].astype(jnp.float32)
    for group in range(1, landing.shape[0]):
        sums = sums + landing[group].astype(jnp.float32)
    sum_ref[...] = sums
    back.finish()
    ring.finish()
    back_ring.finish()


def closing(own, part, norm, proj, rows, cols, context, inverse, scale, size, ident):
    spots = lax.axis_size("tensor")
    count = spots // 2
    groups = lax.axis_size("dp")
    seq, width = norm.shape
    experts, _, slot_rows, _ = part.shape
    slots = jax.ShapeDtypeStruct((experts * slot_rows, width), part.dtype)
    return comm_call(
        partial(closing_kernel, count, scale),
        [slots, jax.ShapeDtypeStruct((width // groups, 4 * size), jnp.float32)],
        [own, part, norm, proj, rows, cols, context, inverse],
        [
            pltpu.VMEM((spots,) + own.shape, own.dtype),
            pltpu.VMEM((3 * size, seq), jnp.bfloat16),
            pltpu.VMEM((seq, LANES), jnp.float32),
            pltpu.VMEM((seq, LANES), jnp.float32),
            pltpu.VMEM((width, 4 * size), jnp.bfloat16),
            pltpu.VMEM((groups, width // groups, 4 * size), jnp.bfloat16),
        ]
        + gather_sems(count)
        + exchange_sems(groups)
        + out_scratch(slots)
        + reduce_scratch(experts * slot_rows, width, part.dtype, count),
        ident,
    )


epsilon = 1e-06
half_root = 1.0 / math.sqrt(2.0)
bell_scale = 1.0 / math.sqrt(2.0 * math.pi)


def norm_parts(row_block):
    widened = row_block.astype(jnp.float32)
    center = widened - jnp.mean(widened, axis=-1, keepdims=True)
    factor = lax.rsqrt(jnp.mean(center * center, axis=-1, keepdims=True) + epsilon)
    return (center * factor, factor)


def norm_back(normal_rows, factor, upstream):
    mean_up = jnp.mean(upstream, axis=-1, keepdims=True)
    mean_mix = jnp.mean(upstream * normal_rows, axis=-1, keepdims=True)
    return factor * (upstream - mean_up - normal_rows * mean_mix)


def gelu_value(pre_act):
    return 0.5 * pre_act * (1.0 + lax.erf(pre_act * half_root))


def gelu_slope(pre_act):
    return (
        0.5 * (1.0 + lax.erf(pre_act * half_root))
        + pre_act * jnp.exp(-0.5 * pre_act * pre_act) * bell_scale
    )


def shards(
    tokens,
    cotangent,
    gate_weights,
    routes,
    slot_index,
    qkv_weight,
    proj_weight,
    up_weight,
    down_weight,
):
    rows_dev, model_width = tokens.shape
    head_size = qkv_weight.shape[2] // 3
    score_scale = head_size ** (-0.5)
    group_count = lax.axis_size("dp")
    spots = lax.axis_size("tensor")
    local_experts = up_weight.shape[0]
    places = group_count * local_experts * CAP
    normal_in, factor_in = norm_parts(tokens)
    normed = normal_in.astype(jnp.bfloat16)
    slot_code = jnp.where(slot_index >= 0, routes * CAP + slot_index, -1)
    positions = jnp.arange(places, dtype=jnp.int32)
    pick_both = (slot_code[None, :, :] == positions[:, None, None]).astype(jnp.bfloat16)
    pick_first = pick_both[:, :, 0]
    pick_second = pick_both[:, :, 1]
    dispatch_rows = pick_first + pick_second
    upstream = cotangent.astype(jnp.float32)
    grad_first = (gate_weights[:, 0:1] * upstream).astype(jnp.bfloat16)
    grad_second = (gate_weights[:, 1:2] * upstream).astype(jnp.bfloat16)
    grad_outgoing = jnp.dot(pick_first, grad_first, preferred_element_type=jnp.float32) + jnp.dot(
        pick_second, grad_second, preferred_element_type=jnp.float32
    )
    full_norm, grad_arrived = opening(
        normed, grad_outgoing.astype(jnp.bfloat16), local_experts, 1
    )
    full_norm = full_norm.reshape(-1, model_width)
    grad_arrived = grad_arrived.reshape(local_experts, -1, model_width)
    pad = ((0, 0), (0, 0), (0, LANES - head_size))
    wide_qkv = jnp.pad(qkv_weight.reshape(model_width, 3, head_size), pad)
    wide_qkv = wide_qkv.reshape(model_width, 3 * LANES)
    wide_proj = jnp.pad(proj_weight[0], ((0, LANES - head_size), (0, 0)))
    qkv_rows, qkv_cols, context, inverse = attend_forward(full_norm, wide_qkv, score_scale)
    attention = reduce_tensor(
        jnp.einsum("ks,kd->sd", context, wide_proj, preferred_element_type=jnp.float32)
        .astype(jnp.bfloat16)
        .reshape(spots, rows_dev, model_width),
        2,
    )
    mid = (tokens.astype(jnp.float32) + attention).astype(jnp.bfloat16)
    normal_mid, factor_mid = norm_parts(mid)
    mid_normed = normal_mid.astype(jnp.bfloat16)
    outgoing = jnp.dot(dispatch_rows, mid_normed, preferred_element_type=jnp.float32).astype(
        jnp.bfloat16
    )
    arrived = slots_out(outgoing, local_experts, 3).reshape(local_experts, -1, model_width)
    pre_act = jnp.einsum("end,edf->enf", arrived, up_weight, preferred_element_type=jnp.float32)
    hidden = gelu_value(pre_act).astype(jnp.bfloat16)
    expert_partial = jnp.einsum(
        "enf,efd->end", hidden, down_weight, preferred_element_type=jnp.float32
    )
    grad_hidden = jnp.einsum(
        "end,efd->enf", grad_arrived, down_weight, preferred_element_type=jnp.float32
    )
    grad_pre = (grad_hidden * gelu_slope(pre_act)).astype(jnp.bfloat16)
    grad_down = jnp.einsum(
        "enf,end->efd", hidden, grad_arrived, preferred_element_type=jnp.float32
    ).astype(jnp.bfloat16)
    grad_up = jnp.einsum(
        "end,enf->edf", arrived, grad_pre, preferred_element_type=jnp.float32
    ).astype(jnp.bfloat16)
    grad_partial = jnp.einsum(
        "enf,edf->end", grad_pre, up_weight, preferred_element_type=jnp.float32
    )
    grad_partial, expert_partial = (
        part.astype(jnp.bfloat16).reshape(local_experts, spots, -1, model_width)
        for part in (grad_partial, expert_partial)
    )
    (grad_back,) = slots_back([grad_partial], 5)
    grad_norm = jnp.einsum(
        "pr,pd->rd", dispatch_rows, grad_back, preferred_element_type=jnp.float32
    )
    grad_mid = (upstream + norm_back(normal_mid, factor_mid, grad_norm)).astype(jnp.bfloat16)
    returned, grad_weights = closing(
        grad_mid,
        expert_partial,
        full_norm,
        wide_proj,
        qkv_rows,
        qkv_cols,
        context,
        inverse,
        score_scale,
        head_size,
        6,
    )
    expert_first = jnp.einsum("pr,pd->rd", pick_first, returned, preferred_element_type=jnp.float32)
    expert_second = jnp.einsum(
        "pr,pd->rd", pick_second, returned, preferred_element_type=jnp.float32
    )
    mixed_rows = gate_weights[:, 0:1] * expert_first + gate_weights[:, 1:2] * expert_second
    layer_out = (mid.astype(jnp.float32) + mixed_rows).astype(jnp.bfloat16)
    gate_grad = jnp.stack(
        [jnp.sum(upstream * expert_first, axis=-1), jnp.sum(upstream * expert_second, axis=-1)],
        axis=1,
    )
    grad_qkv = grad_weights[:, None, : 3 * head_size]
    grad_proj = grad_weights[:, 3 * head_size :].T[None]
    return (layer_out, gate_grad, grad_qkv, grad_proj, grad_up, grad_down)


def solution(mesh):
    return jax.shard_map(
        shards,
        mesh=mesh,
        in_specs=(
            P(("dp", "tensor"), None),
            P(("dp", "tensor"), None),
            P(("dp", "tensor"), None),
            P(("dp", "tensor"), None),
            P(("dp", "tensor"), None),
            P(None, "tensor", None),
            P("tensor", None, None),
            P("dp", None, "tensor"),
            P("dp", "tensor", None),
        ),
        out_specs=(
            P(("dp", "tensor"), None),
            P(("dp", "tensor"), None),
            P("dp", "tensor", None),
            P("tensor", None, "dp"),
            P("dp", None, "tensor"),
            P("dp", "tensor", None),
        ),
        check_vma=False,
    )
```

```python
from functools import partial
import math

import jax
import jax.numpy as jnp
from jax import lax
from jax.experimental import pallas as pl
from jax.experimental.pallas import tpu as pltpu
from jax.sharding import PartitionSpec as P

CAP = 2


MESH = pl.DeviceIdType.MESH
VM = pl.BlockSpec(memory_space=pltpu.VMEM)
DMA = pltpu.SemaphoreType.DMA
PIECES = 4
SIDE = 4


def ring_places():
    spot = lax.axis_index("tensor")
    return spot, lax.div(spot, 2), lax.rem(spot, 2)


def level_at(level, steps, count):
    return lax.rem(level + steps + count, count)


def ring_peers(count):
    spot, level, side = ring_places()
    return (
        level_at(level, 1, count) * 2 + side,
        level_at(level, -1, count) * 2 + side,
        level * 2 + 1 - side,
    )


def plane_peer(along_x, step):
    me = lax.axis_index("dp")
    x, y = lax.div(me, SIDE), lax.rem(me, SIDE)
    if along_x:
        return lax.rem(x + step + SIDE, SIDE) * SIDE + y
    return x * SIDE + lax.rem(y + step + SIDE, SIDE)


def signal(axis, peer):
    pl.semaphore_signal(
        pltpu.get_barrier_semaphore(), inc=1, device_id={axis: peer}, device_id_type=MESH
    )


def greet_ring(count):
    peers = ring_peers(count)
    for peer in peers:
        signal("tensor", peer)
    return len(peers)


def greet_plane():
    for along_x in (True, False):
        for step in range(1, SIDE):
            signal("dp", plane_peer(along_x, step))
    return 2 * (SIDE - 1)


def greet_groups():
    me = lax.axis_index("dp")
    count = lax.axis_size("dp")

    def call(step, carry):
        signal("dp", lax.rem(me + step, count))
        return carry

    lax.fori_loop(1, count, call, 0)
    return count - 1


def await_peers(total):
    pl.semaphore_wait(pltpu.get_barrier_semaphore(), total)


def remote(source, target, send, recv, axis, peer):
    return pltpu.make_async_remote_copy(
        src_ref=source,
        dst_ref=target,
        send_sem=send,
        recv_sem=recv,
        device_id={axis: peer},
        device_id_type=MESH,
    )


def travels(way, step, piece, last):
    return step != last or (piece < PIECES // 2) == (way == 0)


def block_at(ref, spot, piece):
    if len(ref.shape) == 3:
        size = ref.shape[1] // PIECES
        return ref.at[spot, pl.ds(piece * size, size)]
    per = PIECES // ref.shape[0]
    size = ref.shape[2] // per
    return ref.at[piece // per, spot, pl.ds(piece % per * size, size)]


def rows_at(ref, piece):
    size = ref.shape[0] // PIECES
    return ref.at[pl.ds(piece * size, size)]


class GatherRing:
    def __init__(self, own_ref, full_ref, send, recv, give, take, mine, count):
        self.spot, self.level, self.side = ring_places()
        self.peers = ring_peers(count)
        self.refs = (own_ref, full_ref, send, recv, give, take, mine)
        self.count, self.reach = count, count // 2
        self.left, self.moved, self.settled = [], [], []

    def place(self, way, step):
        return level_at(self.level, -step if way == 0 else step, self.count)

    def hop(self, way, step, piece):
        own_ref, full_ref, send, recv = self.refs[:4]
        target = block_at(full_ref, self.place(way, step) * 2 + self.side, piece)
        source = rows_at(own_ref, piece) if step == 0 else target
        item = (way, step, piece)
        return remote(source, target, send.at[item], recv.at[item], "tensor", self.peers[way])

    def landed(self, way, step, piece):
        full_ref, send, recv = self.refs[1:4]
        target = block_at(full_ref, self.place(way, step + 1) * 2 + self.side, piece)
        item = (way, step, piece)
        return remote(target, target, send.at[item], recv.at[item], "tensor", self.peers[way])

    def across(self, way, step, piece, from_side):
        own_ref, full_ref, _, _, give, take, _ = self.refs
        target = block_at(full_ref, self.place(way, step) * 2 + from_side, piece)
        source = rows_at(own_ref, piece) if step == 0 else target
        item = (way, step, piece)
        return remote(source, target, give.at[item], take.at[item], "tensor", self.peers[2])

    def keep(self, piece):
        own_ref, full_ref, mine = self.refs[0], self.refs[1], self.refs[6]
        return pltpu.make_async_copy(
            rows_at(own_ref, piece), block_at(full_ref, self.spot, piece), mine.at[piece]
        )

    def begin(self):
        for piece in range(PIECES):
            for way in range(2):
                self.hop(way, 0, piece).start()
                self.left.append((way, 0, piece))
        for piece in range(PIECES):
            self.keep(piece).start()
            self.across(0, 0, piece, self.side).start()
            self.moved.append((0, 0, piece))

    def run(self, step):
        last = self.reach - 1
        for piece in range(PIECES):
            for way in range(2):
                if not travels(way, step, piece, last):
                    continue
                self.landed(way, step, piece).wait_recv()
                if step < last and travels(way, step + 1, piece, last):
                    self.hop(way, step + 1, piece).start()
                    self.left.append((way, step + 1, piece))
                self.across(way, step + 1, piece, self.side).start()
                self.moved.append((way, step + 1, piece))

    def settle(self, way, step):
        for item in [item for item in self.moved if item[:2] == (way, step)]:
            if step == 0:
                self.keep(item[2]).wait()
            self.across(*item, 1 - self.side).wait_recv()
            self.settled.append(item)

    def finish(self):
        for way, step in [(0, 0)] + [(way, step) for step in range(1, self.reach + 1) for way in range(2)]:
            if not any(item[:2] == (way, step) for item in self.settled):
                self.settle(way, step)
        for item in self.left:
            self.hop(*item).wait_send()
        for item in self.moved:
            self.across(*item, self.side).wait_send()


def gather_sems(count):
    reach = count // 2
    return [
        DMA((2, reach, PIECES)),
        DMA((2, reach, PIECES)),
        DMA((2, reach + 1, PIECES)),
        DMA((2, reach + 1, PIECES)),
        DMA((PIECES,)),
    ]


GATHER_SEMS = 5


def comm_call(kernel, out_shape, operands, scratch, ident):
    single = not isinstance(out_shape, list)
    return pl.pallas_call(
        kernel,
        out_shape=out_shape,
        in_specs=[VM] * len(operands),
        out_specs=VM if single else [VM] * len(out_shape),
        scratch_shapes=scratch,
        compiler_params=pltpu.CompilerParams(
            collective_id=ident, has_side_effects=True, vmem_limit_bytes=60 * 1024 * 1024
        ),
    )(*operands)


class Swap:
    def __init__(self, along_x, source_ref, target_ref, send, recv, mine):
        me = lax.axis_index("dp")
        self.me = lax.div(me, SIDE) if along_x else lax.rem(me, SIDE)
        self.along_x = along_x
        self.refs = (source_ref, target_ref, send, recv)
        self.keep = pltpu.make_async_copy(
            self.block(source_ref, self.me), self.block(target_ref, self.me), mine
        )

    def block(self, ref, index):
        size = ref.shape[0] // SIDE
        return ref.at[pl.ds(pl.multiple_of(index * size, size), size)]

    def copy(self, step, outward):
        source_ref, target_ref, send, recv = self.refs
        there = lax.rem(self.me + (step if outward else SIDE - step), SIDE)
        return remote(
            self.block(source_ref, there),
            self.block(target_ref, self.me if outward else there),
            send.at[step],
            recv.at[step],
            "dp",
            plane_peer(self.along_x, step if outward else -step),
        )

    def start(self):
        for step in range(1, SIDE):
            self.copy(step, True).start()
        self.keep.start()

    def finish(self):
        self.keep.wait()
        for step in range(1, SIDE):
            self.copy(step, False).wait_recv()
        for step in range(1, SIDE):
            self.copy(step, True).wait_send()


def swap_sems():
    return [DMA((SIDE,)), DMA((SIDE,)), DMA(())]


def reorder(rows, kind):
    count = rows.shape[0]
    target = lax.broadcasted_iota(jnp.int32, (count, count), 0)
    source = lax.broadcasted_iota(jnp.int32, (count, count), 1)
    extents = {"x": SIDE, "y": SIDE, "e": count // (SIDE * SIDE * CAP), "c": CAP}

    def code(index, order):
        digits = {}
        for name in reversed(order):
            digits[name] = index % extents[name]
            index = index // extents[name]
        total = digits["x"]
        for name in "yec":
            total = total * extents[name] + digits[name]
        return total

    before, after = kind
    orders = {"x": "xyec", "y": "yexc", "e": "eyxc"}
    pick = (code(target, orders[after]) == code(source, orders[before])).astype(rows.dtype)
    return jnp.dot(pick, rows, preferred_element_type=jnp.float32).astype(rows.dtype)


class SlotsOut:
    def __init__(self, source_ref, first, second, third, done, sems):
        self.refs = (first, second, third, done)
        self.by_x = Swap(True, source_ref, first, *sems[:3])
        self.by_y = Swap(False, second, third, *sems[3:])

    def begin(self):
        self.by_x.start()

    def middle(self):
        first, second = self.refs[:2]
        self.by_x.finish()
        second[...] = reorder(first[...], "xy")
        self.by_y.start()

    def finish(self):
        third, done = self.refs[2:]
        self.by_y.finish()
        done[...] = reorder(third[...], "ye")


def out_scratch(slots):
    return [pltpu.VMEM(slots.shape, slots.dtype)] * 4 + swap_sems() + swap_sems()


OUT_SCRATCH = 10


def slots_shape(slots, local_experts):
    spots = lax.axis_size("tensor")
    rows, width = slots.shape
    return jax.ShapeDtypeStruct((local_experts, spots, rows // local_experts, width), slots.dtype)


class ReduceRing:
    def __init__(self, part_ref, total_ref, pair, stage, landing, send, recv, give, take, count):
        self.spot, self.level, self.side = ring_places()
        self.peers = ring_peers(count)
        self.part, self.total, self.pair = part_ref, total_ref, pair
        self.stage, self.landing = stage, landing
        self.sems = (send, recv, give, take)
        self.count, self.reach = count, count // 2
        self.plan = [
            (way, step, piece)
            for step in range(self.reach)
            for piece in range(PIECES)
            for way in range(2)
            if travels(way, step, piece, 0)
        ]
        self.own = [(0, self.reach, piece) for piece in range(PIECES)]

    def place(self, way, step):
        steps = self.reach - step
        return level_at(self.level, steps if way == 0 else -steps, self.count)

    def rows(self, way, step, piece):
        size = self.stage.shape[2] // PIECES
        return way, step, pl.ds(piece * size, size)

    def across(self, way, step, piece):
        there = self.place(way, step)
        item = (way, step, piece)
        return remote(
            block_at(self.part, there * 2 + 1 - self.side, piece),
            rows_at(self.pair.at[there], piece),
            self.sems[2].at[item],
            self.sems[3].at[item],
            "tensor",
            self.peers[2],
        )

    def hop(self, way, step, piece):
        item = (way, step, piece)
        where = self.rows(*item)
        return remote(
            self.stage.at[where],
            self.landing.at[where],
            self.sems[0].at[item],
            self.sems[1].at[item],
            "tensor",
            self.peers[way],
        )

    def local_sum(self, way, step, piece):
        there = self.place(way, step)
        self.across(way, step, piece).wait_recv()
        mine = block_at(self.part, there * 2 + self.side, piece)[...]
        return mine.astype(jnp.float32) + rows_at(self.pair.at[there], piece)[...].astype(
            jnp.float32
        )

    def arrived(self, way, step, piece):
        self.hop(way, step, piece).wait_recv()
        return self.landing[self.rows(way, step, piece)].astype(jnp.float32)

    def begin_step(self, at):
        for item in self.plan + self.own:
            if item[1] == at:
                self.across(*item).start()

    def begin(self):
        for step in range(self.reach + 1):
            self.begin_step(step)

    def run_step(self, at):
        for way, step, piece in self.plan:
            if step != at:
                continue
            term = self.local_sum(way, step, piece)
            if step > 0 and travels(way, step - 1, piece, 0):
                term = term + self.arrived(way, step - 1, piece)
            self.stage[self.rows(way, step, piece)] = term.astype(self.stage.dtype)
            self.hop(way, step, piece).start()

    def close(self):
        for way, step, piece in self.own:
            term = self.local_sum(way, step, piece)
            for side in range(2):
                term = term + self.arrived(side, self.reach - 1, piece)
            rows_at(self.total, piece)[...] = term.astype(self.total.dtype)

    def run(self):
        for step in range(self.reach):
            self.run_step(step)
        self.close()

    def finish(self):
        for item in self.plan:
            self.hop(*item).wait_send()
        for item in self.plan + self.own:
            self.across(*item).wait_send()


def reduce_scratch(rows, width, dtype, count):
    reach = count // 2
    return [
        pltpu.VMEM((count, rows, width), dtype),
        pltpu.VMEM((2, reach, rows, width), dtype),
        pltpu.VMEM((2, reach, rows, width), dtype),
        DMA((2, reach, PIECES)),
        DMA((2, reach, PIECES)),
        DMA((2, reach + 1, PIECES)),
        DMA((2, reach + 1, PIECES)),
    ]


REDUCE_SCRATCH = 7


class SlotsBack:
    def __init__(self, done, third, second, first, target_ref, sems):
        self.refs = (done, third, second, first)
        self.by_y = Swap(False, third, second, *sems[:3])
        self.by_x = Swap(True, first, target_ref, *sems[3:])

    def begin(self):
        done, third = self.refs[:2]
        third[...] = reorder(done[...], "ey")
        self.by_y.start()

    def middle(self):
        second, first = self.refs[2:]
        self.by_y.finish()
        first[...] = reorder(second[...], "yx")
        self.by_x.start()

    def finish(self):
        self.by_x.finish()


def back_kernel(count, parts, *refs):
    part_refs, refs = refs[:parts], refs[parts:]
    out_refs, refs = refs[:parts], refs[parts:]
    each = len(refs) // parts
    rings, backs = [], []
    for index in range(parts):
        mine = refs[index * each : (index + 1) * each]
        slots, ring = mine[:OUT_SCRATCH], mine[OUT_SCRATCH:]
        rings.append(ReduceRing(part_refs[index], slots[0], *ring, count))
        backs.append(SlotsBack(*slots[:4], out_refs[index], slots[4:]))
    await_peers(greet_plane() + greet_ring(count))
    for ring in rings:
        ring.begin()
    for ring, back in zip(rings, backs):
        ring.run()
        back.begin()
    for back in backs:
        back.middle()
    for back in backs:
        back.finish()
    for ring in rings:
        ring.finish()


def slots_back(part_list, ident):
    count = lax.axis_size("tensor") // 2
    scratch, shapes = [], []
    for part in part_list:
        experts, _, rows, width = part.shape
        slots = jax.ShapeDtypeStruct((experts * rows, width), part.dtype)
        shapes.append(slots)
        scratch += out_scratch(slots) + reduce_scratch(experts * rows, width, part.dtype, count)
    return comm_call(
        partial(back_kernel, count, len(part_list)), shapes, part_list, scratch, ident
    )


class Exchange:
    def __init__(self, source_ref, target_ref, send, recv, local_sem):
        self.me = lax.axis_index("dp")
        self.count = target_ref.shape[0]
        self.refs = (source_ref, target_ref, send, recv)
        self.keep = pltpu.make_async_copy(
            self.block(self.me), target_ref.at[self.me], local_sem
        )

    def block(self, index):
        source_ref, target_ref = self.refs[:2]
        size = target_ref.shape[1]
        return source_ref.at[pl.ds(pl.multiple_of(index * size, size), size)]

    def put(self, step):
        target_ref, send, recv = self.refs[1:]
        peer = lax.rem(self.me + step, self.count)
        return remote(
            self.block(peer), target_ref.at[self.me], send.at[step], recv.at[step], "dp", peer
        )

    def got(self, step):
        target_ref, send, recv = self.refs[1:]
        peer = lax.rem(self.me - step + self.count, self.count)
        return remote(
            self.block(peer), target_ref.at[peer], send.at[step], recv.at[step], "dp", peer
        )

    def start(self):
        def put_one(step, carry):
            self.put(step).start()
            return carry

        lax.fori_loop(1, self.count, put_one, 0)
        self.keep.start()

    def finish(self):
        self.keep.wait()

        def take_one(step, carry):
            self.got(step).wait_recv()
            self.put(step).wait_send()
            return carry

        lax.fori_loop(1, self.count, take_one, 0)


def exchange_sems(groups):
    return [DMA((groups,)), DMA((groups,)), DMA(())]
LANES = 128
QUERY_BLOCK = 512
KEY_BLOCK = 256
BACK_KEYS = 512


def mm(left, right):
    return jnp.dot(left, right, preferred_element_type=jnp.float32)


def project_rows(norm_ref, weight_ref, rows_ref, cols_ref, level):
    size = 2 * norm_ref.shape[1]
    rows = pl.ds(pl.multiple_of(level * size, size), size)
    taken = norm_ref[pl.ds(level * 2, 2)].reshape(size, norm_ref.shape[2])
    block = mm(taken, weight_ref[...])
    rows_ref[rows, :] = block.astype(rows_ref.dtype)
    cols_ref[:, rows] = block.T.astype(cols_ref.dtype)


def attend_block(
    rows_ref, cols_ref, context_ref, inverse_ref, raised_ref, context_rows, index, scale
):
    seq = rows_ref.shape[0]
    here = pl.ds(pl.multiple_of(index * QUERY_BLOCK, QUERY_BLOCK), QUERY_BLOCK)
    queries = cols_ref[0:LANES, here]
    total = jnp.zeros((1, QUERY_BLOCK), jnp.float32)
    for at in range(0, seq, KEY_BLOCK):
        scores = mm(rows_ref[at : at + KEY_BLOCK, LANES : 2 * LANES], queries)
        raised = jnp.exp(scores * scale)
        raised_ref[at : at + KEY_BLOCK, :] = raised
        total = total + jnp.sum(raised, axis=0, keepdims=True)
    inverse = 1.0 / total
    inverse_ref[:, here] = inverse
    context = jnp.zeros((LANES, QUERY_BLOCK), jnp.float32)
    for at in range(0, seq, KEY_BLOCK):
        shares = (raised_ref[at : at + KEY_BLOCK, :] * inverse).astype(jnp.bfloat16)
        context = context + mm(cols_ref[2 * LANES : 3 * LANES, at : at + KEY_BLOCK], shares)
    context_ref[:, here] = context.astype(context_ref.dtype)
    context_rows[here, :] = context.T.astype(context_rows.dtype)


def front_kernel(
    count,
    scale,
    own_ref,
    source_ref,
    tokens_ref,
    dispatch_ref,
    weight_ref,
    proj_ref,
    norm_ref,
    gslots_ref,
    rows_ref,
    cols_ref,
    context_ref,
    inverse_ref,
    mid_ref,
    arrived_ref,
    raised_ref,
    context_rows,
    part_ref,
    total_ref,
    outgoing_ref,
    *refs,
):
    _, level, _ = ring_places()
    reach = count // 2
    grads, refs = refs[:OUT_SCRATCH], refs[OUT_SCRATCH:]
    slots, refs = refs[:OUT_SCRATCH], refs[OUT_SCRATCH:]
    sems, refs = refs[: 3 * GATHER_SEMS], refs[3 * GATHER_SEMS :]
    grads_out = SlotsOut(source_ref, *grads[:4], grads[4:])
    slots_out = SlotsOut(outgoing_ref, *slots[:4], slots[4:])
    first = GatherRing(own_ref, norm_ref, *sems[:GATHER_SEMS], count)
    second = GatherRing(grads[3], gslots_ref, *sems[GATHER_SEMS : 2 * GATHER_SEMS], count)
    third = GatherRing(slots[3], arrived_ref, *sems[2 * GATHER_SEMS :], count)
    reduce = ReduceRing(part_ref, total_ref, *refs, count)
    await_peers(greet_plane() + greet_ring(count))

    def both_ways(act, distance):
        def one_way(way, carry):
            act(level_at(level, (2 * way - 1) * distance, count))
            return carry

        lax.fori_loop(0, 2, one_way, 0)

    def project(place):
        project_rows(norm_ref, weight_ref, rows_ref, cols_ref, place)

    def attend(index, carry):
        attend_block(
            rows_ref, cols_ref, context_ref, inverse_ref, raised_ref, context_rows, index, scale
        )
        return carry

    def fill_part(place):
        size = 2 * part_ref.shape[1]
        rows = pl.ds(pl.multiple_of(place * size, size), size)
        block = mm(context_rows[rows, :], proj_ref[...]).astype(part_ref.dtype)
        part_ref[pl.ds(place * 2, 2)] = block.reshape(2, part_ref.shape[1], part_ref.shape[2])

    grads_out.begin()
    first.begin()
    first.settle(0, 0)
    project(level)
    for step in range(reach):
        first.run(step)
        if step == 0:
            grads_out.middle()
        if step == 1:
            grads_out.finish()
        if step == reach - 1:
            second.begin()
        for way in range(2):
            first.settle(way, step + 1)
        if step < reach - 1:
            both_ways(project, step + 1)
        else:
            project(level_at(level, reach, count))
    blocks = norm_ref.shape[0] * norm_ref.shape[1] // QUERY_BLOCK
    lax.fori_loop(0, blocks // 2, attend, 0)
    second.run(0)
    second.run(1)
    lax.fori_loop(blocks // 2, blocks, attend, 0)
    second.run(2)
    fill_part(level_at(level, reach, count))
    reduce.begin_step(0)
    both_ways(fill_part, reach - 1)
    reduce.begin_step(1)
    second.run(3)
    reduce.run_step(0)
    both_ways(fill_part, reach - 2)
    reduce.begin_step(2)
    reduce.run_step(1)
    both_ways(fill_part, reach - 3)
    reduce.begin_step(3)
    fill_part(level)
    reduce.begin_step(reach)
    reduce.run_step(2)
    reduce.run_step(3)
    first.finish()
    second.finish()
    reduce.close()
    mid = (tokens_ref[...].astype(jnp.float32) + total_ref[...]).astype(mid_ref.dtype)
    mid_ref[...] = mid
    normal, _ = norm_parts(mid)
    outgoing_ref[...] = mm(dispatch_ref[...], normal.astype(jnp.bfloat16)).astype(
        outgoing_ref.dtype
    )
    slots_out.begin()
    slots_out.middle()
    slots_out.finish()
    third.begin()
    for step in range(reach):
        third.run(step)
    third.finish()
    reduce.finish()


def front(own, grad_slots, tokens, dispatch, weight, proj, scale, local_experts, ident):
    spots = lax.axis_size("tensor")
    count = spots // 2
    rows, width = own.shape
    seq = spots * rows
    return comm_call(
        partial(front_kernel, count, scale),
        [
            jax.ShapeDtypeStruct((spots,) + own.shape, own.dtype),
            slots_shape(grad_slots, local_experts),
            jax.ShapeDtypeStruct((seq, 3 * LANES), jnp.bfloat16),
            jax.ShapeDtypeStruct((3 * LANES, seq), jnp.bfloat16),
            jax.ShapeDtypeStruct((LANES, seq), jnp.bfloat16),
            jax.ShapeDtypeStruct((1, seq), jnp.float32),
            jax.ShapeDtypeStruct(tokens.shape, tokens.dtype),
            slots_shape(grad_slots, local_experts),
        ],
        [own, grad_slots, tokens, dispatch, weight, proj],
        [
            pltpu.VMEM((seq, QUERY_BLOCK), jnp.float32),
            pltpu.VMEM((seq, LANES), jnp.bfloat16),
            pltpu.VMEM((spots, rows, width), jnp.bfloat16),
            pltpu.VMEM((rows, width), jnp.float32),
            pltpu.VMEM(grad_slots.shape, grad_slots.dtype),
        ]
        + out_scratch(grad_slots)
        + out_scratch(grad_slots)
        + gather_sems(count) * 3
        + reduce_scratch(rows, width, jnp.bfloat16, count),
        ident,
    )


def backward_block(
    rows_ref, cols_ref, context_ref, inverse_ref, grad_ref, proj_ref, gcols_ref, gkeys, gvals, level, scale
):
    seq = rows_ref.shape[0]
    size = gcols_ref.shape[0] // 3
    block = 2 * grad_ref.shape[1]
    here = pl.ds(pl.multiple_of(level * block, block), block)
    queries = cols_ref[0:LANES, here]
    query_rows = rows_ref[here, 0:LANES]
    wide = lax.dot_general(
        grad_ref[pl.ds(level * 2, 2)].reshape(block, grad_ref.shape[2]),
        proj_ref[...],
        (((1,), (1,)), ((), ())),
        preferred_element_type=jnp.float32,
    )
    grad_rows = wide.astype(jnp.bfloat16)
    grad_cols = wide.T.astype(jnp.bfloat16)
    inverse = inverse_ref[:, here]
    delta = jnp.sum(
        grad_cols.astype(jnp.float32) * context_ref[:, here].astype(jnp.float32),
        axis=0,
        keepdims=True,
    )
    grad_query = jnp.zeros((LANES, block), jnp.float32)
    for at in range(0, seq, BACK_KEYS):
        keys = slice(at, at + BACK_KEYS)
        scores = mm(rows_ref[keys, LANES : 2 * LANES], queries)
        shares = jnp.exp(scores * scale) * inverse
        grad_shares = mm(rows_ref[keys, 2 * LANES : 3 * LANES], grad_cols)
        grad_scores = (shares * (grad_shares - delta)).astype(jnp.bfloat16)
        gvals[keys, :] += mm(shares.astype(jnp.bfloat16), grad_rows)
        gkeys[keys, :] += mm(grad_scores, query_rows)
        grad_query = grad_query + mm(cols_ref[LANES : 2 * LANES, keys], grad_scores)
    gcols_ref[0:size, here] = (grad_query[0:size] * scale).astype(gcols_ref.dtype)


def flip_sums(gcols_ref, gkeys, gvals, scale):
    size = gcols_ref.shape[0] // 3
    for at in range(0, gkeys.shape[0], QUERY_BLOCK):
        there = slice(at, at + QUERY_BLOCK)
        key_cols = (gkeys[there, :] * scale).T
        value_cols = gvals[there, :].T
        gcols_ref[size : 2 * size, there] = key_cols[0:size].astype(gcols_ref.dtype)
        gcols_ref[2 * size : 3 * size, there] = value_cols[0:size].astype(gcols_ref.dtype)


def weight_sums(norm_ref, grad_ref, context_ref, gcols_ref, weights_ref, first, last):
    size = gcols_ref.shape[0] // 3
    step = 2 * LANES
    spare = jnp.zeros((3 * LANES - 4 * size, step), jnp.float32)

    def one(index, carry):
        where = pl.ds(pl.multiple_of(index * step, step), step)
        for_qkv = mm(gcols_ref[...], norm_ref[:, where])
        rows = grad_ref[:, :, where].reshape(norm_ref.shape[0], step)
        for_proj = mm(context_ref[0:size, :], rows)
        block = jnp.concatenate([for_qkv, for_proj, spare], axis=0).T
        weights_ref[where, :] = block[:, 0 : 4 * size].astype(weights_ref.dtype)
        return carry

    lax.fori_loop(first, last, one, 0)


def closing_kernel(
    count,
    scale,
    own_ref,
    part_ref,
    norm_ref,
    proj_ref,
    rows_ref,
    cols_ref,
    context_ref,
    inverse_ref,
    slots_ref,
    sum_ref,
    grad_ref,
    gcols_ref,
    gkeys,
    gvals,
    weights_ref,
    landing,
    *refs,
):
    ring_sems, refs = refs[:GATHER_SEMS], refs[GATHER_SEMS:]
    swap_refs, refs = refs[:3], refs[3:]
    slots, reduce = refs[:OUT_SCRATCH], refs[OUT_SCRATCH:]
    _, level, _ = ring_places()
    ring = GatherRing(own_ref, grad_ref, *ring_sems, count)
    back_ring = ReduceRing(part_ref, slots[0], *reduce, count)
    back = SlotsBack(*slots[:4], slots_ref, slots[4:])
    swap = Exchange(weights_ref, landing, *swap_refs)
    total = greet_groups() + greet_ring(count)
    gkeys[...] = jnp.zeros_like(gkeys)
    gvals[...] = jnp.zeros_like(gvals)
    await_peers(total)

    def block(level):
        backward_block(
            rows_ref, cols_ref, context_ref, inverse_ref, grad_ref, proj_ref, gcols_ref, gkeys, gvals, level, scale
        )

    reach = count // 2
    ring.begin()
    ring.settle(0, 0)
    block(level)
    back_ring.begin()

    for step in range(reach):
        ring.run(step)
        for way in range(2):
            ring.settle(way, step + 1)
        if step < reach - 1:

            def one_way(way, carry, step=step):
                away = (2 * way - 1) * (step + 1)
                block(level_at(level, away, count))
                return carry

            lax.fori_loop(0, 2, one_way, 0)
        else:
            back_ring.run_step(0)
            block(level_at(level, reach, count))
    flip_sums(gcols_ref, gkeys, gvals, scale)
    back_ring.run_step(1)
    parts = norm_ref.shape[1] // (2 * LANES)
    weight_sums(norm_ref, grad_ref, context_ref, gcols_ref, weights_ref, 0, parts // 2)
    back_ring.run_step(2)
    weight_sums(norm_ref, grad_ref, context_ref, gcols_ref, weights_ref, parts // 2, parts)
    swap.start()
    back_ring.run_step(3)
    back_ring.close()
    back.begin()
    back.middle()
    swap.finish()
    sums = landing[0].astype(jnp.float32)
    for group in range(1, landing.shape[0]):
        sums = sums + landing[group].astype(jnp.float32)
    sum_ref[...] = sums
    back.finish()
    ring.finish()
    back_ring.finish()


def closing(own, part, norm, proj, rows, cols, context, inverse, scale, size, ident):
    spots = lax.axis_size("tensor")
    count = spots // 2
    groups = lax.axis_size("dp")
    seq, width = norm.shape
    experts, _, slot_rows, _ = part.shape
    slots = jax.ShapeDtypeStruct((experts * slot_rows, width), part.dtype)
    return comm_call(
        partial(closing_kernel, count, scale),
        [slots, jax.ShapeDtypeStruct((width // groups, 4 * size), jnp.float32)],
        [own, part, norm, proj, rows, cols, context, inverse],
        [
            pltpu.VMEM((spots,) + own.shape, own.dtype),
            pltpu.VMEM((3 * size, seq), jnp.bfloat16),
            pltpu.VMEM((seq, LANES), jnp.float32),
            pltpu.VMEM((seq, LANES), jnp.float32),
            pltpu.VMEM((width, 4 * size), jnp.bfloat16),
            pltpu.VMEM((groups, width // groups, 4 * size), jnp.bfloat16),
        ]
        + gather_sems(count)
        + exchange_sems(groups)
        + out_scratch(slots)
        + reduce_scratch(experts * slot_rows, width, part.dtype, count),
        ident,
    )


epsilon = 1e-06
half_root = 1.0 / math.sqrt(2.0)
bell_scale = 1.0 / math.sqrt(2.0 * math.pi)


def norm_parts(row_block):
    widened = row_block.astype(jnp.float32)
    center = widened - jnp.mean(widened, axis=-1, keepdims=True)
    factor = lax.rsqrt(jnp.mean(center * center, axis=-1, keepdims=True) + epsilon)
    return (center * factor, factor)


def norm_back(normal_rows, factor, upstream):
    mean_up = jnp.mean(upstream, axis=-1, keepdims=True)
    mean_mix = jnp.mean(upstream * normal_rows, axis=-1, keepdims=True)
    return factor * (upstream - mean_up - normal_rows * mean_mix)


def gelu_value(pre_act):
    return 0.5 * pre_act * (1.0 + lax.erf(pre_act * half_root))


def gelu_slope(pre_act):
    return (
        0.5 * (1.0 + lax.erf(pre_act * half_root))
        + pre_act * jnp.exp(-0.5 * pre_act * pre_act) * bell_scale
    )


def shards(
    tokens,
    cotangent,
    gate_weights,
    routes,
    slot_index,
    qkv_weight,
    proj_weight,
    up_weight,
    down_weight,
):
    rows_dev, model_width = tokens.shape
    head_size = qkv_weight.shape[2] // 3
    score_scale = head_size ** (-0.5)
    group_count = lax.axis_size("dp")
    spots = lax.axis_size("tensor")
    local_experts = up_weight.shape[0]
    places = group_count * local_experts * CAP
    normal_in, factor_in = norm_parts(tokens)
    normed = normal_in.astype(jnp.bfloat16)
    slot_code = jnp.where(slot_index >= 0, routes * CAP + slot_index, -1)
    positions = jnp.arange(places, dtype=jnp.int32)
    pick_both = (slot_code[None, :, :] == positions[:, None, None]).astype(jnp.bfloat16)
    pick_first = pick_both[:, :, 0]
    pick_second = pick_both[:, :, 1]
    dispatch_rows = pick_first + pick_second
    upstream = cotangent.astype(jnp.float32)
    grad_first = (gate_weights[:, 0:1] * upstream).astype(jnp.bfloat16)
    grad_second = (gate_weights[:, 1:2] * upstream).astype(jnp.bfloat16)
    grad_outgoing = jnp.dot(pick_first, grad_first, preferred_element_type=jnp.float32) + jnp.dot(
        pick_second, grad_second, preferred_element_type=jnp.float32
    )
    pad = ((0, 0), (0, 0), (0, LANES - head_size))
    wide_qkv = jnp.pad(qkv_weight.reshape(model_width, 3, head_size), pad)
    wide_qkv = wide_qkv.reshape(model_width, 3 * LANES)
    wide_proj = jnp.pad(proj_weight[0], ((0, LANES - head_size), (0, 0)))
    full_norm, grad_arrived, qkv_rows, qkv_cols, context, inverse, mid, arrived = front(
        normed,
        grad_outgoing.astype(jnp.bfloat16),
        tokens,
        dispatch_rows,
        wide_qkv,
        wide_proj,
        score_scale,
        local_experts,
        1,
    )
    full_norm = full_norm.reshape(-1, model_width)
    grad_arrived = grad_arrived.reshape(local_experts, -1, model_width)
    arrived = arrived.reshape(local_experts, -1, model_width)
    normal_mid, factor_mid = norm_parts(mid)
    pre_act = jnp.einsum("end,edf->enf", arrived, up_weight, preferred_element_type=jnp.float32)
    hidden = gelu_value(pre_act).astype(jnp.bfloat16)
    expert_partial = jnp.einsum(
        "enf,efd->end", hidden, down_weight, preferred_element_type=jnp.float32
    )
    grad_hidden = jnp.einsum(
        "end,efd->enf", grad_arrived, down_weight, preferred_element_type=jnp.float32
    )
    grad_pre = (grad_hidden * gelu_slope(pre_act)).astype(jnp.bfloat16)
    grad_down = jnp.einsum(
        "enf,end->efd", hidden, grad_arrived, preferred_element_type=jnp.float32
    ).astype(jnp.bfloat16)
    grad_up = jnp.einsum(
        "end,enf->edf", arrived, grad_pre, preferred_element_type=jnp.float32
    ).astype(jnp.bfloat16)
    grad_partial = jnp.einsum(
        "enf,edf->end", grad_pre, up_weight, preferred_element_type=jnp.float32
    )
    grad_partial, expert_partial = (
        part.astype(jnp.bfloat16).reshape(local_experts, spots, -1, model_width)
        for part in (grad_partial, expert_partial)
    )
    (grad_back,) = slots_back([grad_partial], 5)
    grad_norm = jnp.einsum(
        "pr,pd->rd", dispatch_rows, grad_back, preferred_element_type=jnp.float32
    )
    grad_mid = (upstream + norm_back(normal_mid, factor_mid, grad_norm)).astype(jnp.bfloat16)
    returned, grad_weights = closing(
        grad_mid,
        expert_partial,
        full_norm,
        wide_proj,
        qkv_rows,
        qkv_cols,
        context,
        inverse,
        score_scale,
        head_size,
        6,
    )
    expert_first = jnp.einsum("pr,pd->rd", pick_first, returned, preferred_element_type=jnp.float32)
    expert_second = jnp.einsum(
        "pr,pd->rd", pick_second, returned, preferred_element_type=jnp.float32
    )
    mixed_rows = gate_weights[:, 0:1] * expert_first + gate_weights[:, 1:2] * expert_second
    layer_out = (mid.astype(jnp.float32) + mixed_rows).astype(jnp.bfloat16)
    gate_grad = jnp.stack(
        [jnp.sum(upstream * expert_first, axis=-1), jnp.sum(upstream * expert_second, axis=-1)],
        axis=1,
    )
    grad_qkv = grad_weights[:, None, : 3 * head_size]
    grad_proj = grad_weights[:, 3 * head_size :].T[None]
    return (layer_out, gate_grad, grad_qkv, grad_proj, grad_up, grad_down)


def solution(mesh):
    return jax.shard_map(
        shards,
        mesh=mesh,
        in_specs=(
            P(("dp", "tensor"), None),
            P(("dp", "tensor"), None),
            P(("dp", "tensor"), None),
            P(("dp", "tensor"), None),
            P(("dp", "tensor"), None),
            P(None, "tensor", None),
            P("tensor", None, None),
            P("dp", None, "tensor"),
            P("dp", "tensor", None),
        ),
        out_specs=(
            P(("dp", "tensor"), None),
            P(("dp", "tensor"), None),
            P("dp", "tensor", None),
            P("tensor", None, "dp"),
            P("dp", None, "tensor"),
            P("dp", "tensor", None),
        ),
        check_vma=False,
    )
```

```python
from functools import partial
import math

import jax
import jax.numpy as jnp
from jax import lax
from jax.experimental import pallas as pl
from jax.experimental.pallas import tpu as pltpu
from jax.sharding import PartitionSpec as P

CAP = 2


MESH = pl.DeviceIdType.MESH
VM = pl.BlockSpec(memory_space=pltpu.VMEM)
DMA = pltpu.SemaphoreType.DMA
PIECES = 4
SIDE = 4


def ring_places():
    spot = lax.axis_index("tensor")
    return spot, lax.div(spot, 2), lax.rem(spot, 2)


def level_at(level, steps, count):
    return lax.rem(level + steps + count, count)


def ring_peers(count):
    spot, level, side = ring_places()
    return (
        level_at(level, 1, count) * 2 + side,
        level_at(level, -1, count) * 2 + side,
        level * 2 + 1 - side,
    )


def plane_peer(along_x, step):
    me = lax.axis_index("dp")
    x, y = lax.div(me, SIDE), lax.rem(me, SIDE)
    if along_x:
        return lax.rem(x + step + SIDE, SIDE) * SIDE + y
    return x * SIDE + lax.rem(y + step + SIDE, SIDE)


def signal(axis, peer):
    pl.semaphore_signal(
        pltpu.get_barrier_semaphore(), inc=1, device_id={axis: peer}, device_id_type=MESH
    )


def greet_ring(count):
    peers = ring_peers(count)
    for peer in peers:
        signal("tensor", peer)
    return len(peers)


def greet_plane():
    for along_x in (True, False):
        for step in range(1, SIDE):
            signal("dp", plane_peer(along_x, step))
    return 2 * (SIDE - 1)


def greet_groups():
    me = lax.axis_index("dp")
    count = lax.axis_size("dp")

    def call(step, carry):
        signal("dp", lax.rem(me + step, count))
        return carry

    lax.fori_loop(1, count, call, 0)
    return count - 1


def await_peers(total):
    pl.semaphore_wait(pltpu.get_barrier_semaphore(), total)


def remote(source, target, send, recv, axis, peer):
    return pltpu.make_async_remote_copy(
        src_ref=source,
        dst_ref=target,
        send_sem=send,
        recv_sem=recv,
        device_id={axis: peer},
        device_id_type=MESH,
    )


def travels(way, step, piece, last):
    return step != last or (piece < PIECES // 2) == (way == 0)


def block_at(ref, spot, piece):
    if len(ref.shape) == 3:
        size = ref.shape[1] // PIECES
        return ref.at[spot, pl.ds(piece * size, size)]
    per = PIECES // ref.shape[0]
    size = ref.shape[2] // per
    return ref.at[piece // per, spot, pl.ds(piece % per * size, size)]


def rows_at(ref, piece):
    size = ref.shape[0] // PIECES
    return ref.at[pl.ds(piece * size, size)]


class GatherRing:
    def __init__(self, own_ref, full_ref, send, recv, give, take, mine, count):
        self.spot, self.level, self.side = ring_places()
        self.peers = ring_peers(count)
        self.refs = (own_ref, full_ref, send, recv, give, take, mine)
        self.count, self.reach = count, count // 2
        self.left, self.moved, self.settled = [], [], []

    def place(self, way, step):
        return level_at(self.level, -step if way == 0 else step, self.count)

    def hop(self, way, step, piece):
        own_ref, full_ref, send, recv = self.refs[:4]
        target = block_at(full_ref, self.place(way, step) * 2 + self.side, piece)
        source = rows_at(own_ref, piece) if step == 0 else target
        item = (way, step, piece)
        return remote(source, target, send.at[item], recv.at[item], "tensor", self.peers[way])

    def landed(self, way, step, piece):
        full_ref, send, recv = self.refs[1:4]
        target = block_at(full_ref, self.place(way, step + 1) * 2 + self.side, piece)
        item = (way, step, piece)
        return remote(target, target, send.at[item], recv.at[item], "tensor", self.peers[way])

    def across(self, way, step, piece, from_side):
        own_ref, full_ref, _, _, give, take, _ = self.refs
        target = block_at(full_ref, self.place(way, step) * 2 + from_side, piece)
        source = rows_at(own_ref, piece) if step == 0 else target
        item = (way, step, piece)
        return remote(source, target, give.at[item], take.at[item], "tensor", self.peers[2])

    def keep(self, piece):
        own_ref, full_ref, mine = self.refs[0], self.refs[1], self.refs[6]
        return pltpu.make_async_copy(
            rows_at(own_ref, piece), block_at(full_ref, self.spot, piece), mine.at[piece]
        )

    def begin(self):
        for piece in range(PIECES):
            for way in range(2):
                self.hop(way, 0, piece).start()
                self.left.append((way, 0, piece))
        for piece in range(PIECES):
            self.keep(piece).start()
            self.across(0, 0, piece, self.side).start()
            self.moved.append((0, 0, piece))

    def run(self, step):
        last = self.reach - 1
        for piece in range(PIECES):
            for way in range(2):
                if not travels(way, step, piece, last):
                    continue
                self.landed(way, step, piece).wait_recv()
                if step < last and travels(way, step + 1, piece, last):
                    self.hop(way, step + 1, piece).start()
                    self.left.append((way, step + 1, piece))
                self.across(way, step + 1, piece, self.side).start()
                self.moved.append((way, step + 1, piece))

    def settle(self, way, step):
        for item in [item for item in self.moved if item[:2] == (way, step)]:
            if step == 0:
                self.keep(item[2]).wait()
            self.across(*item, 1 - self.side).wait_recv()
            self.settled.append(item)

    def finish(self):
        for way, step in [(0, 0)] + [(way, step) for step in range(1, self.reach + 1) for way in range(2)]:
            if not any(item[:2] == (way, step) for item in self.settled):
                self.settle(way, step)
        for item in self.left:
            self.hop(*item).wait_send()
        for item in self.moved:
            self.across(*item, self.side).wait_send()


def gather_sems(count):
    reach = count // 2
    return [
        DMA((2, reach, PIECES)),
        DMA((2, reach, PIECES)),
        DMA((2, reach + 1, PIECES)),
        DMA((2, reach + 1, PIECES)),
        DMA((PIECES,)),
    ]


GATHER_SEMS = 5


def comm_call(kernel, out_shape, operands, scratch, ident, far_in=0, far_out=0):
    far = pl.BlockSpec(memory_space=pl.ANY)
    return pl.pallas_call(
        kernel,
        out_shape=out_shape,
        in_specs=[VM] * (len(operands) - far_in) + [far] * far_in,
        out_specs=[VM] * (len(out_shape) - far_out) + [far] * far_out,
        scratch_shapes=scratch,
        compiler_params=pltpu.CompilerParams(
            collective_id=ident, has_side_effects=True, vmem_limit_bytes=60 * 1024 * 1024
        ),
    )(*operands)


class Swap:
    def __init__(self, along_x, source_ref, target_ref, send, recv, mine):
        me = lax.axis_index("dp")
        self.me = lax.div(me, SIDE) if along_x else lax.rem(me, SIDE)
        self.along_x = along_x
        self.refs = (source_ref, target_ref, send, recv)
        self.keep = pltpu.make_async_copy(
            self.block(source_ref, self.me), self.block(target_ref, self.me), mine
        )

    def block(self, ref, index):
        size = ref.shape[0] // SIDE
        return ref.at[pl.ds(pl.multiple_of(index * size, size), size)]

    def copy(self, step, outward):
        source_ref, target_ref, send, recv = self.refs
        there = lax.rem(self.me + (step if outward else SIDE - step), SIDE)
        return remote(
            self.block(source_ref, there),
            self.block(target_ref, self.me if outward else there),
            send.at[step],
            recv.at[step],
            "dp",
            plane_peer(self.along_x, step if outward else -step),
        )

    def start(self):
        for step in range(1, SIDE):
            self.copy(step, True).start()
        self.keep.start()

    def finish(self):
        self.keep.wait()
        for step in range(1, SIDE):
            self.copy(step, False).wait_recv()
        for step in range(1, SIDE):
            self.copy(step, True).wait_send()


def swap_sems():
    return [DMA((SIDE,)), DMA((SIDE,)), DMA(())]


def reorder(rows, kind):
    count = rows.shape[0]
    target = lax.broadcasted_iota(jnp.int32, (count, count), 0)
    source = lax.broadcasted_iota(jnp.int32, (count, count), 1)
    extents = {"x": SIDE, "y": SIDE, "e": count // (SIDE * SIDE * CAP), "c": CAP}

    def code(index, order):
        digits = {}
        for name in reversed(order):
            digits[name] = index % extents[name]
            index = index // extents[name]
        total = digits["x"]
        for name in "yec":
            total = total * extents[name] + digits[name]
        return total

    before, after = kind
    orders = {"x": "xyec", "y": "yexc", "e": "eyxc"}
    pick = (code(target, orders[after]) == code(source, orders[before])).astype(rows.dtype)
    return jnp.dot(pick, rows, preferred_element_type=jnp.float32).astype(rows.dtype)


class SlotsOut:
    def __init__(self, source_ref, first, second, third, done, sems):
        self.refs = (first, second, third, done)
        self.by_x = Swap(True, source_ref, first, *sems[:3])
        self.by_y = Swap(False, second, third, *sems[3:])

    def begin(self):
        self.by_x.start()

    def middle(self):
        first, second = self.refs[:2]
        self.by_x.finish()
        second[...] = reorder(first[...], "xy")
        self.by_y.start()

    def finish(self):
        third, done = self.refs[2:]
        self.by_y.finish()
        done[...] = reorder(third[...], "ye")


def out_scratch(slots):
    return [pltpu.VMEM(slots.shape, slots.dtype)] * 4 + swap_sems() + swap_sems()


OUT_SCRATCH = 10


def slots_shape(slots, local_experts):
    spots = lax.axis_size("tensor")
    rows, width = slots.shape
    return jax.ShapeDtypeStruct((local_experts, spots, rows // local_experts, width), slots.dtype)


class ReduceRing:
    def __init__(self, part_ref, total_ref, pair, stage, landing, send, recv, give, take, count):
        self.spot, self.level, self.side = ring_places()
        self.peers = ring_peers(count)
        self.part, self.total, self.pair = part_ref, total_ref, pair
        self.stage, self.landing = stage, landing
        self.sems = (send, recv, give, take)
        self.count, self.reach = count, count // 2
        self.plan = [
            (way, step, piece)
            for step in range(self.reach)
            for piece in range(PIECES)
            for way in range(2)
            if travels(way, step, piece, 0)
        ]
        self.own = [(0, self.reach, piece) for piece in range(PIECES)]

    def place(self, way, step):
        steps = self.reach - step
        return level_at(self.level, steps if way == 0 else -steps, self.count)

    def rows(self, way, step, piece):
        size = self.stage.shape[2] // PIECES
        return way, step, pl.ds(piece * size, size)

    def across(self, way, step, piece):
        there = self.place(way, step)
        item = (way, step, piece)
        return remote(
            block_at(self.part, there * 2 + 1 - self.side, piece),
            rows_at(self.pair.at[there], piece),
            self.sems[2].at[item],
            self.sems[3].at[item],
            "tensor",
            self.peers[2],
        )

    def hop(self, way, step, piece):
        item = (way, step, piece)
        where = self.rows(*item)
        return remote(
            self.stage.at[where],
            self.landing.at[where],
            self.sems[0].at[item],
            self.sems[1].at[item],
            "tensor",
            self.peers[way],
        )

    def local_sum(self, way, step, piece):
        there = self.place(way, step)
        self.across(way, step, piece).wait_recv()
        mine = block_at(self.part, there * 2 + self.side, piece)[...]
        return mine.astype(jnp.float32) + rows_at(self.pair.at[there], piece)[...].astype(
            jnp.float32
        )

    def arrived(self, way, step, piece):
        self.hop(way, step, piece).wait_recv()
        return self.landing[self.rows(way, step, piece)].astype(jnp.float32)

    def begin_step(self, at):
        for item in self.plan + self.own:
            if item[1] == at:
                self.across(*item).start()

    def begin(self):
        for step in range(self.reach + 1):
            self.begin_step(step)

    def run_step(self, at):
        for way, step, piece in self.plan:
            if step != at:
                continue
            term = self.local_sum(way, step, piece)
            if step > 0 and travels(way, step - 1, piece, 0):
                term = term + self.arrived(way, step - 1, piece)
            self.stage[self.rows(way, step, piece)] = term.astype(self.stage.dtype)
            self.hop(way, step, piece).start()

    def close(self):
        for way, step, piece in self.own:
            term = self.local_sum(way, step, piece)
            for side in range(2):
                term = term + self.arrived(side, self.reach - 1, piece)
            rows_at(self.total, piece)[...] = term.astype(self.total.dtype)

    def run(self):
        for step in range(self.reach):
            self.run_step(step)
        self.close()

    def finish(self):
        for item in self.plan:
            self.hop(*item).wait_send()
        for item in self.plan + self.own:
            self.across(*item).wait_send()


def reduce_scratch(rows, width, dtype, count):
    reach = count // 2
    return [
        pltpu.VMEM((count, rows, width), dtype),
        pltpu.VMEM((2, reach, rows, width), dtype),
        pltpu.VMEM((2, reach, rows, width), dtype),
        DMA((2, reach, PIECES)),
        DMA((2, reach, PIECES)),
        DMA((2, reach + 1, PIECES)),
        DMA((2, reach + 1, PIECES)),
    ]


REDUCE_SCRATCH = 7


class SlotsBack:
    def __init__(self, done, third, second, first, target_ref, sems):
        self.refs = (done, third, second, first)
        self.by_y = Swap(False, third, second, *sems[:3])
        self.by_x = Swap(True, first, target_ref, *sems[3:])

    def begin(self):
        done, third = self.refs[:2]
        third[...] = reorder(done[...], "ey")
        self.by_y.start()

    def middle(self):
        second, first = self.refs[2:]
        self.by_y.finish()
        first[...] = reorder(second[...], "yx")
        self.by_x.start()

    def finish(self):
        self.by_x.finish()


class Exchange:
    def __init__(self, source_ref, target_ref, send, recv, local_sem):
        self.me = lax.axis_index("dp")
        self.count = target_ref.shape[0]
        self.refs = (source_ref, target_ref, send, recv)
        self.keep = pltpu.make_async_copy(
            self.block(self.me), target_ref.at[self.me], local_sem
        )

    def block(self, index):
        source_ref, target_ref = self.refs[:2]
        size = target_ref.shape[1]
        return source_ref.at[pl.ds(pl.multiple_of(index * size, size), size)]

    def put(self, step):
        target_ref, send, recv = self.refs[1:]
        peer = lax.rem(self.me + step, self.count)
        return remote(
            self.block(peer), target_ref.at[self.me], send.at[step], recv.at[step], "dp", peer
        )

    def got(self, step):
        target_ref, send, recv = self.refs[1:]
        peer = lax.rem(self.me - step + self.count, self.count)
        return remote(
            self.block(peer), target_ref.at[peer], send.at[step], recv.at[step], "dp", peer
        )

    def start(self):
        def put_one(step, carry):
            self.put(step).start()
            return carry

        lax.fori_loop(1, self.count, put_one, 0)
        self.keep.start()

    def finish(self):
        self.keep.wait()

        def take_one(step, carry):
            self.got(step).wait_recv()
            self.put(step).wait_send()
            return carry

        lax.fori_loop(1, self.count, take_one, 0)


def exchange_sems(groups):
    return [DMA((groups,)), DMA((groups,)), DMA(())]
LANES = 128
QUERY_BLOCK = 512
KEY_BLOCK = 256
BACK_KEYS = 512


def mm(left, right):
    return jnp.dot(left, right, preferred_element_type=jnp.float32)


def project_rows(norm_ref, weight_ref, rows_ref, cols_ref, level):
    size = 2 * norm_ref.shape[1]
    rows = pl.ds(pl.multiple_of(level * size, size), size)
    taken = norm_ref[pl.ds(level * 2, 2)].reshape(size, norm_ref.shape[2])
    block = mm(taken, weight_ref[...])
    rows_ref[rows, :] = block.astype(rows_ref.dtype)
    cols_ref[:, rows] = block.T.astype(cols_ref.dtype)


def attend_block(
    rows_ref, cols_ref, context_ref, inverse_ref, raised_ref, context_rows, index, scale
):
    seq = rows_ref.shape[0]
    here = pl.ds(pl.multiple_of(index * QUERY_BLOCK, QUERY_BLOCK), QUERY_BLOCK)
    queries = cols_ref[0:LANES, here]
    total = jnp.zeros((1, QUERY_BLOCK), jnp.float32)
    for at in range(0, seq, KEY_BLOCK):
        scores = mm(rows_ref[at : at + KEY_BLOCK, LANES : 2 * LANES], queries)
        raised = jnp.exp(scores * scale)
        raised_ref[at : at + KEY_BLOCK, :] = raised
        total = total + jnp.sum(raised, axis=0, keepdims=True)
    inverse = 1.0 / total
    inverse_ref[:, here] = inverse
    context = jnp.zeros((LANES, QUERY_BLOCK), jnp.float32)
    for at in range(0, seq, KEY_BLOCK):
        shares = (raised_ref[at : at + KEY_BLOCK, :] * inverse).astype(jnp.bfloat16)
        context = context + mm(cols_ref[2 * LANES : 3 * LANES, at : at + KEY_BLOCK], shares)
    context_ref[:, here] = context.astype(context_ref.dtype)
    context_rows[here, :] = context.T.astype(context_rows.dtype)


def front_kernel(
    count,
    scale,
    own_ref,
    source_ref,
    tokens_ref,
    dispatch_ref,
    weight_ref,
    proj_ref,
    norm_ref,
    gslots_ref,
    rows_ref,
    cols_ref,
    context_ref,
    inverse_ref,
    mid_ref,
    arrived_ref,
    raised_ref,
    context_rows,
    part_ref,
    total_ref,
    outgoing_ref,
    *refs,
):
    _, level, _ = ring_places()
    reach = count // 2
    grads, refs = refs[:OUT_SCRATCH], refs[OUT_SCRATCH:]
    slots, refs = refs[:OUT_SCRATCH], refs[OUT_SCRATCH:]
    sems, refs = refs[: 3 * GATHER_SEMS], refs[3 * GATHER_SEMS :]
    grads_out = SlotsOut(source_ref, *grads[:4], grads[4:])
    slots_out = SlotsOut(outgoing_ref, *slots[:4], slots[4:])
    first = GatherRing(own_ref, norm_ref, *sems[:GATHER_SEMS], count)
    second = GatherRing(grads[3], gslots_ref, *sems[GATHER_SEMS : 2 * GATHER_SEMS], count)
    third = GatherRing(slots[3], arrived_ref, *sems[2 * GATHER_SEMS :], count)
    reduce = ReduceRing(part_ref, total_ref, *refs, count)
    await_peers(greet_plane() + greet_ring(count))

    def both_ways(act, distance):
        def one_way(way, carry):
            act(level_at(level, (2 * way - 1) * distance, count))
            return carry

        lax.fori_loop(0, 2, one_way, 0)

    def project(place):
        project_rows(norm_ref, weight_ref, rows_ref, cols_ref, place)

    def attend(index, carry):
        attend_block(
            rows_ref, cols_ref, context_ref, inverse_ref, raised_ref, context_rows, index, scale
        )
        return carry

    def fill_part(place):
        size = 2 * part_ref.shape[1]
        rows = pl.ds(pl.multiple_of(place * size, size), size)
        block = mm(context_rows[rows, :], proj_ref[...]).astype(part_ref.dtype)
        part_ref[pl.ds(place * 2, 2)] = block.reshape(2, part_ref.shape[1], part_ref.shape[2])

    grads_out.begin()
    first.begin()
    first.settle(0, 0)
    project(level)
    for step in range(reach):
        first.run(step)
        if step == 0:
            grads_out.middle()
        if step == 1:
            grads_out.finish()
        if step == reach - 1:
            second.begin()
        for way in range(2):
            first.settle(way, step + 1)
        if step < reach - 1:
            both_ways(project, step + 1)
        else:
            project(level_at(level, reach, count))
    blocks = norm_ref.shape[0] * norm_ref.shape[1] // QUERY_BLOCK
    lax.fori_loop(0, blocks // 2, attend, 0)
    second.run(0)
    second.run(1)
    lax.fori_loop(blocks // 2, blocks, attend, 0)
    second.run(2)
    fill_part(level_at(level, reach, count))
    reduce.begin_step(0)
    both_ways(fill_part, reach - 1)
    reduce.begin_step(1)
    second.run(3)
    reduce.run_step(0)
    both_ways(fill_part, reach - 2)
    reduce.begin_step(2)
    reduce.run_step(1)
    both_ways(fill_part, reach - 3)
    reduce.begin_step(3)
    fill_part(level)
    reduce.begin_step(reach)
    reduce.run_step(2)
    reduce.run_step(3)
    first.finish()
    second.finish()
    reduce.close()
    mid = (tokens_ref[...].astype(jnp.float32) + total_ref[...]).astype(mid_ref.dtype)
    mid_ref[...] = mid
    normal, _ = norm_parts(mid)
    outgoing_ref[...] = mm(dispatch_ref[...], normal.astype(jnp.bfloat16)).astype(
        outgoing_ref.dtype
    )
    slots_out.begin()
    slots_out.middle()
    slots_out.finish()
    third.begin()
    for step in range(reach):
        third.run(step)
    third.finish()
    reduce.finish()


def front(own, grad_slots, tokens, dispatch, weight, proj, scale, local_experts, ident):
    spots = lax.axis_size("tensor")
    count = spots // 2
    rows, width = own.shape
    seq = spots * rows
    return comm_call(
        partial(front_kernel, count, scale),
        [
            jax.ShapeDtypeStruct((spots,) + own.shape, own.dtype),
            slots_shape(grad_slots, local_experts),
            jax.ShapeDtypeStruct((seq, 3 * LANES), jnp.bfloat16),
            jax.ShapeDtypeStruct((3 * LANES, seq), jnp.bfloat16),
            jax.ShapeDtypeStruct((LANES, seq), jnp.bfloat16),
            jax.ShapeDtypeStruct((1, seq), jnp.float32),
            jax.ShapeDtypeStruct(tokens.shape, tokens.dtype),
            slots_shape(grad_slots, local_experts),
        ],
        [own, grad_slots, tokens, dispatch, weight, proj],
        [
            pltpu.VMEM((seq, QUERY_BLOCK), jnp.float32),
            pltpu.VMEM((seq, LANES), jnp.bfloat16),
            pltpu.VMEM((spots, rows, width), jnp.bfloat16),
            pltpu.VMEM((rows, width), jnp.float32),
            pltpu.VMEM(grad_slots.shape, grad_slots.dtype),
        ]
        + out_scratch(grad_slots)
        + out_scratch(grad_slots)
        + gather_sems(count) * 3
        + reduce_scratch(rows, width, jnp.bfloat16, count),
        ident,
    )


def backward_block(
    rows_ref, cols_ref, context_ref, inverse_ref, grad_ref, proj_ref, gcols_ref, gkeys, gvals, level, scale
):
    seq = rows_ref.shape[0]
    size = gcols_ref.shape[0] // 3
    block = 2 * grad_ref.shape[1]
    here = pl.ds(pl.multiple_of(level * block, block), block)
    queries = cols_ref[0:LANES, here]
    query_rows = rows_ref[here, 0:LANES]
    wide = lax.dot_general(
        grad_ref[pl.ds(level * 2, 2)].reshape(block, grad_ref.shape[2]),
        proj_ref[...],
        (((1,), (1,)), ((), ())),
        preferred_element_type=jnp.float32,
    )
    grad_rows = wide.astype(jnp.bfloat16)
    grad_cols = wide.T.astype(jnp.bfloat16)
    inverse = inverse_ref[:, here]
    delta = jnp.sum(
        grad_cols.astype(jnp.float32) * context_ref[:, here].astype(jnp.float32),
        axis=0,
        keepdims=True,
    )
    grad_query = jnp.zeros((LANES, block), jnp.float32)
    for at in range(0, seq, BACK_KEYS):
        keys = slice(at, at + BACK_KEYS)
        scores = mm(rows_ref[keys, LANES : 2 * LANES], queries)
        shares = jnp.exp(scores * scale) * inverse
        grad_shares = mm(rows_ref[keys, 2 * LANES : 3 * LANES], grad_cols)
        grad_scores = (shares * (grad_shares - delta)).astype(jnp.bfloat16)
        gvals[keys, :] += mm(shares.astype(jnp.bfloat16), grad_rows)
        gkeys[keys, :] += mm(grad_scores, query_rows)
        grad_query = grad_query + mm(cols_ref[LANES : 2 * LANES, keys], grad_scores)
    gcols_ref[0:size, here] = (grad_query[0:size] * scale).astype(gcols_ref.dtype)


def flip_sums(gcols_ref, gkeys, gvals, scale):
    size = gcols_ref.shape[0] // 3
    for at in range(0, gkeys.shape[0], QUERY_BLOCK):
        there = slice(at, at + QUERY_BLOCK)
        key_cols = (gkeys[there, :] * scale).T
        value_cols = gvals[there, :].T
        gcols_ref[size : 2 * size, there] = key_cols[0:size].astype(gcols_ref.dtype)
        gcols_ref[2 * size : 3 * size, there] = value_cols[0:size].astype(gcols_ref.dtype)


def weight_sums(norm_ref, grad_ref, context_ref, gcols_ref, weights_ref, first, last):
    size = gcols_ref.shape[0] // 3
    step = 2 * LANES
    spare = jnp.zeros((3 * LANES - 4 * size, step), jnp.float32)

    def one(index, carry):
        where = pl.ds(pl.multiple_of(index * step, step), step)
        for_qkv = mm(gcols_ref[...], norm_ref[:, where])
        rows = grad_ref[:, :, where].reshape(norm_ref.shape[0], step)
        for_proj = mm(context_ref[0:size, :], rows)
        block = jnp.concatenate([for_qkv, for_proj, spare], axis=0).T
        weights_ref[where, :] = block[:, 0 : 4 * size].astype(weights_ref.dtype)
        return carry

    lax.fori_loop(first, last, one, 0)


def product(left, right):
    return lax.dot_general(
        left, right, (((0,), (0,)), ((), ())), preferred_element_type=jnp.float32
    )


def closing_kernel(
    count,
    scale,
    gpart_ref,
    cotangent_ref,
    mid_ref,
    collect_ref,
    proj_ref,
    context_ref,
    inverse_ref,
    hidden_far,
    down_far,
    garrived_far,
    gpre_far,
    arrived_far,
    rows_far,
    cols_far,
    norm_far,
    slots_ref,
    sum_ref,
    gdown_far,
    gup_far,
    hidden_ref,
    down_ref,
    garrived_ref,
    gpre_ref,
    arrived_ref,
    rows_ref,
    cols_ref,
    norm_ref,
    gdown_ref,
    gup_ref,
    load_sems,
    save_sems,
    part_ref,
    back_ref,
    own_ref,
    grad_ref,
    gcols_ref,
    gkeys,
    gvals,
    weights_ref,
    landing,
    *refs,
):
    fars = (hidden_far, down_far, garrived_far, gpre_far, arrived_far, rows_far, cols_far, norm_far)
    nears = (hidden_ref, down_ref, garrived_ref, gpre_ref, arrived_ref, rows_ref, cols_ref, norm_ref)
    loads = [
        pltpu.make_async_copy(far, near, load_sems.at[index])
        for index, (far, near) in enumerate(zip(fars, nears))
    ]
    ring_sems, refs = refs[:GATHER_SEMS], refs[GATHER_SEMS:]
    swap_refs, refs = refs[:3], refs[3:]
    each = OUT_SCRATCH + REDUCE_SCRATCH
    gslots, greduce = refs[:OUT_SCRATCH], refs[OUT_SCRATCH:each]
    slots, reduce = refs[each : each + OUT_SCRATCH], refs[each + OUT_SCRATCH :]
    _, level, _ = ring_places()
    grad_ring = ReduceRing(gpart_ref, gslots[0], *greduce, count)
    grad_back = SlotsBack(*gslots[:4], back_ref, gslots[4:])
    ring = GatherRing(own_ref, grad_ref, *ring_sems, count)
    back_ring = ReduceRing(part_ref, slots[0], *reduce, count)
    back = SlotsBack(*slots[:4], slots_ref, slots[4:])
    swap = Exchange(weights_ref, landing, *swap_refs)
    total = greet_groups() + greet_ring(count)
    for load in loads:
        load.start()
    gkeys[...] = jnp.zeros_like(gkeys)
    gvals[...] = jnp.zeros_like(gvals)
    await_peers(total)
    experts = hidden_ref.shape[0]

    def to_part(expert, carry):
        block = mm(hidden_ref[expert], down_ref[expert]).astype(part_ref.dtype)
        part_ref[expert] = block.reshape(part_ref.shape[1:])
        return carry

    def to_down(expert, carry):
        gdown_ref[expert] = product(hidden_ref[expert], garrived_ref[expert]).astype(
            gdown_ref.dtype
        )
        return carry

    def to_up(expert, carry):
        gup_ref[expert] = product(arrived_ref[expert], gpre_ref[expert]).astype(gup_ref.dtype)
        return carry

    grad_ring.begin()
    grad_ring.run_step(0)
    loads[0].wait()
    loads[1].wait()
    lax.fori_loop(0, experts, to_part, 0)
    grad_ring.run_step(1)
    back_ring.begin()
    loads[2].wait()
    lax.fori_loop(0, experts, to_down, 0)
    save_down = pltpu.make_async_copy(gdown_ref, gdown_far, save_sems.at[0])
    save_down.start()
    grad_ring.run_step(2)
    loads[3].wait()
    loads[4].wait()
    lax.fori_loop(0, experts, to_up, 0)
    save_up = pltpu.make_async_copy(gup_ref, gup_far, save_sems.at[1])
    save_up.start()
    grad_ring.run_step(3)
    normal, factor = norm_parts(mid_ref[...])
    grad_ring.close()
    grad_back.begin()
    back_ring.run_step(0)
    grad_back.middle()
    back_ring.run_step(1)
    grad_back.finish()
    grad_norm = mm(collect_ref[...], back_ref[...])
    grad_mid = cotangent_ref[...].astype(jnp.float32) + norm_back(normal, factor, grad_norm)
    own_ref[...] = grad_mid.astype(own_ref.dtype)

    def block(place):
        backward_block(
            rows_ref, cols_ref, context_ref, inverse_ref, grad_ref, proj_ref, gcols_ref, gkeys, gvals, place, scale
        )

    reach = count // 2
    ring.begin()
    for load in loads[5:]:
        load.wait()
    ring.settle(0, 0)
    block(level)
    for step in range(reach):
        ring.run(step)
        for way in range(2):
            ring.settle(way, step + 1)
        if step < reach - 1:

            def one_way(way, carry, step=step):
                block(level_at(level, (2 * way - 1) * (step + 1), count))
                return carry

            lax.fori_loop(0, 2, one_way, 0)
        else:
            back_ring.run_step(2)
            block(level_at(level, reach, count))
    flip_sums(gcols_ref, gkeys, gvals, scale)
    back_ring.run_step(3)
    parts = norm_ref.shape[1] // (2 * LANES)
    weight_sums(norm_ref, grad_ref, context_ref, gcols_ref, weights_ref, 0, parts)
    back_ring.close()
    back.begin()
    swap.start()
    back.middle()
    back.finish()
    swap.finish()
    sums = landing[0].astype(jnp.float32)
    for group in range(1, landing.shape[0]):
        sums = sums + landing[group].astype(jnp.float32)
    sum_ref[...] = sums
    save_down.wait()
    save_up.wait()
    ring.finish()
    grad_ring.finish()
    back_ring.finish()


def closing(near, far, scale, size, ident):
    spots = lax.axis_size("tensor")
    count = spots // 2
    groups = lax.axis_size("dp")
    gpart, cotangent = near[:2]
    hidden, down, _, _, arrived = far[:5]
    seq, width = far[-1].shape
    experts, _, slot_rows, _ = gpart.shape
    slots = jax.ShapeDtypeStruct((experts * slot_rows, width), gpart.dtype)
    up_shape = (experts, width, down.shape[1])
    return comm_call(
        partial(closing_kernel, count, scale),
        [
            slots,
            jax.ShapeDtypeStruct((width // groups, 4 * size), jnp.float32),
            jax.ShapeDtypeStruct(down.shape, jnp.bfloat16),
            jax.ShapeDtypeStruct(up_shape, jnp.bfloat16),
        ],
        near + far,
        [pltpu.VMEM(item.shape, item.dtype) for item in far]
        + [
            pltpu.VMEM(down.shape, jnp.bfloat16),
            pltpu.VMEM(up_shape, jnp.bfloat16),
            DMA((len(far),)),
            DMA((2,)),
            pltpu.VMEM(gpart.shape, gpart.dtype),
            pltpu.VMEM(slots.shape, slots.dtype),
            pltpu.VMEM(cotangent.shape, jnp.bfloat16),
            pltpu.VMEM((spots,) + cotangent.shape, jnp.bfloat16),
            pltpu.VMEM((3 * size, seq), jnp.bfloat16),
            pltpu.VMEM((seq, LANES), jnp.float32),
            pltpu.VMEM((seq, LANES), jnp.float32),
            pltpu.VMEM((width, 4 * size), jnp.bfloat16),
            pltpu.VMEM((groups, width // groups, 4 * size), jnp.bfloat16),
        ]
        + gather_sems(count)
        + exchange_sems(groups)
        + (out_scratch(slots) + reduce_scratch(experts * slot_rows, width, gpart.dtype, count)) * 2,
        ident,
        len(far),
        2,
    )


epsilon = 1e-06
half_root = 1.0 / math.sqrt(2.0)
bell_scale = 1.0 / math.sqrt(2.0 * math.pi)


def norm_parts(row_block):
    widened = row_block.astype(jnp.float32)
    center = widened - jnp.mean(widened, axis=-1, keepdims=True)
    factor = lax.rsqrt(jnp.mean(center * center, axis=-1, keepdims=True) + epsilon)
    return (center * factor, factor)


def norm_back(normal_rows, factor, upstream):
    mean_up = jnp.mean(upstream, axis=-1, keepdims=True)
    mean_mix = jnp.mean(upstream * normal_rows, axis=-1, keepdims=True)
    return factor * (upstream - mean_up - normal_rows * mean_mix)


def gelu_value(pre_act):
    return 0.5 * pre_act * (1.0 + lax.erf(pre_act * half_root))


def gelu_slope(pre_act):
    return (
        0.5 * (1.0 + lax.erf(pre_act * half_root))
        + pre_act * jnp.exp(-0.5 * pre_act * pre_act) * bell_scale
    )


def shards(
    tokens,
    cotangent,
    gate_weights,
    routes,
    slot_index,
    qkv_weight,
    proj_weight,
    up_weight,
    down_weight,
):
    rows_dev, model_width = tokens.shape
    head_size = qkv_weight.shape[2] // 3
    score_scale = head_size ** (-0.5)
    group_count = lax.axis_size("dp")
    spots = lax.axis_size("tensor")
    local_experts = up_weight.shape[0]
    places = group_count * local_experts * CAP
    normal_in, _ = norm_parts(tokens)
    normed = normal_in.astype(jnp.bfloat16)
    slot_code = jnp.where(slot_index >= 0, routes * CAP + slot_index, -1)
    positions = jnp.arange(places, dtype=jnp.int32)
    pick_both = (slot_code[None, :, :] == positions[:, None, None]).astype(jnp.bfloat16)
    pick_first = pick_both[:, :, 0]
    pick_second = pick_both[:, :, 1]
    dispatch_rows = pick_first + pick_second
    upstream = cotangent.astype(jnp.float32)
    grad_first = (gate_weights[:, 0:1] * upstream).astype(jnp.bfloat16)
    grad_second = (gate_weights[:, 1:2] * upstream).astype(jnp.bfloat16)
    grad_outgoing = jnp.dot(pick_first, grad_first, preferred_element_type=jnp.float32) + jnp.dot(
        pick_second, grad_second, preferred_element_type=jnp.float32
    )
    pad = ((0, 0), (0, 0), (0, LANES - head_size))
    wide_qkv = jnp.pad(qkv_weight.reshape(model_width, 3, head_size), pad)
    wide_qkv = wide_qkv.reshape(model_width, 3 * LANES)
    wide_proj = jnp.pad(proj_weight[0], ((0, LANES - head_size), (0, 0)))
    full_norm, grad_arrived, qkv_rows, qkv_cols, context, inverse, mid, arrived = front(
        normed,
        grad_outgoing.astype(jnp.bfloat16),
        tokens,
        dispatch_rows,
        wide_qkv,
        wide_proj,
        score_scale,
        local_experts,
        1,
    )
    full_norm = full_norm.reshape(-1, model_width)
    grad_arrived = grad_arrived.reshape(local_experts, -1, model_width)
    arrived = arrived.reshape(local_experts, -1, model_width)
    pre_act = jnp.einsum("end,edf->enf", arrived, up_weight, preferred_element_type=jnp.float32)
    hidden = gelu_value(pre_act).astype(jnp.bfloat16)
    grad_hidden = jnp.einsum(
        "end,efd->enf", grad_arrived, down_weight, preferred_element_type=jnp.float32
    )
    grad_pre = (grad_hidden * gelu_slope(pre_act)).astype(jnp.bfloat16)
    grad_partial = jnp.einsum(
        "enf,edf->end", grad_pre, up_weight, preferred_element_type=jnp.float32
    )
    returned, grad_weights, grad_down, grad_up = closing(
        [
            grad_partial.astype(jnp.bfloat16).reshape(local_experts, spots, -1, model_width),
            cotangent,
            mid,
            dispatch_rows.T,
            wide_proj,
            context,
            inverse,
        ],
        [hidden, down_weight, grad_arrived, grad_pre, arrived, qkv_rows, qkv_cols, full_norm],
        score_scale,
        head_size,
        6,
    )
    expert_first = jnp.einsum("pr,pd->rd", pick_first, returned, preferred_element_type=jnp.float32)
    expert_second = jnp.einsum(
        "pr,pd->rd", pick_second, returned, preferred_element_type=jnp.float32
    )
    mixed_rows = gate_weights[:, 0:1] * expert_first + gate_weights[:, 1:2] * expert_second
    layer_out = (mid.astype(jnp.float32) + mixed_rows).astype(jnp.bfloat16)
    gate_grad = jnp.stack(
        [jnp.sum(upstream * expert_first, axis=-1), jnp.sum(upstream * expert_second, axis=-1)],
        axis=1,
    )
    grad_qkv = grad_weights[:, None, : 3 * head_size]
    grad_proj = grad_weights[:, 3 * head_size :].T[None]
    return (layer_out, gate_grad, grad_qkv, grad_proj, grad_up, grad_down)


def solution(mesh):
    return jax.shard_map(
        shards,
        mesh=mesh,
        in_specs=(
            P(("dp", "tensor"), None),
            P(("dp", "tensor"), None),
            P(("dp", "tensor"), None),
            P(("dp", "tensor"), None),
            P(("dp", "tensor"), None),
            P(None, "tensor", None),
            P("tensor", None, None),
            P("dp", None, "tensor"),
            P("dp", "tensor", None),
        ),
        out_specs=(
            P(("dp", "tensor"), None),
            P(("dp", "tensor"), None),
            P("dp", "tensor", None),
            P("tensor", None, "dp"),
            P("dp", None, "tensor"),
            P("dp", "tensor", None),
        ),
        check_vma=False,
    )
```

```python
from functools import partial
import math

import jax
import jax.numpy as jnp
from jax import lax
from jax.experimental import pallas as pl
from jax.experimental.pallas import tpu as pltpu
from jax.sharding import PartitionSpec as P

CAP = 2


MESH = pl.DeviceIdType.MESH
VM = pl.BlockSpec(memory_space=pltpu.VMEM)
DMA = pltpu.SemaphoreType.DMA
PIECES = 4
SIDE = 4


def ring_places():
    spot = lax.axis_index("tensor")
    return spot, lax.div(spot, 2), lax.rem(spot, 2)


def level_at(level, steps, count):
    return lax.rem(level + steps + count, count)


def ring_peers(count):
    spot, level, side = ring_places()
    return (
        level_at(level, 1, count) * 2 + side,
        level_at(level, -1, count) * 2 + side,
        level * 2 + 1 - side,
    )


def plane_peer(along_x, step):
    me = lax.axis_index("dp")
    x, y = lax.div(me, SIDE), lax.rem(me, SIDE)
    if along_x:
        return lax.rem(x + step + SIDE, SIDE) * SIDE + y
    return x * SIDE + lax.rem(y + step + SIDE, SIDE)


def signal(axis, peer):
    pl.semaphore_signal(
        pltpu.get_barrier_semaphore(), inc=1, device_id={axis: peer}, device_id_type=MESH
    )


def greet_ring(count):
    peers = ring_peers(count)
    for peer in peers:
        signal("tensor", peer)
    return len(peers)


def greet_plane():
    for along_x in (True, False):
        for step in range(1, SIDE):
            signal("dp", plane_peer(along_x, step))
    return 2 * (SIDE - 1)


def greet_axis(axis):
    me = lax.axis_index(axis)
    count = lax.axis_size(axis)

    def call(step, carry):
        signal(axis, lax.rem(me + step, count))
        return carry

    lax.fori_loop(1, count, call, 0)
    return count - 1


def await_peers(total):
    pl.semaphore_wait(pltpu.get_barrier_semaphore(), total)


def remote(source, target, send, recv, axis, peer):
    return pltpu.make_async_remote_copy(
        src_ref=source,
        dst_ref=target,
        send_sem=send,
        recv_sem=recv,
        device_id={axis: peer},
        device_id_type=MESH,
    )


def travels(way, step, piece, last):
    return step != last or (piece < PIECES // 2) == (way == 0)


def block_at(ref, spot, piece):
    if len(ref.shape) == 3:
        size = ref.shape[1] // PIECES
        return ref.at[spot, pl.ds(piece * size, size)]
    per = PIECES // ref.shape[0]
    size = ref.shape[2] // per
    return ref.at[piece // per, spot, pl.ds(piece % per * size, size)]


def rows_at(ref, piece):
    size = ref.shape[0] // PIECES
    return ref.at[pl.ds(piece * size, size)]


class GatherRing:
    def __init__(self, own_ref, full_ref, send, recv, give, take, mine, count):
        self.spot, self.level, self.side = ring_places()
        self.peers = ring_peers(count)
        self.refs = (own_ref, full_ref, send, recv, give, take, mine)
        self.count, self.reach = count, count // 2
        self.left, self.moved, self.settled = [], [], []

    def place(self, way, step):
        return level_at(self.level, -step if way == 0 else step, self.count)

    def hop(self, way, step, piece):
        own_ref, full_ref, send, recv = self.refs[:4]
        target = block_at(full_ref, self.place(way, step) * 2 + self.side, piece)
        source = rows_at(own_ref, piece) if step == 0 else target
        item = (way, step, piece)
        return remote(source, target, send.at[item], recv.at[item], "tensor", self.peers[way])

    def landed(self, way, step, piece):
        full_ref, send, recv = self.refs[1:4]
        target = block_at(full_ref, self.place(way, step + 1) * 2 + self.side, piece)
        item = (way, step, piece)
        return remote(target, target, send.at[item], recv.at[item], "tensor", self.peers[way])

    def across(self, way, step, piece, from_side):
        own_ref, full_ref, _, _, give, take, _ = self.refs
        target = block_at(full_ref, self.place(way, step) * 2 + from_side, piece)
        source = rows_at(own_ref, piece) if step == 0 else target
        item = (way, step, piece)
        return remote(source, target, give.at[item], take.at[item], "tensor", self.peers[2])

    def keep(self, piece):
        own_ref, full_ref, mine = self.refs[0], self.refs[1], self.refs[6]
        return pltpu.make_async_copy(
            rows_at(own_ref, piece), block_at(full_ref, self.spot, piece), mine.at[piece]
        )

    def begin(self):
        for piece in range(PIECES):
            for way in range(2):
                self.hop(way, 0, piece).start()
                self.left.append((way, 0, piece))
        for piece in range(PIECES):
            self.keep(piece).start()
            self.across(0, 0, piece, self.side).start()
            self.moved.append((0, 0, piece))

    def run(self, step):
        last = self.reach - 1
        for piece in range(PIECES):
            for way in range(2):
                if not travels(way, step, piece, last):
                    continue
                self.landed(way, step, piece).wait_recv()
                if step < last and travels(way, step + 1, piece, last):
                    self.hop(way, step + 1, piece).start()
                    self.left.append((way, step + 1, piece))
                self.across(way, step + 1, piece, self.side).start()
                self.moved.append((way, step + 1, piece))

    def settle(self, way, step):
        for item in [item for item in self.moved if item[:2] == (way, step)]:
            if step == 0:
                self.keep(item[2]).wait()
            self.across(*item, 1 - self.side).wait_recv()
            self.settled.append(item)

    def finish(self):
        for way, step in [(0, 0)] + [(way, step) for step in range(1, self.reach + 1) for way in range(2)]:
            if not any(item[:2] == (way, step) for item in self.settled):
                self.settle(way, step)
        for item in self.left:
            self.hop(*item).wait_send()
        for item in self.moved:
            self.across(*item, self.side).wait_send()


def gather_sems(count):
    reach = count // 2
    return [
        DMA((2, reach, PIECES)),
        DMA((2, reach, PIECES)),
        DMA((2, reach + 1, PIECES)),
        DMA((2, reach + 1, PIECES)),
        DMA((PIECES,)),
    ]


GATHER_SEMS = 5


def comm_call(kernel, out_shape, operands, scratch, ident, far_in=0, far_out=0):
    far = pl.BlockSpec(memory_space=pl.ANY)
    return pl.pallas_call(
        kernel,
        out_shape=out_shape,
        in_specs=[VM] * (len(operands) - far_in) + [far] * far_in,
        out_specs=[VM] * (len(out_shape) - far_out) + [far] * far_out,
        scratch_shapes=scratch,
        compiler_params=pltpu.CompilerParams(
            collective_id=ident, has_side_effects=True, vmem_limit_bytes=60 * 1024 * 1024
        ),
    )(*operands)


class Swap:
    def __init__(self, along_x, source_ref, target_ref, send, recv, mine):
        me = lax.axis_index("dp")
        self.me = lax.div(me, SIDE) if along_x else lax.rem(me, SIDE)
        self.along_x = along_x
        self.refs = (source_ref, target_ref, send, recv)
        self.keep = pltpu.make_async_copy(
            self.block(source_ref, self.me), self.block(target_ref, self.me), mine
        )

    def block(self, ref, index):
        size = ref.shape[0] // SIDE
        return ref.at[pl.ds(pl.multiple_of(index * size, size), size)]

    def copy(self, step, outward):
        source_ref, target_ref, send, recv = self.refs
        there = lax.rem(self.me + (step if outward else SIDE - step), SIDE)
        return remote(
            self.block(source_ref, there),
            self.block(target_ref, self.me if outward else there),
            send.at[step],
            recv.at[step],
            "dp",
            plane_peer(self.along_x, step if outward else -step),
        )

    def start(self):
        for step in range(1, SIDE):
            self.copy(step, True).start()
        self.keep.start()

    def finish(self):
        self.keep.wait()
        for step in range(1, SIDE):
            self.copy(step, False).wait_recv()
        for step in range(1, SIDE):
            self.copy(step, True).wait_send()


def swap_sems():
    return [DMA((SIDE,)), DMA((SIDE,)), DMA(())]


def reorder(rows, kind):
    count = rows.shape[0]
    target = lax.broadcasted_iota(jnp.int32, (count, count), 0)
    source = lax.broadcasted_iota(jnp.int32, (count, count), 1)
    extents = {"x": SIDE, "y": SIDE, "e": count // (SIDE * SIDE * CAP), "c": CAP}

    def code(index, order):
        digits = {}
        for name in reversed(order):
            digits[name] = index % extents[name]
            index = index // extents[name]
        total = digits["x"]
        for name in "yec":
            total = total * extents[name] + digits[name]
        return total

    before, after = kind
    orders = {"x": "xyec", "y": "yexc", "e": "eyxc"}
    pick = (code(target, orders[after]) == code(source, orders[before])).astype(rows.dtype)
    return jnp.dot(pick, rows, preferred_element_type=jnp.float32).astype(rows.dtype)


class SlotsOut:
    def __init__(self, source_ref, first, second, third, done, sems):
        self.refs = (first, second, third, done)
        self.by_x = Swap(True, source_ref, first, *sems[:3])
        self.by_y = Swap(False, second, third, *sems[3:])

    def begin(self):
        self.by_x.start()

    def middle(self):
        first, second = self.refs[:2]
        self.by_x.finish()
        second[...] = reorder(first[...], "xy")
        self.by_y.start()

    def finish(self):
        third, done = self.refs[2:]
        self.by_y.finish()
        done[...] = reorder(third[...], "ye")


def out_scratch(slots):
    return [pltpu.VMEM(slots.shape, slots.dtype)] * 4 + swap_sems() + swap_sems()


OUT_SCRATCH = 10


def slots_shape(slots, local_experts):
    spots = lax.axis_size("tensor")
    rows, width = slots.shape
    return jax.ShapeDtypeStruct((local_experts, spots, rows // local_experts, width), slots.dtype)


class ReduceRing:
    def __init__(self, part_ref, total_ref, pair, stage, landing, send, recv, give, take, count):
        self.spot, self.level, self.side = ring_places()
        self.peers = ring_peers(count)
        self.part, self.total, self.pair = part_ref, total_ref, pair
        self.stage, self.landing = stage, landing
        self.sems = (send, recv, give, take)
        self.count, self.reach = count, count // 2
        self.plan = [
            (way, step, piece)
            for step in range(self.reach)
            for piece in range(PIECES)
            for way in range(2)
            if travels(way, step, piece, 0)
        ]
        self.own = [(0, self.reach, piece) for piece in range(PIECES)]

    def place(self, way, step):
        steps = self.reach - step
        return level_at(self.level, steps if way == 0 else -steps, self.count)

    def rows(self, way, step, piece):
        size = self.stage.shape[2] // PIECES
        return way, step, pl.ds(piece * size, size)

    def across(self, way, step, piece):
        there = self.place(way, step)
        item = (way, step, piece)
        return remote(
            block_at(self.part, there * 2 + 1 - self.side, piece),
            rows_at(self.pair.at[there], piece),
            self.sems[2].at[item],
            self.sems[3].at[item],
            "tensor",
            self.peers[2],
        )

    def hop(self, way, step, piece):
        item = (way, step, piece)
        where = self.rows(*item)
        return remote(
            self.stage.at[where],
            self.landing.at[where],
            self.sems[0].at[item],
            self.sems[1].at[item],
            "tensor",
            self.peers[way],
        )

    def local_sum(self, way, step, piece):
        there = self.place(way, step)
        self.across(way, step, piece).wait_recv()
        mine = block_at(self.part, there * 2 + self.side, piece)[...]
        return mine.astype(jnp.float32) + rows_at(self.pair.at[there], piece)[...].astype(
            jnp.float32
        )

    def arrived(self, way, step, piece):
        self.hop(way, step, piece).wait_recv()
        return self.landing[self.rows(way, step, piece)].astype(jnp.float32)

    def begin_step(self, at):
        for item in self.plan + self.own:
            if item[1] == at:
                self.across(*item).start()

    def begin(self):
        for step in range(self.reach + 1):
            self.begin_step(step)

    def run_step(self, at):
        for way, step, piece in self.plan:
            if step != at:
                continue
            term = self.local_sum(way, step, piece)
            if step > 0 and travels(way, step - 1, piece, 0):
                term = term + self.arrived(way, step - 1, piece)
            self.stage[self.rows(way, step, piece)] = term.astype(self.stage.dtype)
            self.hop(way, step, piece).start()

    def close(self):
        for way, step, piece in self.own:
            term = self.local_sum(way, step, piece)
            for side in range(2):
                term = term + self.arrived(side, self.reach - 1, piece)
            rows_at(self.total, piece)[...] = term.astype(self.total.dtype)

    def run(self):
        for step in range(self.reach):
            self.run_step(step)
        self.close()

    def finish(self):
        for item in self.plan:
            self.hop(*item).wait_send()
        for item in self.plan + self.own:
            self.across(*item).wait_send()


def reduce_scratch(rows, width, dtype, count):
    reach = count // 2
    return [
        pltpu.VMEM((count, rows, width), dtype),
        pltpu.VMEM((2, reach, rows, width), dtype),
        pltpu.VMEM((2, reach, rows, width), dtype),
        DMA((2, reach, PIECES)),
        DMA((2, reach, PIECES)),
        DMA((2, reach + 1, PIECES)),
        DMA((2, reach + 1, PIECES)),
    ]


REDUCE_SCRATCH = 7


class SlotsBack:
    def __init__(self, done, third, second, first, target_ref, sems):
        self.refs = (done, third, second, first)
        self.by_y = Swap(False, third, second, *sems[:3])
        self.by_x = Swap(True, first, target_ref, *sems[3:])

    def begin(self):
        done, third = self.refs[:2]
        third[...] = reorder(done[...], "ey")
        self.by_y.start()

    def middle(self):
        second, first = self.refs[2:]
        self.by_y.finish()
        first[...] = reorder(second[...], "yx")
        self.by_x.start()

    def finish(self):
        self.by_x.finish()


class Exchange:
    def __init__(self, source_ref, target_ref, send, recv, local_sem):
        self.me = lax.axis_index("dp")
        self.count = target_ref.shape[0]
        self.refs = (source_ref, target_ref, send, recv)
        self.keep = pltpu.make_async_copy(
            self.block(self.me), target_ref.at[self.me], local_sem
        )

    def block(self, index):
        source_ref, target_ref = self.refs[:2]
        size = target_ref.shape[1]
        return source_ref.at[pl.ds(pl.multiple_of(index * size, size), size)]

    def put(self, step):
        target_ref, send, recv = self.refs[1:]
        peer = lax.rem(self.me + step, self.count)
        return remote(
            self.block(peer), target_ref.at[self.me], send.at[step], recv.at[step], "dp", peer
        )

    def got(self, step):
        target_ref, send, recv = self.refs[1:]
        peer = lax.rem(self.me - step + self.count, self.count)
        return remote(
            self.block(peer), target_ref.at[peer], send.at[step], recv.at[step], "dp", peer
        )

    def start(self):
        def put_one(step, carry):
            self.put(step).start()
            return carry

        lax.fori_loop(1, self.count, put_one, 0)
        self.keep.start()

    def finish(self):
        self.keep.wait()

        def take_one(step, carry):
            self.got(step).wait_recv()
            self.put(step).wait_send()
            return carry

        lax.fori_loop(1, self.count, take_one, 0)


def exchange_sems(groups):
    return [DMA((groups,)), DMA((groups,)), DMA(())]
LANES = 128
QUERY_BLOCK = 512
KEY_BLOCK = 256
BACK_KEYS = 512


def mm(left, right):
    return jnp.dot(left, right, preferred_element_type=jnp.float32)


def project_rows(norm_ref, weight_ref, rows_ref, cols_ref, level):
    size = 2 * norm_ref.shape[1]
    rows = pl.ds(pl.multiple_of(level * size, size), size)
    taken = norm_ref[pl.ds(level * 2, 2)].reshape(size, norm_ref.shape[2])
    block = mm(taken, weight_ref[...])
    rows_ref[rows, :] = block.astype(rows_ref.dtype)
    cols_ref[:, rows] = block.T.astype(cols_ref.dtype)


def attend_block(rows_ref, cols_ref, context_ref, inverse_ref, raised_ref, index, scale):
    seq = rows_ref.shape[0]
    here = pl.ds(pl.multiple_of(index * QUERY_BLOCK, QUERY_BLOCK), QUERY_BLOCK)
    queries = cols_ref[0:LANES, here]
    total = jnp.zeros((1, QUERY_BLOCK), jnp.float32)
    for at in range(0, seq, KEY_BLOCK):
        scores = mm(rows_ref[at : at + KEY_BLOCK, LANES : 2 * LANES], queries)
        raised = jnp.exp(scores * scale)
        raised_ref[at : at + KEY_BLOCK, :] = raised
        total = total + jnp.sum(raised, axis=0, keepdims=True)
    inverse = 1.0 / total
    inverse_ref[:, here] = inverse
    context = jnp.zeros((LANES, QUERY_BLOCK), jnp.float32)
    for at in range(0, seq, KEY_BLOCK):
        shares = (raised_ref[at : at + KEY_BLOCK, :] * inverse).astype(jnp.bfloat16)
        context = context + mm(cols_ref[2 * LANES : 3 * LANES, at : at + KEY_BLOCK], shares)
    context_ref[:, here] = context.astype(context_ref.dtype)


def product(left, right):
    return lax.dot_general(
        left, right, (((0,), (0,)), ((), ())), preferred_element_type=jnp.float32
    )


class HeadWeights:
    def __init__(self, own_ref, half_ref, full_ref, count, sems):
        self.spot, self.level, self.side = ring_places()
        self.peers = ring_peers(count)
        self.me = lax.axis_index("dp")
        self.groups = lax.axis_size("dp")
        self.count = count
        self.away = level_at(self.level, count - lax.div(self.me, 2), count)
        self.at_home = self.spot == self.me
        self.own, self.half, self.full = own_ref, half_ref, full_ref
        self.chain_send, self.chain_recv, self.chain_keep = sems[:3]
        self.send, self.recv, self.keep_sem, self.give, self.take = sems[3:]

    def lanes(self, side):
        width = self.half.shape[1]
        return pl.ds(pl.multiple_of(side * width, LANES), width)

    def to_partner(self):
        source = self.own.at[:, self.lanes(1 - self.side)]
        return remote(
            source, self.half, self.chain_send.at[2], self.chain_recv, "tensor", self.peers[2]
        )

    def onward(self, way):
        return remote(
            self.half, self.half, self.chain_send.at[way], self.chain_recv, "tensor", self.peers[way]
        )

    def begin(self):
        @pl.when(self.at_home)
        def _():
            self.to_partner().start()
            keep = pltpu.make_async_copy(
                self.own.at[:, self.lanes(self.side)], self.half, self.chain_keep
            )
            keep.start()
            keep.wait()
            self.onward(0).start()
            self.onward(1).start()
            self.spread()

    def pass_on(self, distance):
        if distance == 0:

            @pl.when(jnp.logical_and(self.away == 0, jnp.logical_not(self.at_home)))
            def _():
                self.onward(0).wait_recv()
                self.onward(0).start()
                self.onward(1).start()
                self.spread()

            return
        reach = self.count // 2

        @pl.when(self.away == distance)
        def _():
            self.onward(0).wait_recv()
            if distance < reach:
                self.onward(0).start()
            self.spread()

        if distance < reach:

            @pl.when(self.away == self.count - distance)
            def _():
                self.onward(1).wait_recv()
                if distance < reach - 1:
                    self.onward(1).start()
                self.spread()

    def put(self, step):
        peer = lax.rem(self.me + step, self.groups)
        target = self.full.at[self.me, :, self.lanes(self.side)]
        return remote(self.half, target, self.send.at[step], self.recv.at[step], "dp", peer)

    def keep(self):
        target = self.full.at[self.me, :, self.lanes(self.side)]
        return pltpu.make_async_copy(self.half, target, self.keep_sem)

    def spread(self):
        def put_one(step, carry):
            self.put(step).start()
            return carry

        lax.fori_loop(1, self.groups, put_one, 0)
        self.keep().start()

    def across(self, step, side):
        head = lax.rem(self.me - step + self.groups, self.groups)
        block = self.full.at[head, :, self.lanes(side)]
        return remote(
            block, block, self.give.at[step], self.take.at[step], "tensor", self.peers[2]
        )

    def swap_halves(self):
        self.keep().wait()
        self.across(0, self.side).start()

        def one(step, carry):
            head = lax.rem(self.me - step + self.groups, self.groups)
            block = self.full.at[head, :, self.lanes(self.side)]
            remote(
                self.half, block, self.send.at[step], self.recv.at[step], "dp", head
            ).wait_recv()
            self.across(step, self.side).start()
            return carry

        lax.fori_loop(1, self.groups, one, 0)

    def settle(self):
        def one(step, carry):
            self.across(step, 1 - self.side).wait_recv()
            return carry

        lax.fori_loop(0, self.groups, one, 0)

    def finish(self):
        reach = self.count // 2

        @pl.when(self.at_home)
        def _():
            self.to_partner().wait_send()

        @pl.when(self.away < reach)
        def _():
            self.onward(0).wait_send()

        @pl.when(jnp.logical_or(self.away == 0, self.away > reach + 1))
        def _():
            self.onward(1).wait_send()

        def one(step, carry):
            self.put(step).wait_send()
            return carry

        lax.fori_loop(1, self.groups, one, 0)

        def two(step, carry):
            self.across(step, self.side).wait_send()
            return carry

        lax.fori_loop(0, self.groups, two, 0)


class ContextSwap:
    def __init__(self, context_ref, target_ref, send, recv, mine):
        self.spot = lax.axis_index("tensor")
        self.count = lax.axis_size("tensor")
        self.refs = (context_ref, target_ref, send, recv)
        self.keep = pltpu.make_async_copy(self.block(self.spot), target_ref.at[self.spot], mine)

    def block(self, spot):
        context_ref, target_ref = self.refs[:2]
        _, size, rows = target_ref.shape
        return context_ref.at[pl.ds(0, size), pl.ds(pl.multiple_of(spot * rows, rows), rows)]

    def copy(self, step, outward):
        _, target_ref, send, recv = self.refs
        peer = lax.rem(self.spot + (step if outward else self.count - step), self.count)
        target = target_ref.at[self.spot if outward else peer]
        return remote(self.block(peer), target, send.at[step], recv.at[step], "tensor", peer)

    def start(self):
        def one(step, carry):
            self.copy(step, True).start()
            return carry

        lax.fori_loop(1, self.count, one, 0)
        self.keep.start()

    def finish(self):
        self.keep.wait()

        def one(step, carry):
            self.copy(step, False).wait_recv()
            self.copy(step, True).wait_send()
            return carry

        lax.fori_loop(1, self.count, one, 0)


def front_kernel(
    count,
    scale,
    own_ref,
    source_ref,
    tokens_ref,
    dispatch_ref,
    weight_ref,
    proj_ref,
    norm_ref,
    gslots_ref,
    rows_ref,
    cols_ref,
    context_ref,
    inverse_ref,
    mid_ref,
    arrived_ref,
    raised_ref,
    half_ref,
    heads_ref,
    context_all,
    outgoing_ref,
    *refs,
):
    _, level, _ = ring_places()
    reach = count // 2
    grads, refs = refs[:OUT_SCRATCH], refs[OUT_SCRATCH:]
    slots, refs = refs[:OUT_SCRATCH], refs[OUT_SCRATCH:]
    sems, refs = refs[: 3 * GATHER_SEMS], refs[3 * GATHER_SEMS :]
    weights = HeadWeights(proj_ref, half_ref, heads_ref, count, refs[:8])
    contexts = ContextSwap(context_ref, context_all, *refs[8:])
    grads_out = SlotsOut(source_ref, *grads[:4], grads[4:])
    slots_out = SlotsOut(outgoing_ref, *slots[:4], slots[4:])
    first = GatherRing(own_ref, norm_ref, *sems[:GATHER_SEMS], count)
    second = GatherRing(grads[3], gslots_ref, *sems[GATHER_SEMS : 2 * GATHER_SEMS], count)
    third = GatherRing(slots[3], arrived_ref, *sems[2 * GATHER_SEMS :], count)
    await_peers(greet_axis("dp") + greet_axis("tensor"))

    def both_ways(act, distance):
        def one_way(way, carry):
            act(level_at(level, (2 * way - 1) * distance, count))
            return carry

        lax.fori_loop(0, 2, one_way, 0)

    def project(place):
        project_rows(norm_ref, weight_ref, rows_ref, cols_ref, place)

    def attend(index, carry):
        attend_block(
            rows_ref, cols_ref, context_ref, inverse_ref, raised_ref, index, scale
        )
        return carry

    grads_out.begin()
    first.begin()
    weights.begin()
    first.settle(0, 0)
    project(level)
    weights.pass_on(0)
    for step in range(reach):
        first.run(step)
        weights.pass_on(step + 1)
        if step == 0:
            grads_out.middle()
        if step == 1:
            grads_out.finish()
        if step == reach - 1:
            second.begin()
        for way in range(2):
            first.settle(way, step + 1)
        if step < reach - 1:
            both_ways(project, step + 1)
        else:
            project(level_at(level, reach, count))
    blocks = norm_ref.shape[0] * norm_ref.shape[1] // QUERY_BLOCK
    lax.fori_loop(0, blocks // 2, attend, 0)
    second.run(0)
    second.run(1)
    lax.fori_loop(blocks // 2, blocks, attend, 0)
    contexts.start()
    second.run(2)
    weights.swap_halves()
    second.run(3)
    first.finish()
    second.finish()
    contexts.finish()
    weights.settle()
    spots, size, rows = context_all.shape
    attention = product(
        context_all[...].reshape(spots * size, rows),
        heads_ref[...].reshape(spots * size, heads_ref.shape[2]),
    )
    mid = (tokens_ref[...].astype(jnp.float32) + attention).astype(mid_ref.dtype)
    mid_ref[...] = mid
    normal, _ = norm_parts(mid)
    outgoing_ref[...] = mm(dispatch_ref[...], normal.astype(jnp.bfloat16)).astype(
        outgoing_ref.dtype
    )
    slots_out.begin()
    slots_out.middle()
    slots_out.finish()
    third.begin()
    for step in range(reach):
        third.run(step)
    third.finish()
    weights.finish()


def front(own, grad_slots, tokens, dispatch, weight, proj, scale, local_experts, ident):
    spots = lax.axis_size("tensor")
    count = spots // 2
    rows, width = own.shape
    seq = spots * rows
    size = proj.shape[0]
    return comm_call(
        partial(front_kernel, count, scale),
        [
            jax.ShapeDtypeStruct((spots,) + own.shape, own.dtype),
            slots_shape(grad_slots, local_experts),
            jax.ShapeDtypeStruct((seq, 3 * LANES), jnp.bfloat16),
            jax.ShapeDtypeStruct((3 * LANES, seq), jnp.bfloat16),
            jax.ShapeDtypeStruct((LANES, seq), jnp.bfloat16),
            jax.ShapeDtypeStruct((1, seq), jnp.float32),
            jax.ShapeDtypeStruct(tokens.shape, tokens.dtype),
            slots_shape(grad_slots, local_experts),
        ],
        [own, grad_slots, tokens, dispatch, weight, proj],
        [
            pltpu.VMEM((seq, QUERY_BLOCK), jnp.float32),
            pltpu.VMEM((size, width // 2), jnp.bfloat16),
            pltpu.VMEM((spots, size, width), jnp.bfloat16),
            pltpu.VMEM((spots, size, rows), jnp.bfloat16),
            pltpu.VMEM(grad_slots.shape, grad_slots.dtype),
        ]
        + out_scratch(grad_slots)
        + out_scratch(grad_slots)
        + gather_sems(count) * 3
        + [DMA((3,)), DMA(()), DMA(())]
        + [DMA((spots,)), DMA((spots,)), DMA(()), DMA((spots,)), DMA((spots,))]
        + [DMA((spots,)), DMA((spots,)), DMA(())],
        ident,
    )


def backward_block(
    rows_ref, cols_ref, context_ref, inverse_ref, grad_ref, proj_ref, gcols_ref, gkeys, gvals, level, scale
):
    seq = rows_ref.shape[0]
    size = gcols_ref.shape[0] // 3
    block = 2 * grad_ref.shape[1]
    here = pl.ds(pl.multiple_of(level * block, block), block)
    queries = cols_ref[0:LANES, here]
    query_rows = rows_ref[here, 0:LANES]
    wide = lax.dot_general(
        grad_ref[pl.ds(level * 2, 2)].reshape(block, grad_ref.shape[2]),
        proj_ref[...],
        (((1,), (1,)), ((), ())),
        preferred_element_type=jnp.float32,
    )
    grad_rows = wide.astype(jnp.bfloat16)
    grad_cols = wide.T.astype(jnp.bfloat16)
    inverse = inverse_ref[:, here]
    delta = jnp.sum(
        grad_cols.astype(jnp.float32) * context_ref[:, here].astype(jnp.float32),
        axis=0,
        keepdims=True,
    )
    grad_query = jnp.zeros((LANES, block), jnp.float32)
    for at in range(0, seq, BACK_KEYS):
        keys = slice(at, at + BACK_KEYS)
        scores = mm(rows_ref[keys, LANES : 2 * LANES], queries)
        shares = jnp.exp(scores * scale) * inverse
        grad_shares = mm(rows_ref[keys, 2 * LANES : 3 * LANES], grad_cols)
        grad_scores = (shares * (grad_shares - delta)).astype(jnp.bfloat16)
        gvals[keys, :] += mm(shares.astype(jnp.bfloat16), grad_rows)
        gkeys[keys, :] += mm(grad_scores, query_rows)
        grad_query = grad_query + mm(cols_ref[LANES : 2 * LANES, keys], grad_scores)
    gcols_ref[0:size, here] = (grad_query[0:size] * scale).astype(gcols_ref.dtype)


def flip_sums(gcols_ref, gkeys, gvals, scale):
    size = gcols_ref.shape[0] // 3
    for at in range(0, gkeys.shape[0], QUERY_BLOCK):
        there = slice(at, at + QUERY_BLOCK)
        key_cols = (gkeys[there, :] * scale).T
        value_cols = gvals[there, :].T
        gcols_ref[size : 2 * size, there] = key_cols[0:size].astype(gcols_ref.dtype)
        gcols_ref[2 * size : 3 * size, there] = value_cols[0:size].astype(gcols_ref.dtype)


def weight_sums(norm_ref, grad_ref, context_ref, gcols_ref, weights_ref, first, last):
    size = gcols_ref.shape[0] // 3
    step = 2 * LANES
    spare = jnp.zeros((3 * LANES - 4 * size, step), jnp.float32)

    def one(index, carry):
        where = pl.ds(pl.multiple_of(index * step, step), step)
        for_qkv = mm(gcols_ref[...], norm_ref[:, where])
        rows = grad_ref[:, :, where].reshape(norm_ref.shape[0], step)
        for_proj = mm(context_ref[0:size, :], rows)
        block = jnp.concatenate([for_qkv, for_proj, spare], axis=0).T
        weights_ref[where, :] = block[:, 0 : 4 * size].astype(weights_ref.dtype)
        return carry

    lax.fori_loop(first, last, one, 0)


def closing_kernel(
    count,
    scale,
    gpart_ref,
    cotangent_ref,
    mid_ref,
    collect_ref,
    proj_ref,
    context_ref,
    inverse_ref,
    hidden_far,
    down_far,
    garrived_far,
    gpre_far,
    arrived_far,
    rows_far,
    cols_far,
    norm_far,
    slots_ref,
    sum_ref,
    gdown_far,
    gup_far,
    hidden_ref,
    down_ref,
    garrived_ref,
    gpre_ref,
    arrived_ref,
    rows_ref,
    cols_ref,
    norm_ref,
    gdown_ref,
    gup_ref,
    load_sems,
    save_sems,
    part_ref,
    back_ref,
    own_ref,
    grad_ref,
    gcols_ref,
    gkeys,
    gvals,
    weights_ref,
    landing,
    *refs,
):
    fars = (hidden_far, down_far, garrived_far, gpre_far, arrived_far, rows_far, cols_far, norm_far)
    nears = (hidden_ref, down_ref, garrived_ref, gpre_ref, arrived_ref, rows_ref, cols_ref, norm_ref)
    loads = [
        pltpu.make_async_copy(far, near, load_sems.at[index])
        for index, (far, near) in enumerate(zip(fars, nears))
    ]
    ring_sems, refs = refs[:GATHER_SEMS], refs[GATHER_SEMS:]
    swap_refs, refs = refs[:3], refs[3:]
    each = OUT_SCRATCH + REDUCE_SCRATCH
    gslots, greduce = refs[:OUT_SCRATCH], refs[OUT_SCRATCH:each]
    slots, reduce = refs[each : each + OUT_SCRATCH], refs[each + OUT_SCRATCH :]
    _, level, _ = ring_places()
    grad_ring = ReduceRing(gpart_ref, gslots[0], *greduce, count)
    grad_back = SlotsBack(*gslots[:4], back_ref, gslots[4:])
    ring = GatherRing(own_ref, grad_ref, *ring_sems, count)
    back_ring = ReduceRing(part_ref, slots[0], *reduce, count)
    back = SlotsBack(*slots[:4], slots_ref, slots[4:])
    swap = Exchange(weights_ref, landing, *swap_refs)
    total = greet_axis("dp") + greet_ring(count)
    for load in loads:
        load.start()
    gkeys[...] = jnp.zeros_like(gkeys)
    gvals[...] = jnp.zeros_like(gvals)
    await_peers(total)
    experts = hidden_ref.shape[0]

    def to_part(expert, carry):
        block = mm(hidden_ref[expert], down_ref[expert]).astype(part_ref.dtype)
        part_ref[expert] = block.reshape(part_ref.shape[1:])
        return carry

    def to_down(expert, carry):
        gdown_ref[expert] = product(hidden_ref[expert], garrived_ref[expert]).astype(
            gdown_ref.dtype
        )
        return carry

    def to_up(expert, carry):
        gup_ref[expert] = product(gpre_ref[expert], arrived_ref[expert]).astype(gup_ref.dtype)
        return carry

    grad_ring.begin()
    grad_ring.run_step(0)
    loads[0].wait()
    loads[1].wait()
    lax.fori_loop(0, experts, to_part, 0)
    grad_ring.run_step(1)
    back_ring.begin()
    loads[2].wait()
    lax.fori_loop(0, experts, to_down, 0)
    save_down = pltpu.make_async_copy(gdown_ref, gdown_far, save_sems.at[0])
    save_down.start()
    grad_ring.run_step(2)
    loads[3].wait()
    loads[4].wait()
    lax.fori_loop(0, experts, to_up, 0)
    save_up = pltpu.make_async_copy(gup_ref, gup_far, save_sems.at[1])
    save_up.start()
    grad_ring.run_step(3)
    normal, factor = norm_parts(mid_ref[...])
    grad_ring.close()
    grad_back.begin()
    back_ring.run_step(0)
    grad_back.middle()
    back_ring.run_step(1)
    grad_back.finish()
    grad_norm = mm(collect_ref[...], back_ref[...])
    grad_mid = cotangent_ref[...].astype(jnp.float32) + norm_back(normal, factor, grad_norm)
    own_ref[...] = grad_mid.astype(own_ref.dtype)

    def block(place):
        backward_block(
            rows_ref, cols_ref, context_ref, inverse_ref, grad_ref, proj_ref, gcols_ref, gkeys, gvals, place, scale
        )

    reach = count // 2
    ring.begin()
    for load in loads[5:]:
        load.wait()
    ring.settle(0, 0)
    block(level)
    for step in range(reach):
        ring.run(step)
        for way in range(2):
            ring.settle(way, step + 1)
        if step < reach - 1:

            def one_way(way, carry, step=step):
                block(level_at(level, (2 * way - 1) * (step + 1), count))
                return carry

            lax.fori_loop(0, 2, one_way, 0)
        else:
            back_ring.run_step(2)
            block(level_at(level, reach, count))
    flip_sums(gcols_ref, gkeys, gvals, scale)
    back_ring.run_step(3)
    parts = norm_ref.shape[1] // (2 * LANES)
    weight_sums(norm_ref, grad_ref, context_ref, gcols_ref, weights_ref, 0, parts)
    back_ring.close()
    back.begin()
    swap.start()
    back.middle()
    back.finish()
    swap.finish()
    sums = landing[0].astype(jnp.float32)
    for group in range(1, landing.shape[0]):
        sums = sums + landing[group].astype(jnp.float32)
    sum_ref[...] = sums
    save_down.wait()
    save_up.wait()
    ring.finish()
    grad_ring.finish()
    back_ring.finish()


def closing(near, far, scale, size, ident):
    spots = lax.axis_size("tensor")
    count = spots // 2
    groups = lax.axis_size("dp")
    gpart, cotangent = near[:2]
    hidden, down, _, _, arrived = far[:5]
    seq, width = far[-1].shape
    experts, _, slot_rows, _ = gpart.shape
    slots = jax.ShapeDtypeStruct((experts * slot_rows, width), gpart.dtype)
    return comm_call(
        partial(closing_kernel, count, scale),
        [
            slots,
            jax.ShapeDtypeStruct((width // groups, 4 * size), jnp.float32),
            jax.ShapeDtypeStruct(down.shape, jnp.bfloat16),
            jax.ShapeDtypeStruct(down.shape, jnp.bfloat16),
        ],
        near + far,
        [pltpu.VMEM(item.shape, item.dtype) for item in far]
        + [
            pltpu.VMEM(down.shape, jnp.bfloat16),
            pltpu.VMEM(down.shape, jnp.bfloat16),
            DMA((len(far),)),
            DMA((2,)),
            pltpu.VMEM(gpart.shape, gpart.dtype),
            pltpu.VMEM(slots.shape, slots.dtype),
            pltpu.VMEM(cotangent.shape, jnp.bfloat16),
            pltpu.VMEM((spots,) + cotangent.shape, jnp.bfloat16),
            pltpu.VMEM((3 * size, seq), jnp.bfloat16),
            pltpu.VMEM((seq, LANES), jnp.float32),
            pltpu.VMEM((seq, LANES), jnp.float32),
            pltpu.VMEM((width, 4 * size), jnp.bfloat16),
            pltpu.VMEM((groups, width // groups, 4 * size), jnp.bfloat16),
        ]
        + gather_sems(count)
        + exchange_sems(groups)
        + (out_scratch(slots) + reduce_scratch(experts * slot_rows, width, gpart.dtype, count)) * 2,
        ident,
        len(far),
        2,
    )


epsilon = 1e-06
half_root = 1.0 / math.sqrt(2.0)
bell_scale = 1.0 / math.sqrt(2.0 * math.pi)


def norm_parts(row_block):
    widened = row_block.astype(jnp.float32)
    center = widened - jnp.mean(widened, axis=-1, keepdims=True)
    factor = lax.rsqrt(jnp.mean(center * center, axis=-1, keepdims=True) + epsilon)
    return (center * factor, factor)


def norm_back(normal_rows, factor, upstream):
    mean_up = jnp.mean(upstream, axis=-1, keepdims=True)
    mean_mix = jnp.mean(upstream * normal_rows, axis=-1, keepdims=True)
    return factor * (upstream - mean_up - normal_rows * mean_mix)


def gelu_value(pre_act):
    return 0.5 * pre_act * (1.0 + lax.erf(pre_act * half_root))


def gelu_slope(pre_act):
    return (
        0.5 * (1.0 + lax.erf(pre_act * half_root))
        + pre_act * jnp.exp(-0.5 * pre_act * pre_act) * bell_scale
    )


def shards(
    tokens,
    cotangent,
    gate_weights,
    routes,
    slot_index,
    qkv_weight,
    proj_weight,
    up_weight,
    down_weight,
):
    rows_dev, model_width = tokens.shape
    head_size = qkv_weight.shape[2] // 3
    score_scale = head_size ** (-0.5)
    group_count = lax.axis_size("dp")
    spots = lax.axis_size("tensor")
    local_experts = up_weight.shape[0]
    places = group_count * local_experts * CAP
    normal_in, _ = norm_parts(tokens)
    normed = normal_in.astype(jnp.bfloat16)
    slot_code = jnp.where(slot_index >= 0, routes * CAP + slot_index, -1)
    positions = jnp.arange(places, dtype=jnp.int32)
    pick_both = (slot_code[None, :, :] == positions[:, None, None]).astype(jnp.bfloat16)
    pick_first = pick_both[:, :, 0]
    pick_second = pick_both[:, :, 1]
    dispatch_rows = pick_first + pick_second
    upstream = cotangent.astype(jnp.float32)
    grad_first = (gate_weights[:, 0:1] * upstream).astype(jnp.bfloat16)
    grad_second = (gate_weights[:, 1:2] * upstream).astype(jnp.bfloat16)
    grad_outgoing = jnp.dot(pick_first, grad_first, preferred_element_type=jnp.float32) + jnp.dot(
        pick_second, grad_second, preferred_element_type=jnp.float32
    )
    pad = ((0, 0), (0, 0), (0, LANES - head_size))
    wide_qkv = jnp.pad(qkv_weight.reshape(model_width, 3, head_size), pad)
    wide_qkv = wide_qkv.reshape(model_width, 3 * LANES)
    wide_proj = jnp.pad(proj_weight[0], ((0, LANES - head_size), (0, 0)))
    full_norm, grad_arrived, qkv_rows, qkv_cols, context, inverse, mid, arrived = front(
        normed,
        grad_outgoing.astype(jnp.bfloat16),
        tokens,
        dispatch_rows,
        wide_qkv,
        proj_weight[0],
        score_scale,
        local_experts,
        1,
    )
    full_norm = full_norm.reshape(-1, model_width)
    grad_arrived = grad_arrived.reshape(local_experts, -1, model_width)
    arrived = arrived.reshape(local_experts, -1, model_width)
    pre_act = jnp.einsum("end,edf->enf", arrived, up_weight, preferred_element_type=jnp.float32)
    hidden = gelu_value(pre_act).astype(jnp.bfloat16)
    grad_hidden = jnp.einsum(
        "end,efd->enf", grad_arrived, down_weight, preferred_element_type=jnp.float32
    )
    grad_pre = (grad_hidden * gelu_slope(pre_act)).astype(jnp.bfloat16)
    grad_partial = jnp.einsum(
        "enf,edf->end", grad_pre, up_weight, preferred_element_type=jnp.float32
    )
    returned, grad_weights, grad_down, grad_up = closing(
        [
            grad_partial.astype(jnp.bfloat16).reshape(local_experts, spots, -1, model_width),
            cotangent,
            mid,
            dispatch_rows.T,
            wide_proj,
            context,
            inverse,
        ],
        [hidden, down_weight, grad_arrived, grad_pre, arrived, qkv_rows, qkv_cols, full_norm],
        score_scale,
        head_size,
        6,
    )
    expert_first = jnp.einsum("pr,pd->rd", pick_first, returned, preferred_element_type=jnp.float32)
    expert_second = jnp.einsum(
        "pr,pd->rd", pick_second, returned, preferred_element_type=jnp.float32
    )
    mixed_rows = gate_weights[:, 0:1] * expert_first + gate_weights[:, 1:2] * expert_second
    layer_out = (mid.astype(jnp.float32) + mixed_rows).astype(jnp.bfloat16)
    gate_grad = jnp.stack(
        [jnp.sum(upstream * expert_first, axis=-1), jnp.sum(upstream * expert_second, axis=-1)],
        axis=1,
    )
    grad_qkv = grad_weights[:, None, : 3 * head_size]
    grad_proj = grad_weights[:, 3 * head_size :].T[None]
    return (layer_out, gate_grad, grad_qkv, grad_proj, grad_up.swapaxes(1, 2), grad_down)


def solution(mesh):
    return jax.shard_map(
        shards,
        mesh=mesh,
        in_specs=(
            P(("dp", "tensor"), None),
            P(("dp", "tensor"), None),
            P(("dp", "tensor"), None),
            P(("dp", "tensor"), None),
            P(("dp", "tensor"), None),
            P(None, "tensor", None),
            P("tensor", None, None),
            P("dp", None, "tensor"),
            P("dp", "tensor", None),
        ),
        out_specs=(
            P(("dp", "tensor"), None),
            P(("dp", "tensor"), None),
            P("dp", "tensor", None),
            P("tensor", None, "dp"),
            P("dp", None, "tensor"),
            P("dp", "tensor", None),
        ),
        check_vma=False,
    )
```

```python
from functools import partial
import math

import jax
import jax.numpy as jnp
from jax import lax
from jax.experimental import pallas as pl
from jax.experimental.pallas import tpu as pltpu
from jax.sharding import PartitionSpec as P

CAP = 2


MESH = pl.DeviceIdType.MESH
VM = pl.BlockSpec(memory_space=pltpu.VMEM)
DMA = pltpu.SemaphoreType.DMA
PIECES = 4
SIDE = 4


def ring_places():
    spot = lax.axis_index("tensor")
    return spot, lax.div(spot, 2), lax.rem(spot, 2)


def level_at(level, steps, count):
    return lax.rem(level + steps + count, count)


def ring_peers(count):
    spot, level, side = ring_places()
    return (
        level_at(level, 1, count) * 2 + side,
        level_at(level, -1, count) * 2 + side,
        level * 2 + 1 - side,
    )


def plane_peer(along_x, step):
    me = lax.axis_index("dp")
    x, y = lax.div(me, SIDE), lax.rem(me, SIDE)
    if along_x:
        return lax.rem(x + step + SIDE, SIDE) * SIDE + y
    return x * SIDE + lax.rem(y + step + SIDE, SIDE)


def signal(axis, peer):
    pl.semaphore_signal(
        pltpu.get_barrier_semaphore(), inc=1, device_id={axis: peer}, device_id_type=MESH
    )


def greet_ring(count):
    peers = ring_peers(count)
    for peer in peers:
        signal("tensor", peer)
    return len(peers)


def greet_plane():
    for along_x in (True, False):
        for step in range(1, SIDE):
            signal("dp", plane_peer(along_x, step))
    return 2 * (SIDE - 1)


def greet_axis(axis):
    me = lax.axis_index(axis)
    count = lax.axis_size(axis)

    def call(step, carry):
        signal(axis, lax.rem(me + step, count))
        return carry

    lax.fori_loop(1, count, call, 0)
    return count - 1


def await_peers(total):
    pl.semaphore_wait(pltpu.get_barrier_semaphore(), total)


def remote(source, target, send, recv, axis, peer):
    return pltpu.make_async_remote_copy(
        src_ref=source,
        dst_ref=target,
        send_sem=send,
        recv_sem=recv,
        device_id={axis: peer},
        device_id_type=MESH,
    )


def travels(way, step, piece, last):
    return step != last or (piece < PIECES // 2) == (way == 0)


def block_at(ref, spot, piece):
    if len(ref.shape) == 3:
        size = ref.shape[1] // PIECES
        return ref.at[spot, pl.ds(piece * size, size)]
    per = PIECES // ref.shape[0]
    size = ref.shape[2] // per
    return ref.at[piece // per, spot, pl.ds(piece % per * size, size)]


def rows_at(ref, piece):
    size = ref.shape[0] // PIECES
    return ref.at[pl.ds(piece * size, size)]


class GatherRing:
    def __init__(self, own_ref, full_ref, send, recv, give, take, mine, count):
        self.spot, self.level, self.side = ring_places()
        self.peers = ring_peers(count)
        self.refs = (own_ref, full_ref, send, recv, give, take, mine)
        self.count, self.reach = count, count // 2
        self.left, self.moved, self.settled = [], [], []

    def place(self, way, step):
        return level_at(self.level, -step if way == 0 else step, self.count)

    def hop(self, way, step, piece):
        own_ref, full_ref, send, recv = self.refs[:4]
        target = block_at(full_ref, self.place(way, step) * 2 + self.side, piece)
        source = rows_at(own_ref, piece) if step == 0 else target
        item = (way, step, piece)
        return remote(source, target, send.at[item], recv.at[item], "tensor", self.peers[way])

    def landed(self, way, step, piece):
        full_ref, send, recv = self.refs[1:4]
        target = block_at(full_ref, self.place(way, step + 1) * 2 + self.side, piece)
        item = (way, step, piece)
        return remote(target, target, send.at[item], recv.at[item], "tensor", self.peers[way])

    def across(self, way, step, piece, from_side):
        own_ref, full_ref, _, _, give, take, _ = self.refs
        target = block_at(full_ref, self.place(way, step) * 2 + from_side, piece)
        source = rows_at(own_ref, piece) if step == 0 else target
        item = (way, step, piece)
        return remote(source, target, give.at[item], take.at[item], "tensor", self.peers[2])

    def keep(self, piece):
        own_ref, full_ref, mine = self.refs[0], self.refs[1], self.refs[6]
        return pltpu.make_async_copy(
            rows_at(own_ref, piece), block_at(full_ref, self.spot, piece), mine.at[piece]
        )

    def begin(self):
        for piece in range(PIECES):
            for way in range(2):
                self.hop(way, 0, piece).start()
                self.left.append((way, 0, piece))
        for piece in range(PIECES):
            self.keep(piece).start()
            self.across(0, 0, piece, self.side).start()
            self.moved.append((0, 0, piece))

    def run(self, step):
        last = self.reach - 1
        for piece in range(PIECES):
            for way in range(2):
                if not travels(way, step, piece, last):
                    continue
                self.landed(way, step, piece).wait_recv()
                if step < last and travels(way, step + 1, piece, last):
                    self.hop(way, step + 1, piece).start()
                    self.left.append((way, step + 1, piece))
                self.across(way, step + 1, piece, self.side).start()
                self.moved.append((way, step + 1, piece))

    def settle(self, way, step):
        for item in [item for item in self.moved if item[:2] == (way, step)]:
            if step == 0:
                self.keep(item[2]).wait()
            self.across(*item, 1 - self.side).wait_recv()
            self.settled.append(item)

    def finish(self):
        for way, step in [(0, 0)] + [(way, step) for step in range(1, self.reach + 1) for way in range(2)]:
            if not any(item[:2] == (way, step) for item in self.settled):
                self.settle(way, step)
        for item in self.left:
            self.hop(*item).wait_send()
        for item in self.moved:
            self.across(*item, self.side).wait_send()


def gather_sems(count):
    reach = count // 2
    return [
        DMA((2, reach, PIECES)),
        DMA((2, reach, PIECES)),
        DMA((2, reach + 1, PIECES)),
        DMA((2, reach + 1, PIECES)),
        DMA((PIECES,)),
    ]


GATHER_SEMS = 5


def comm_call(kernel, out_shape, operands, scratch, ident, far_in=0, far_out=0):
    far = pl.BlockSpec(memory_space=pl.ANY)
    return pl.pallas_call(
        kernel,
        out_shape=out_shape,
        in_specs=[VM] * (len(operands) - far_in) + [far] * far_in,
        out_specs=[VM] * (len(out_shape) - far_out) + [far] * far_out,
        scratch_shapes=scratch,
        compiler_params=pltpu.CompilerParams(
            collective_id=ident, has_side_effects=True, vmem_limit_bytes=60 * 1024 * 1024
        ),
    )(*operands)


class Swap:
    def __init__(self, along_x, source_ref, target_ref, send, recv, mine):
        me = lax.axis_index("dp")
        self.me = lax.div(me, SIDE) if along_x else lax.rem(me, SIDE)
        self.along_x = along_x
        self.refs = (source_ref, target_ref, send, recv)
        self.keep = pltpu.make_async_copy(
            self.block(source_ref, self.me), self.block(target_ref, self.me), mine
        )

    def block(self, ref, index):
        size = ref.shape[0] // SIDE
        return ref.at[pl.ds(pl.multiple_of(index * size, size), size)]

    def copy(self, step, outward):
        source_ref, target_ref, send, recv = self.refs
        there = lax.rem(self.me + (step if outward else SIDE - step), SIDE)
        return remote(
            self.block(source_ref, there),
            self.block(target_ref, self.me if outward else there),
            send.at[step],
            recv.at[step],
            "dp",
            plane_peer(self.along_x, step if outward else -step),
        )

    def start(self):
        for step in range(1, SIDE):
            self.copy(step, True).start()
        self.keep.start()

    def finish(self):
        self.keep.wait()
        for step in range(1, SIDE):
            self.copy(step, False).wait_recv()
        for step in range(1, SIDE):
            self.copy(step, True).wait_send()


def swap_sems():
    return [DMA((SIDE,)), DMA((SIDE,)), DMA(())]


def reorder(rows, kind):
    count = rows.shape[0]
    target = lax.broadcasted_iota(jnp.int32, (count, count), 0)
    source = lax.broadcasted_iota(jnp.int32, (count, count), 1)
    extents = {"x": SIDE, "y": SIDE, "e": count // (SIDE * SIDE * CAP), "c": CAP}

    def code(index, order):
        digits = {}
        for name in reversed(order):
            digits[name] = index % extents[name]
            index = index // extents[name]
        total = digits["x"]
        for name in "yec":
            total = total * extents[name] + digits[name]
        return total

    before, after = kind
    orders = {"x": "xyec", "y": "yexc", "e": "eyxc"}
    pick = (code(target, orders[after]) == code(source, orders[before])).astype(rows.dtype)
    return jnp.dot(pick, rows, preferred_element_type=jnp.float32).astype(rows.dtype)


class SlotsOut:
    def __init__(self, source_ref, first, second, third, done, sems):
        self.refs = (first, second, third, done)
        self.by_x = Swap(True, source_ref, first, *sems[:3])
        self.by_y = Swap(False, second, third, *sems[3:])

    def begin(self):
        self.by_x.start()

    def middle(self):
        first, second = self.refs[:2]
        self.by_x.finish()
        second[...] = reorder(first[...], "xy")
        self.by_y.start()

    def finish(self):
        third, done = self.refs[2:]
        self.by_y.finish()
        done[...] = reorder(third[...], "ye")


def out_scratch(slots):
    return [pltpu.VMEM(slots.shape, slots.dtype)] * 4 + swap_sems() + swap_sems()


OUT_SCRATCH = 10


def slots_shape(slots, local_experts):
    spots = lax.axis_size("tensor")
    rows, width = slots.shape
    return jax.ShapeDtypeStruct((local_experts, spots, rows // local_experts, width), slots.dtype)


class ReduceRing:
    def __init__(self, part_ref, total_ref, pair, stage, landing, send, recv, give, take, count):
        self.spot, self.level, self.side = ring_places()
        self.peers = ring_peers(count)
        self.part, self.total, self.pair = part_ref, total_ref, pair
        self.stage, self.landing = stage, landing
        self.sems = (send, recv, give, take)
        self.count, self.reach = count, count // 2
        self.plan = [
            (way, step, piece)
            for step in range(self.reach)
            for piece in range(PIECES)
            for way in range(2)
            if travels(way, step, piece, 0)
        ]
        self.own = [(0, self.reach, piece) for piece in range(PIECES)]

    def place(self, way, step):
        steps = self.reach - step
        return level_at(self.level, steps if way == 0 else -steps, self.count)

    def rows(self, way, step, piece):
        size = self.stage.shape[2] // PIECES
        return way, step, pl.ds(piece * size, size)

    def across(self, way, step, piece):
        there = self.place(way, step)
        item = (way, step, piece)
        return remote(
            block_at(self.part, there * 2 + 1 - self.side, piece),
            rows_at(self.pair.at[there], piece),
            self.sems[2].at[item],
            self.sems[3].at[item],
            "tensor",
            self.peers[2],
        )

    def hop(self, way, step, piece):
        item = (way, step, piece)
        where = self.rows(*item)
        return remote(
            self.stage.at[where],
            self.landing.at[where],
            self.sems[0].at[item],
            self.sems[1].at[item],
            "tensor",
            self.peers[way],
        )

    def local_sum(self, way, step, piece):
        there = self.place(way, step)
        self.across(way, step, piece).wait_recv()
        mine = block_at(self.part, there * 2 + self.side, piece)[...]
        return mine.astype(jnp.float32) + rows_at(self.pair.at[there], piece)[...].astype(
            jnp.float32
        )

    def arrived(self, way, step, piece):
        self.hop(way, step, piece).wait_recv()
        return self.landing[self.rows(way, step, piece)].astype(jnp.float32)

    def begin_step(self, at):
        for item in self.plan + self.own:
            if item[1] == at:
                self.across(*item).start()

    def begin(self):
        for step in range(self.reach + 1):
            self.begin_step(step)

    def run_step(self, at):
        for way, step, piece in self.plan:
            if step != at:
                continue
            term = self.local_sum(way, step, piece)
            if step > 0 and travels(way, step - 1, piece, 0):
                term = term + self.arrived(way, step - 1, piece)
            self.stage[self.rows(way, step, piece)] = term.astype(self.stage.dtype)
            self.hop(way, step, piece).start()

    def close(self):
        for way, step, piece in self.own:
            term = self.local_sum(way, step, piece)
            for side in range(2):
                term = term + self.arrived(side, self.reach - 1, piece)
            rows_at(self.total, piece)[...] = term.astype(self.total.dtype)

    def run(self):
        for step in range(self.reach):
            self.run_step(step)
        self.close()

    def finish(self):
        for item in self.plan:
            self.hop(*item).wait_send()
        for item in self.plan + self.own:
            self.across(*item).wait_send()


def reduce_scratch(rows, width, dtype, count):
    reach = count // 2
    return [
        pltpu.VMEM((count, rows, width), dtype),
        pltpu.VMEM((2, reach, rows, width), dtype),
        pltpu.VMEM((2, reach, rows, width), dtype),
        DMA((2, reach, PIECES)),
        DMA((2, reach, PIECES)),
        DMA((2, reach + 1, PIECES)),
        DMA((2, reach + 1, PIECES)),
    ]


REDUCE_SCRATCH = 7


class SlotsBack:
    def __init__(self, done, third, second, first, target_ref, sems):
        self.refs = (done, third, second, first)
        self.by_y = Swap(False, third, second, *sems[:3])
        self.by_x = Swap(True, first, target_ref, *sems[3:])

    def begin(self):
        done, third = self.refs[:2]
        third[...] = reorder(done[...], "ey")
        self.by_y.start()

    def middle(self):
        second, first = self.refs[2:]
        self.by_y.finish()
        first[...] = reorder(second[...], "yx")
        self.by_x.start()

    def finish(self):
        self.by_x.finish()


class Exchange:
    def __init__(self, source_ref, target_ref, send, recv, local_sem):
        self.me = lax.axis_index("dp")
        self.count = target_ref.shape[0]
        self.refs = (source_ref, target_ref, send, recv)
        self.keep = pltpu.make_async_copy(
            self.block(self.me), target_ref.at[self.me], local_sem
        )

    def block(self, index):
        source_ref, target_ref = self.refs[:2]
        size = target_ref.shape[1]
        return source_ref.at[pl.ds(pl.multiple_of(index * size, size), size)]

    def put(self, step):
        target_ref, send, recv = self.refs[1:]
        peer = lax.rem(self.me + step, self.count)
        return remote(
            self.block(peer), target_ref.at[self.me], send.at[step], recv.at[step], "dp", peer
        )

    def got(self, step):
        target_ref, send, recv = self.refs[1:]
        peer = lax.rem(self.me - step + self.count, self.count)
        return remote(
            self.block(peer), target_ref.at[peer], send.at[step], recv.at[step], "dp", peer
        )

    def start(self):
        def put_one(step, carry):
            self.put(step).start()
            return carry

        lax.fori_loop(1, self.count, put_one, 0)
        self.keep.start()

    def finish(self):
        self.keep.wait()

        def take_one(step, carry):
            self.got(step).wait_recv()
            self.put(step).wait_send()
            return carry

        lax.fori_loop(1, self.count, take_one, 0)


def exchange_sems(groups):
    return [DMA((groups,)), DMA((groups,)), DMA(())]
LANES = 128
QUERY_BLOCK = 512
KEY_BLOCK = 256
BACK_KEYS = 512


def mm(left, right):
    return jnp.dot(left, right, preferred_element_type=jnp.float32)


def project_rows(norm_ref, weight_ref, rows_ref, cols_ref, level):
    size = 2 * norm_ref.shape[1]
    rows = pl.ds(pl.multiple_of(level * size, size), size)
    taken = norm_ref[pl.ds(level * 2, 2)].reshape(size, norm_ref.shape[2])
    block = mm(taken, weight_ref[...])
    rows_ref[rows, :] = block.astype(rows_ref.dtype)
    cols_ref[:, rows] = block.T.astype(cols_ref.dtype)


def attend_block(rows_ref, cols_ref, context_ref, inverse_ref, raised_ref, index, scale):
    seq = rows_ref.shape[0]
    here = pl.ds(pl.multiple_of(index * QUERY_BLOCK, QUERY_BLOCK), QUERY_BLOCK)
    queries = cols_ref[0:LANES, here]
    total = jnp.zeros((1, QUERY_BLOCK), jnp.float32)
    for at in range(0, seq, KEY_BLOCK):
        scores = mm(rows_ref[at : at + KEY_BLOCK, LANES : 2 * LANES], queries)
        raised = jnp.exp(scores * scale)
        raised_ref[at : at + KEY_BLOCK, :] = raised
        total = total + jnp.sum(raised, axis=0, keepdims=True)
    inverse = 1.0 / total
    inverse_ref[:, here] = inverse
    context = jnp.zeros((LANES, QUERY_BLOCK), jnp.float32)
    for at in range(0, seq, KEY_BLOCK):
        shares = (raised_ref[at : at + KEY_BLOCK, :] * inverse).astype(jnp.bfloat16)
        context = context + mm(cols_ref[2 * LANES : 3 * LANES, at : at + KEY_BLOCK], shares)
    context_ref[:, here] = context.astype(context_ref.dtype)


def product(left, right):
    return lax.dot_general(
        left, right, (((0,), (0,)), ((), ())), preferred_element_type=jnp.float32
    )


class HeadWeights:
    def __init__(self, own_ref, half_ref, full_ref, count, sems):
        self.spot, self.level, self.side = ring_places()
        self.peers = ring_peers(count)
        self.me = lax.axis_index("dp")
        self.groups = lax.axis_size("dp")
        self.count = count
        self.away = level_at(self.level, count - lax.div(self.me, 2), count)
        self.at_home = self.spot == self.me
        self.own, self.half, self.full = own_ref, half_ref, full_ref
        self.chain_send, self.chain_recv, self.chain_keep = sems[:3]
        self.send, self.recv, self.keep_sem, self.give, self.take = sems[3:]

    def lanes(self, side):
        width = self.half.shape[1]
        return pl.ds(pl.multiple_of(side * width, LANES), width)

    def to_partner(self):
        source = self.own.at[:, self.lanes(1 - self.side)]
        return remote(
            source, self.half, self.chain_send.at[2], self.chain_recv, "tensor", self.peers[2]
        )

    def onward(self, way):
        return remote(
            self.half, self.half, self.chain_send.at[way], self.chain_recv, "tensor", self.peers[way]
        )

    def begin(self):
        @pl.when(self.at_home)
        def _():
            self.to_partner().start()
            keep = pltpu.make_async_copy(
                self.own.at[:, self.lanes(self.side)], self.half, self.chain_keep
            )
            keep.start()
            keep.wait()
            self.onward(0).start()
            self.onward(1).start()
            self.spread()

    def pass_on(self, distance):
        if distance == 0:

            @pl.when(jnp.logical_and(self.away == 0, jnp.logical_not(self.at_home)))
            def _():
                self.onward(0).wait_recv()
                self.onward(0).start()
                self.onward(1).start()
                self.spread()

            return
        reach = self.count // 2

        @pl.when(self.away == distance)
        def _():
            self.onward(0).wait_recv()
            if distance < reach:
                self.onward(0).start()
            self.spread()

        if distance < reach:

            @pl.when(self.away == self.count - distance)
            def _():
                self.onward(1).wait_recv()
                if distance < reach - 1:
                    self.onward(1).start()
                self.spread()

    def put(self, step):
        peer = lax.rem(self.me + step, self.groups)
        target = self.full.at[self.me, :, self.lanes(self.side)]
        return remote(self.half, target, self.send.at[step], self.recv.at[step], "dp", peer)

    def keep(self):
        target = self.full.at[self.me, :, self.lanes(self.side)]
        return pltpu.make_async_copy(self.half, target, self.keep_sem)

    def spread(self):
        def put_one(step, carry):
            self.put(step).start()
            return carry

        lax.fori_loop(1, self.groups, put_one, 0)
        self.keep().start()

    def across(self, step, side):
        head = lax.rem(self.me - step + self.groups, self.groups)
        block = self.full.at[head, :, self.lanes(side)]
        return remote(
            block, block, self.give.at[step], self.take.at[step], "tensor", self.peers[2]
        )

    def swap_halves(self):
        self.keep().wait()
        self.across(0, self.side).start()

        def one(step, carry):
            head = lax.rem(self.me - step + self.groups, self.groups)
            block = self.full.at[head, :, self.lanes(self.side)]
            remote(
                self.half, block, self.send.at[step], self.recv.at[step], "dp", head
            ).wait_recv()
            self.across(step, self.side).start()
            return carry

        lax.fori_loop(1, self.groups, one, 0)

    def settle(self):
        def one(step, carry):
            self.across(step, 1 - self.side).wait_recv()
            return carry

        lax.fori_loop(0, self.groups, one, 0)

    def finish(self):
        reach = self.count // 2

        @pl.when(self.at_home)
        def _():
            self.to_partner().wait_send()

        @pl.when(self.away < reach)
        def _():
            self.onward(0).wait_send()

        @pl.when(jnp.logical_or(self.away == 0, self.away > reach + 1))
        def _():
            self.onward(1).wait_send()

        def one(step, carry):
            self.put(step).wait_send()
            return carry

        lax.fori_loop(1, self.groups, one, 0)

        def two(step, carry):
            self.across(step, self.side).wait_send()
            return carry

        lax.fori_loop(0, self.groups, two, 0)


class ContextSwap:
    def __init__(self, context_ref, target_ref, send, recv, mine):
        self.spot = lax.axis_index("tensor")
        self.count = lax.axis_size("tensor")
        self.refs = (context_ref, target_ref, send, recv)
        self.keep = pltpu.make_async_copy(self.block(self.spot), target_ref.at[self.spot], mine)

    def block(self, spot):
        context_ref, target_ref = self.refs[:2]
        _, size, rows = target_ref.shape
        return context_ref.at[pl.ds(0, size), pl.ds(pl.multiple_of(spot * rows, rows), rows)]

    def copy(self, step, outward):
        _, target_ref, send, recv = self.refs
        peer = lax.rem(self.spot + (step if outward else self.count - step), self.count)
        target = target_ref.at[self.spot if outward else peer]
        return remote(self.block(peer), target, send.at[step], recv.at[step], "tensor", peer)

    def start(self):
        def one(step, carry):
            self.copy(step, True).start()
            return carry

        lax.fori_loop(1, self.count, one, 0)
        self.keep.start()

    def finish(self):
        self.keep.wait()

        def one(step, carry):
            self.copy(step, False).wait_recv()
            self.copy(step, True).wait_send()
            return carry

        lax.fori_loop(1, self.count, one, 0)


def front_kernel(
    count,
    scale,
    own_ref,
    source_ref,
    tokens_ref,
    dispatch_ref,
    weight_ref,
    proj_ref,
    norm_ref,
    gslots_ref,
    rows_ref,
    cols_ref,
    context_ref,
    inverse_ref,
    mid_ref,
    arrived_ref,
    raised_ref,
    half_ref,
    heads_ref,
    context_all,
    outgoing_ref,
    *refs,
):
    _, level, _ = ring_places()
    reach = count // 2
    grads, refs = refs[:OUT_SCRATCH], refs[OUT_SCRATCH:]
    slots, refs = refs[:OUT_SCRATCH], refs[OUT_SCRATCH:]
    sems, refs = refs[: 3 * GATHER_SEMS], refs[3 * GATHER_SEMS :]
    weights = HeadWeights(proj_ref, half_ref, heads_ref, count, refs[:8])
    contexts = ContextSwap(context_ref, context_all, *refs[8:])
    grads_out = SlotsOut(source_ref, *grads[:4], grads[4:])
    slots_out = SlotsOut(outgoing_ref, *slots[:4], slots[4:])
    first = GatherRing(own_ref, norm_ref, *sems[:GATHER_SEMS], count)
    second = GatherRing(grads[3], gslots_ref, *sems[GATHER_SEMS : 2 * GATHER_SEMS], count)
    third = GatherRing(slots[3], arrived_ref, *sems[2 * GATHER_SEMS :], count)
    await_peers(greet_axis("dp") + greet_axis("tensor"))

    def both_ways(act, distance):
        def one_way(way, carry):
            act(level_at(level, (2 * way - 1) * distance, count))
            return carry

        lax.fori_loop(0, 2, one_way, 0)

    def project(place):
        project_rows(norm_ref, weight_ref, rows_ref, cols_ref, place)

    def attend(index, carry):
        attend_block(
            rows_ref, cols_ref, context_ref, inverse_ref, raised_ref, index, scale
        )
        return carry

    grads_out.begin()
    first.begin()
    weights.begin()
    first.settle(0, 0)
    project(level)
    weights.pass_on(0)
    for step in range(reach):
        first.run(step)
        weights.pass_on(step + 1)
        if step == 0:
            grads_out.middle()
        if step == 1:
            grads_out.finish()
        if step == reach - 1:
            second.begin()
        for way in range(2):
            first.settle(way, step + 1)
        if step < reach - 1:
            both_ways(project, step + 1)
        else:
            project(level_at(level, reach, count))
    blocks = norm_ref.shape[0] * norm_ref.shape[1] // QUERY_BLOCK
    lax.fori_loop(0, blocks // 2, attend, 0)
    second.run(0)
    lax.fori_loop(blocks // 2, blocks, attend, 0)
    contexts.start()
    weights.swap_halves()
    first.finish()
    contexts.finish()
    weights.settle()
    spots, size, rows = context_all.shape
    attention = product(
        context_all[...].reshape(spots * size, rows),
        heads_ref[...].reshape(spots * size, heads_ref.shape[2]),
    )
    mid = (tokens_ref[...].astype(jnp.float32) + attention).astype(mid_ref.dtype)
    mid_ref[...] = mid
    normal, _ = norm_parts(mid)
    outgoing_ref[...] = mm(dispatch_ref[...], normal.astype(jnp.bfloat16)).astype(
        outgoing_ref.dtype
    )
    slots_out.begin()
    second.run(1)
    slots_out.middle()
    second.run(2)
    slots_out.finish()
    third.begin()
    second.run(3)
    for step in range(reach):
        third.run(step)
    second.finish()
    third.finish()
    weights.finish()


def front(own, grad_slots, tokens, dispatch, weight, proj, scale, local_experts, ident):
    spots = lax.axis_size("tensor")
    count = spots // 2
    rows, width = own.shape
    seq = spots * rows
    size = proj.shape[0]
    return comm_call(
        partial(front_kernel, count, scale),
        [
            jax.ShapeDtypeStruct((spots,) + own.shape, own.dtype),
            slots_shape(grad_slots, local_experts),
            jax.ShapeDtypeStruct((seq, 3 * LANES), jnp.bfloat16),
            jax.ShapeDtypeStruct((3 * LANES, seq), jnp.bfloat16),
            jax.ShapeDtypeStruct((LANES, seq), jnp.bfloat16),
            jax.ShapeDtypeStruct((1, seq), jnp.float32),
            jax.ShapeDtypeStruct(tokens.shape, tokens.dtype),
            slots_shape(grad_slots, local_experts),
        ],
        [own, grad_slots, tokens, dispatch, weight, proj],
        [
            pltpu.VMEM((seq, QUERY_BLOCK), jnp.float32),
            pltpu.VMEM((size, width // 2), jnp.bfloat16),
            pltpu.VMEM((spots, size, width), jnp.bfloat16),
            pltpu.VMEM((spots, size, rows), jnp.bfloat16),
            pltpu.VMEM(grad_slots.shape, grad_slots.dtype),
        ]
        + out_scratch(grad_slots)
        + out_scratch(grad_slots)
        + gather_sems(count) * 3
        + [DMA((3,)), DMA(()), DMA(())]
        + [DMA((spots,)), DMA((spots,)), DMA(()), DMA((spots,)), DMA((spots,))]
        + [DMA((spots,)), DMA((spots,)), DMA(())],
        ident,
    )


def backward_block(
    rows_ref, cols_ref, context_ref, inverse_ref, grad_ref, proj_ref, gcols_ref, gkeys, gvals, level, scale
):
    seq = rows_ref.shape[0]
    size = gcols_ref.shape[0] // 3
    block = 2 * grad_ref.shape[1]
    here = pl.ds(pl.multiple_of(level * block, block), block)
    queries = cols_ref[0:LANES, here]
    query_rows = rows_ref[here, 0:LANES]
    wide = lax.dot_general(
        grad_ref[pl.ds(level * 2, 2)].reshape(block, grad_ref.shape[2]),
        proj_ref[...],
        (((1,), (1,)), ((), ())),
        preferred_element_type=jnp.float32,
    )
    grad_rows = wide.astype(jnp.bfloat16)
    grad_cols = wide.T.astype(jnp.bfloat16)
    inverse = inverse_ref[:, here]
    delta = jnp.sum(
        grad_cols.astype(jnp.float32) * context_ref[:, here].astype(jnp.float32),
        axis=0,
        keepdims=True,
    )
    grad_query = jnp.zeros((LANES, block), jnp.float32)
    for at in range(0, seq, BACK_KEYS):
        keys = slice(at, at + BACK_KEYS)
        scores = mm(rows_ref[keys, LANES : 2 * LANES], queries)
        shares = jnp.exp(scores * scale) * inverse
        grad_shares = mm(rows_ref[keys, 2 * LANES : 3 * LANES], grad_cols)
        grad_scores = (shares * (grad_shares - delta)).astype(jnp.bfloat16)
        gvals[keys, :] += mm(shares.astype(jnp.bfloat16), grad_rows)
        gkeys[keys, :] += mm(grad_scores, query_rows)
        grad_query = grad_query + mm(cols_ref[LANES : 2 * LANES, keys], grad_scores)
    gcols_ref[0:size, here] = (grad_query[0:size] * scale).astype(gcols_ref.dtype)


def flip_sums(gcols_ref, gkeys, gvals, scale):
    size = gcols_ref.shape[0] // 3
    for at in range(0, gkeys.shape[0], QUERY_BLOCK):
        there = slice(at, at + QUERY_BLOCK)
        key_cols = (gkeys[there, :] * scale).T
        value_cols = gvals[there, :].T
        gcols_ref[size : 2 * size, there] = key_cols[0:size].astype(gcols_ref.dtype)
        gcols_ref[2 * size : 3 * size, there] = value_cols[0:size].astype(gcols_ref.dtype)


def weight_sums(norm_ref, grad_ref, context_ref, gcols_ref, weights_ref, first, last):
    size = gcols_ref.shape[0] // 3
    step = 2 * LANES
    spare = jnp.zeros((3 * LANES - 4 * size, step), jnp.float32)

    def one(index, carry):
        where = pl.ds(pl.multiple_of(index * step, step), step)
        for_qkv = mm(gcols_ref[...], norm_ref[:, where])
        rows = grad_ref[:, :, where].reshape(norm_ref.shape[0], step)
        for_proj = mm(context_ref[0:size, :], rows)
        block = jnp.concatenate([for_qkv, for_proj, spare], axis=0).T
        weights_ref[where, :] = block[:, 0 : 4 * size].astype(weights_ref.dtype)
        return carry

    lax.fori_loop(first, last, one, 0)


def closing_kernel(
    count,
    scale,
    gpart_ref,
    cotangent_ref,
    mid_ref,
    collect_ref,
    proj_ref,
    context_ref,
    inverse_ref,
    hidden_far,
    down_far,
    garrived_far,
    gpre_far,
    arrived_far,
    rows_far,
    cols_far,
    norm_far,
    slots_ref,
    sum_ref,
    gdown_far,
    gup_far,
    hidden_ref,
    down_ref,
    garrived_ref,
    gpre_ref,
    arrived_ref,
    rows_ref,
    cols_ref,
    norm_ref,
    gdown_ref,
    gup_ref,
    load_sems,
    save_sems,
    part_ref,
    back_ref,
    own_ref,
    grad_ref,
    gcols_ref,
    gkeys,
    gvals,
    weights_ref,
    landing,
    *refs,
):
    fars = (hidden_far, down_far, garrived_far, gpre_far, arrived_far, rows_far, cols_far, norm_far)
    nears = (hidden_ref, down_ref, garrived_ref, gpre_ref, arrived_ref, rows_ref, cols_ref, norm_ref)
    loads = [
        pltpu.make_async_copy(far, near, load_sems.at[index])
        for index, (far, near) in enumerate(zip(fars, nears))
    ]
    ring_sems, refs = refs[:GATHER_SEMS], refs[GATHER_SEMS:]
    swap_refs, refs = refs[:3], refs[3:]
    each = OUT_SCRATCH + REDUCE_SCRATCH
    gslots, greduce = refs[:OUT_SCRATCH], refs[OUT_SCRATCH:each]
    slots, reduce = refs[each : each + OUT_SCRATCH], refs[each + OUT_SCRATCH :]
    _, level, _ = ring_places()
    grad_ring = ReduceRing(gpart_ref, gslots[0], *greduce, count)
    grad_back = SlotsBack(*gslots[:4], back_ref, gslots[4:])
    ring = GatherRing(own_ref, grad_ref, *ring_sems, count)
    back_ring = ReduceRing(part_ref, slots[0], *reduce, count)
    back = SlotsBack(*slots[:4], slots_ref, slots[4:])
    swap = Exchange(weights_ref, landing, *swap_refs)
    total = greet_axis("dp") + greet_ring(count)
    for load in loads:
        load.start()
    gkeys[...] = jnp.zeros_like(gkeys)
    gvals[...] = jnp.zeros_like(gvals)
    await_peers(total)
    experts = hidden_ref.shape[0]

    def to_part(expert, carry):
        block = mm(hidden_ref[expert], down_ref[expert]).astype(part_ref.dtype)
        part_ref[expert] = block.reshape(part_ref.shape[1:])
        return carry

    def to_down(expert, carry):
        gdown_ref[expert] = product(hidden_ref[expert], garrived_ref[expert]).astype(
            gdown_ref.dtype
        )
        return carry

    def to_up(expert, carry):
        gup_ref[expert] = product(gpre_ref[expert], arrived_ref[expert]).astype(gup_ref.dtype)
        return carry

    grad_ring.begin()
    grad_ring.run_step(0)
    loads[0].wait()
    loads[1].wait()
    lax.fori_loop(0, experts, to_part, 0)
    grad_ring.run_step(1)
    back_ring.begin()
    loads[2].wait()
    lax.fori_loop(0, experts, to_down, 0)
    save_down = pltpu.make_async_copy(gdown_ref, gdown_far, save_sems.at[0])
    save_down.start()
    grad_ring.run_step(2)
    loads[3].wait()
    loads[4].wait()
    lax.fori_loop(0, experts, to_up, 0)
    save_up = pltpu.make_async_copy(gup_ref, gup_far, save_sems.at[1])
    save_up.start()
    grad_ring.run_step(3)
    normal, factor = norm_parts(mid_ref[...])
    grad_ring.close()
    grad_back.begin()
    back_ring.run_step(0)
    grad_back.middle()
    back_ring.run_step(1)
    grad_back.finish()
    grad_norm = mm(collect_ref[...], back_ref[...])
    grad_mid = cotangent_ref[...].astype(jnp.float32) + norm_back(normal, factor, grad_norm)
    own_ref[...] = grad_mid.astype(own_ref.dtype)

    def block(place):
        backward_block(
            rows_ref, cols_ref, context_ref, inverse_ref, grad_ref, proj_ref, gcols_ref, gkeys, gvals, place, scale
        )

    reach = count // 2
    ring.begin()
    for load in loads[5:]:
        load.wait()
    ring.settle(0, 0)
    block(level)
    for step in range(reach):
        ring.run(step)
        if step >= 2:
            back_ring.run_step(step)
        for way in range(2):
            ring.settle(way, step + 1)
        if step < reach - 1:

            def one_way(way, carry, step=step):
                block(level_at(level, (2 * way - 1) * (step + 1), count))
                return carry

            lax.fori_loop(0, 2, one_way, 0)
        else:
            block(level_at(level, reach, count))
    flip_sums(gcols_ref, gkeys, gvals, scale)
    parts = norm_ref.shape[1] // (2 * LANES)
    weight_sums(norm_ref, grad_ref, context_ref, gcols_ref, weights_ref, 0, parts)
    back_ring.close()
    back.begin()
    swap.start()
    back.middle()
    back.finish()
    swap.finish()
    sums = landing[0].astype(jnp.float32)
    for group in range(1, landing.shape[0]):
        sums = sums + landing[group].astype(jnp.float32)
    sum_ref[...] = sums
    save_down.wait()
    save_up.wait()
    ring.finish()
    grad_ring.finish()
    back_ring.finish()


def closing(near, far, scale, size, ident):
    spots = lax.axis_size("tensor")
    count = spots // 2
    groups = lax.axis_size("dp")
    gpart, cotangent = near[:2]
    hidden, down, _, _, arrived = far[:5]
    seq, width = far[-1].shape
    experts, _, slot_rows, _ = gpart.shape
    slots = jax.ShapeDtypeStruct((experts * slot_rows, width), gpart.dtype)
    return comm_call(
        partial(closing_kernel, count, scale),
        [
            slots,
            jax.ShapeDtypeStruct((width // groups, 4 * size), jnp.float32),
            jax.ShapeDtypeStruct(down.shape, jnp.bfloat16),
            jax.ShapeDtypeStruct(down.shape, jnp.bfloat16),
        ],
        near + far,
        [pltpu.VMEM(item.shape, item.dtype) for item in far]
        + [
            pltpu.VMEM(down.shape, jnp.bfloat16),
            pltpu.VMEM(down.shape, jnp.bfloat16),
            DMA((len(far),)),
            DMA((2,)),
            pltpu.VMEM(gpart.shape, gpart.dtype),
            pltpu.VMEM(slots.shape, slots.dtype),
            pltpu.VMEM(cotangent.shape, jnp.bfloat16),
            pltpu.VMEM((spots,) + cotangent.shape, jnp.bfloat16),
            pltpu.VMEM((3 * size, seq), jnp.bfloat16),
            pltpu.VMEM((seq, LANES), jnp.float32),
            pltpu.VMEM((seq, LANES), jnp.float32),
            pltpu.VMEM((width, 4 * size), jnp.bfloat16),
            pltpu.VMEM((groups, width // groups, 4 * size), jnp.bfloat16),
        ]
        + gather_sems(count)
        + exchange_sems(groups)
        + (out_scratch(slots) + reduce_scratch(experts * slot_rows, width, gpart.dtype, count)) * 2,
        ident,
        len(far),
        2,
    )


epsilon = 1e-06
half_root = 1.0 / math.sqrt(2.0)
bell_scale = 1.0 / math.sqrt(2.0 * math.pi)


def norm_parts(row_block):
    widened = row_block.astype(jnp.float32)
    center = widened - jnp.mean(widened, axis=-1, keepdims=True)
    factor = lax.rsqrt(jnp.mean(center * center, axis=-1, keepdims=True) + epsilon)
    return (center * factor, factor)


def norm_back(normal_rows, factor, upstream):
    mean_up = jnp.mean(upstream, axis=-1, keepdims=True)
    mean_mix = jnp.mean(upstream * normal_rows, axis=-1, keepdims=True)
    return factor * (upstream - mean_up - normal_rows * mean_mix)


def gelu_value(pre_act):
    return 0.5 * pre_act * (1.0 + lax.erf(pre_act * half_root))


def gelu_slope(pre_act):
    return (
        0.5 * (1.0 + lax.erf(pre_act * half_root))
        + pre_act * jnp.exp(-0.5 * pre_act * pre_act) * bell_scale
    )


def shards(
    tokens,
    cotangent,
    gate_weights,
    routes,
    slot_index,
    qkv_weight,
    proj_weight,
    up_weight,
    down_weight,
):
    rows_dev, model_width = tokens.shape
    head_size = qkv_weight.shape[2] // 3
    score_scale = head_size ** (-0.5)
    group_count = lax.axis_size("dp")
    spots = lax.axis_size("tensor")
    local_experts = up_weight.shape[0]
    places = group_count * local_experts * CAP
    normal_in, _ = norm_parts(tokens)
    normed = normal_in.astype(jnp.bfloat16)
    slot_code = jnp.where(slot_index >= 0, routes * CAP + slot_index, -1)
    positions = jnp.arange(places, dtype=jnp.int32)
    pick_both = (slot_code[None, :, :] == positions[:, None, None]).astype(jnp.bfloat16)
    pick_first = pick_both[:, :, 0]
    pick_second = pick_both[:, :, 1]
    dispatch_rows = pick_first + pick_second
    upstream = cotangent.astype(jnp.float32)
    grad_first = (gate_weights[:, 0:1] * upstream).astype(jnp.bfloat16)
    grad_second = (gate_weights[:, 1:2] * upstream).astype(jnp.bfloat16)
    grad_outgoing = jnp.dot(pick_first, grad_first, preferred_element_type=jnp.float32) + jnp.dot(
        pick_second, grad_second, preferred_element_type=jnp.float32
    )
    pad = ((0, 0), (0, 0), (0, LANES - head_size))
    wide_qkv = jnp.pad(qkv_weight.reshape(model_width, 3, head_size), pad)
    wide_qkv = wide_qkv.reshape(model_width, 3 * LANES)
    wide_proj = jnp.pad(proj_weight[0], ((0, LANES - head_size), (0, 0)))
    full_norm, grad_arrived, qkv_rows, qkv_cols, context, inverse, mid, arrived = front(
        normed,
        grad_outgoing.astype(jnp.bfloat16),
        tokens,
        dispatch_rows,
        wide_qkv,
        proj_weight[0],
        score_scale,
        local_experts,
        1,
    )
    full_norm = full_norm.reshape(-1, model_width)
    grad_arrived = grad_arrived.reshape(local_experts, -1, model_width)
    arrived = arrived.reshape(local_experts, -1, model_width)
    pre_act = jnp.einsum("end,edf->enf", arrived, up_weight, preferred_element_type=jnp.float32)
    hidden = gelu_value(pre_act).astype(jnp.bfloat16)
    grad_hidden = jnp.einsum(
        "end,efd->enf", grad_arrived, down_weight, preferred_element_type=jnp.float32
    )
    grad_pre = (grad_hidden * gelu_slope(pre_act)).astype(jnp.bfloat16)
    grad_partial = jnp.einsum(
        "enf,edf->end", grad_pre, up_weight, preferred_element_type=jnp.float32
    )
    returned, grad_weights, grad_down, grad_up = closing(
        [
            grad_partial.astype(jnp.bfloat16).reshape(local_experts, spots, -1, model_width),
            cotangent,
            mid,
            dispatch_rows.T,
            wide_proj,
            context,
            inverse,
        ],
        [hidden, down_weight, grad_arrived, grad_pre, arrived, qkv_rows, qkv_cols, full_norm],
        score_scale,
        head_size,
        6,
    )
    expert_first = jnp.einsum("pr,pd->rd", pick_first, returned, preferred_element_type=jnp.float32)
    expert_second = jnp.einsum(
        "pr,pd->rd", pick_second, returned, preferred_element_type=jnp.float32
    )
    mixed_rows = gate_weights[:, 0:1] * expert_first + gate_weights[:, 1:2] * expert_second
    layer_out = (mid.astype(jnp.float32) + mixed_rows).astype(jnp.bfloat16)
    gate_grad = jnp.stack(
        [jnp.sum(upstream * expert_first, axis=-1), jnp.sum(upstream * expert_second, axis=-1)],
        axis=1,
    )
    grad_qkv = grad_weights[:, None, : 3 * head_size]
    grad_proj = grad_weights[:, 3 * head_size :].T[None]
    return (layer_out, gate_grad, grad_qkv, grad_proj, grad_up.swapaxes(1, 2), grad_down)


def solution(mesh):
    return jax.shard_map(
        shards,
        mesh=mesh,
        in_specs=(
            P(("dp", "tensor"), None),
            P(("dp", "tensor"), None),
            P(("dp", "tensor"), None),
            P(("dp", "tensor"), None),
            P(("dp", "tensor"), None),
            P(None, "tensor", None),
            P("tensor", None, None),
            P("dp", None, "tensor"),
            P("dp", "tensor", None),
        ),
        out_specs=(
            P(("dp", "tensor"), None),
            P(("dp", "tensor"), None),
            P("dp", "tensor", None),
            P("tensor", None, "dp"),
            P("dp", None, "tensor"),
            P("dp", "tensor", None),
        ),
        check_vma=False,
    )
```
